32 devices in a mesh: fsdp: 16 (over z, y, x), mp: 2 (over core).
Axes of the slice: x: 2, y: 2, z: 4, core: 2. Of those that a mesh axis runs over, the one named last changes fastest.
Arguments:
- values: bfloat16 [4096, 32], P('fsdp'), may hold values from -6 to 6
- lengths: int32 [64], P('fsdp'), may hold values from 1 to 64, 2560 in all
- w_in1: bfloat16 [64, 1280], P(None, 'fsdp'), may hold values from -0.75 to 0.75
- b_in1: bfloat16 [1280], P('fsdp'), may hold values from -3 to 3
- w_in2: bfloat16 [1280, 1280], P('fsdp'), may hold values from -0.15625 to 0.15625
- b_in2: bfloat16 [1280], P('fsdp'), may hold values from -3 to 3
- w_res: bfloat16 [64, 1280], P(None, 'fsdp'), may hold values from -0.75 to 0.75
- g_attn: bfloat16 [1280], P('fsdp'), may hold values from 0.099609375 to 1.8984375
- w_qkv: bfloat16 [1280, 3, 1280], P('fsdp', None, 'mp'), may hold values from -0.15625 to 0.15625
- w_out: bfloat16 [1280, 1280], P('mp', 'fsdp'), may hold values from -0.5 to 0.5
- g_mlp: bfloat16 [1280], P('fsdp'), may hold values from 0.099609375 to 1.8984375
- w_up: bfloat16 [1280, 1280], P('fsdp', 'mp'), may hold values from -0.15625 to 0.15625
- w_down: bfloat16 [1280, 1280], P('mp', 'fsdp'), may hold values from -0.25 to 0.25
- cotangent: bfloat16 [4096, 1280], P('fsdp'), may hold values from -6 to 6
Outputs:
- output: bfloat16 [4096, 1280], P('fsdp')
- d_values: float32 [4096, 32], P('fsdp')
- d_w_in1: float32 [64, 1280], P(None, 'fsdp')
- d_b_in1: float32 [1280], P('fsdp')
- d_w_in2: float32 [1280, 1280], P('fsdp')
- d_b_in2: float32 [1280], P('fsdp')
- d_w_res: float32 [64, 1280], P(None, 'fsdp')
- d_g_attn: float32 [1280], P('fsdp')
- d_w_qkv: float32 [1280, 3, 1280], P('fsdp', None, 'mp')
- d_w_out: float32 [1280, 1280], P('mp', 'fsdp')
- d_g_mlp: float32 [1280], P('fsdp')
- d_w_up: float32 [1280, 1280], P('fsdp', 'mp')
- d_w_down: float32 [1280, 1280], P('mp', 'fsdp')
The draws below stay inside these ranges and needn't reach their ends.
Inputs may be any that keep to these rules, and one draw needn't show every extreme that they name: `lengths`: patches of series s; its padded slots come first.
All inputs are finite; a program needn't handle non-finite values. No bound on the sum of `lengths` on one device may be relied on, other than what follows from the above.
Results may differ from the reference program's by a relative error of at most 0.014.
Values may be sent and summed in bfloat16 or wider, within the bound.
A program may use at most 192 MiB of HBM per device.

```python
import math
import jax
import jax.numpy as jnp
import numpy as np
from jax import lax

D = 1280
TH = 1280
PATCH = 32
HEADS = 16
HD = 80
FF = 1280
SEQ = 64
TOKIN = 64
SERIES = 64
TOKENS = 4096


def steps_of(stream_key, dims, split, low, top_value):
    def one(position, shards_of):
        steps = jax.random.uniform(jax.random.fold_in(jax.random.fold_in(stream_key, 6), position), (shards_of,), jnp.float32, low / len(split), top_value / len(split))
        return jnp.repeat(jnp.exp(steps), dims[position] // shards_of).reshape((-1,) + (1,) * (len(dims) - position - 1))

    loudness = one(*split[0])
    for cut in split[1:]:
        loudness = loudness * one(*cut)
    return loudness


def split_up(number_of, total, most, skew):
    portions = [(1 << 20) // math.isqrt(rank ** skew) + 1 for rank in range(2, number_of + 1)]
    surplus, counts = total - most - (number_of - 1), [1] * (number_of - 1)
    while surplus > 0:
        free = [i for i in range(number_of - 1) if counts[i] < most]
        mass, budget = sum([portions[i] for i in free]), surplus
        for i in free:
            more = min(most - counts[i], max(1, budget * portions[i] // mass), surplus)
            counts[i] = counts[i] + more
            surplus = surplus - more
    return np.array([most] + counts)


def ragged_sizes(key, amount, total, limit, skew):
    if amount == 2:
        one = jax.random.randint(key, (), max(1, total - limit), min(limit, total - 1) + 1)
        return jnp.stack([one, total - one])
    tallies = jnp.asarray(split_up(amount, total, limit, skew), jnp.int32)
    pairs = (amount - 1) // 2
    donor, sink = tallies[1:1 + 2 * pairs:2], tallies[2:2 + 2 * pairs:2]
    slack = jnp.minimum(donor - 1, limit - sink)
    shifted = jax.random.randint(jax.random.fold_in(key, 1), (pairs,), 0, 1 << 20) % (slack + 1)
    tallies = tallies.at[1:1 + 2 * pairs:2].set(donor - shifted).at[2:2 + 2 * pairs:2].set(sink + shifted)
    return tallies[jax.random.permutation(jax.random.fold_in(key, 2), amount)]


def centred(rng, extent, spread, bound, cuts=(), kind=jnp.bfloat16):
    values = jax.random.normal(rng, extent, jnp.float32) * spread
    if len(cuts) > 0:
        values = steps_of(rng, extent, cuts, -0.22, 0.18) * values
    return jnp.clip(values, min=-bound, max=bound).astype(kind)


def setup_inputs(seed: int = 0) -> dict:
    key_of = jax.random.split(jax.random.key(seed), 15)
    values = centred(key_of[0], (TOKENS, PATCH), 1.0, 6.0, ((0, 16),))
    lengths = ragged_sizes(key_of[1], SERIES, SERIES * SEQ * 5 // 8, SEQ, 2).astype(jnp.int32)
    w_in1 = centred(key_of[2], (TOKIN, TH), TOKIN ** -0.5, 0.75, ((1, 16),))
    b_in1 = centred(key_of[3], (TH,), 0.5, 3.0, ((0, 16),))
    w_in2 = centred(key_of[4], (TH, D), TH ** -0.5, 0.15625, ((0, 16),))
    b_in2 = centred(key_of[5], (D,), 0.5, 3.0, ((0, 16),))
    w_res = centred(key_of[6], (TOKIN, D), TOKIN ** -0.5, 0.75, ((1, 16),))
    g_attn = jnp.clip(1.0 + 0.18 * jax.random.normal(key_of[7], (D,), jnp.float32), 0.099609375, 1.8984375).astype(jnp.bfloat16)
    w_qkv = centred(key_of[8], (D, 3, HEADS * HD), D ** -0.5, 0.15625, ((0, 16), (2, 2)))
    w_out = centred(key_of[9], (HEADS * HD, D), (HEADS * HD // 8) ** -0.5, 0.5, ((0, 2), (1, 16)))
    g_mlp = jnp.clip(1.0 + 0.18 * jax.random.normal(key_of[10], (D,), jnp.float32), 0.099609375, 1.8984375).astype(jnp.bfloat16)
    w_up = centred(key_of[11], (D, FF), D ** -0.5, 0.15625, ((0, 16), (1, 2)))
    w_down = centred(key_of[12], (FF, D), (FF // 2) ** -0.5, 0.25, ((0, 2), (1, 16)))
    cotangent = centred(key_of[13], (TOKENS, D), 1.0, 6.0, ((0, 16),))
    return {"values": values, "lengths": lengths, "w_in1": w_in1, "b_in1": b_in1, "w_in2": w_in2, "b_in2": b_in2, "w_res": w_res, "g_attn": g_attn, "w_qkv": w_qkv, "w_out": w_out, "g_mlp": g_mlp, "w_up": w_up, "w_down": w_down, "cotangent": cotangent}


@jax.custom_vjp
def low(v):
    return lax.optimization_barrier(v.astype(jnp.bfloat16)).astype(jnp.float32)

@jax.custom_vjp
def low_back(v):
    return v

def low_keep(v):
    return (low(v), None)

def low_pass(kept, grad):
    return (grad,)

def back_keep(v):
    return (v, None)

def back_low(kept, grad):
    return (low(grad),)
low.defvjp(low_keep, low_pass)
low_back.defvjp(back_keep, back_low)
highest = lax.Precision.HIGHEST

def matmul(left, right):
    return jnp.dot(left, right, precision=highest)

def rotate(vectors, places):
    half_width = vectors.shape[-1] // 2
    frequency = 10000.0 ** (-2.0 * jnp.arange(half_width, dtype=jnp.float32) / vectors.shape[-1])
    angles = places[:, :, None, None] * frequency
    cosine = jnp.cos(angles)
    sine_val = jnp.sin(angles)
    first_half = vectors[..., :half_width]
    second_half = vectors[..., half_width:]
    return jnp.concatenate([first_half * cosine - second_half * sine_val, second_half * cosine + first_half * sine_val], -1)

def rms_norm(resid_rows, gain_vec):
    return resid_rows * lax.rsqrt(lax.optimization_barrier(jnp.mean(resid_rows * resid_rows, -1, keepdims=True)) + 1e-06) * gain_vec

def forward(given_vals, length_rows, parameters):
    w_in1, b_in1, w_in2, b_in2, w_res, g_attn, w_qkv, w_out, g_mlp, w_up, w_down = parameters
    series = length_rows.shape[0]
    slot_ids = jnp.arange(SEQ, dtype=jnp.int32)
    pad_count = (SEQ - length_rows).astype(jnp.int32)
    padded = slot_ids[None, :] < pad_count[:, None]
    places = (slot_ids[None, :] - pad_count[:, None]).astype(jnp.float32)
    keep_mask = (1.0 - padded.astype(jnp.float32)).reshape(-1, 1)
    inputs = low(jnp.concatenate([given_vals * keep_mask, jnp.broadcast_to(1.0 - keep_mask, given_vals.shape)], 1))
    pre_act = low_back(matmul(inputs, w_in1) + b_in1)
    hidden = low(jax.nn.silu(pre_act))
    resid0 = low_back(matmul(hidden, w_in2) + b_in2 + matmul(inputs, w_res))
    normed = low(rms_norm(resid0, g_attn))
    projected = jnp.einsum('td,dch->tch', normed, w_qkv, precision=highest)
    head_shape = (series, SEQ, HEADS, HD)
    queries = low(rotate(low_back(projected[:, 0]).reshape(head_shape), places))
    key_rows = low(rotate(low_back(projected[:, 1]).reshape(head_shape), places))
    value_heads = low(low_back(projected[:, 2])).reshape(head_shape)
    scores = low_back(jnp.einsum('sqhe,skhe->shqk', queries, key_rows, precision=highest) * HD ** (-0.5))
    causal = slot_ids[None, :] <= slot_ids[:, None]
    diagonal = slot_ids[None, :] == slot_ids[:, None]
    allowed = causal[None] & (jnp.logical_not(padded)[:, None, :] | diagonal[None])
    scores = jnp.where(allowed[:, None], scores, -1e+30)
    row_max = lax.optimization_barrier(jnp.max(scores, -1, keepdims=True))
    exponent = jnp.exp(scores - row_max)
    attn_probs = low(exponent / lax.optimization_barrier(jnp.sum(exponent, -1, keepdims=True)))
    attended = low(low_back(jnp.einsum('shqk,skhe->sqhe', attn_probs, value_heads, precision=highest))).reshape(-1, HEADS * HD)
    resid1 = resid0 + low_back(matmul(attended, w_out))
    normed2 = low(rms_norm(resid1, g_mlp))
    up_pre = low_back(matmul(normed2, w_up))
    mlp_hidden = low(jax.nn.gelu(up_pre, approximate=False))
    return resid1 + low_back(matmul(mlp_hidden, w_down))

def reference(values, lengths, w_in1, b_in1, w_in2, b_in2, w_res, g_attn, w_qkv, w_out, g_mlp, w_up, w_down, cotangent):
    weights = tuple((weight.astype(jnp.float32) for weight in (w_in1, b_in1, w_in2, b_in2, w_res, g_attn, w_qkv, w_out, g_mlp, w_up, w_down)))
    group_size = math.gcd(SERIES, max(1, 4096 // SEQ))
    group_count = SERIES // group_size
    value_rows = values.astype(jnp.float32).reshape(group_count, group_size * SEQ, PATCH)
    length_rows = lengths.reshape(group_count, group_size)
    cot_rows = cotangent.astype(jnp.float32).reshape(group_count, group_size * SEQ, D)

    def one_group(totals, pieces):
        part_vals, part_lens, part_cot = pieces
        result, pullback = jax.vjp(lambda given_vals, *parameters: forward(given_vals, part_lens, parameters), part_vals, *weights)
        gradients = pullback(part_cot)
        totals = tuple((total + grad_part for total, grad_part in zip(totals, gradients[1:])))
        return (totals, (result.astype(jnp.bfloat16), gradients[0]))
    zeros_init = tuple((jnp.zeros_like(weight) for weight in weights))
    totals, (outputs, value_grads) = lax.scan(one_group, zeros_init, (value_rows, length_rows, cot_rows))
    return (outputs.reshape(TOKENS, D), value_grads.reshape(TOKENS, PATCH), totals[0], totals[1], totals[2], totals[3], totals[4], totals[5], totals[6], totals[7], totals[8], totals[9], totals[10])
```

```python
import functools
import math

import jax
import jax.numpy as jnp
from jax import lax
from jax.experimental import pallas as pl
from jax.experimental.pallas import tpu as pltpu
from jax.sharding import PartitionSpec as P

HD = 80
MESH = pl.DeviceIdType.MESH
f32 = jnp.float32
bf16 = jnp.bfloat16

IN2, WQ, WK, WV, WOUT, WUP, WDOWN, PACK = range(8)
NW = 7
PL = 128
SLOT_A, SLOT_X, SLOT_Y, SLOT_V, SLOT_V2, SLOTS = 0, 4, 8, 12, 16, 17
VMEM_BYTES = 63 * 2**20


def dot(left, right, left_dim, right_dim):
    return lax.dot_general(
        left, right, (((left_dim,), (right_dim,)), ((), ())), preferred_element_type=f32
    )


def fused_kernel(
    lengths,
    values,
    pack,
    in2,
    qkv,
    out_t,
    up,
    down_t,
    cot_hbm,
    o_out,
    o_dval,
    o_pack,
    o_in2,
    o_qkv,
    o_wout,
    o_up,
    o_down,
    W,
    PK,
    G,
    GP,
    R,
    RP,
    R0,
    R1,
    S,
    X,
    SB,
    XB,
    hid,
    nrm,
    nrm2,
    q,
    k,
    v,
    prob,
    att,
    gprime,
    mlp,
    cot,
    dup,
    dq,
    dk,
    dv,
    tmp,
    dr0,
    rope_c,
    rope_s,
    bias,
    inx,
    gains,
    dgs,
    accg,
    keep_col,
    acc,
    accp,
    fin_in2,
    fin_pack,
    ag_send,
    ag_recv,
    rs_send,
    rs_recv,
    ex_send,
    ex_recv,
    lsem,
):
    rows, width = cot.shape
    half = W.shape[2]
    blk = in2.shape[0]
    series = lengths.shape[0]
    seq = rows // series
    heads = half // HD
    patch = values.shape[1]

    f = lax.axis_index("fsdp")
    m = lax.axis_index("mp")
    x = lax.rem(f, 2)
    y = lax.rem(lax.div(f, 2), 2)
    z = lax.div(f, 4)
    xn = f + 1 - 2 * x
    yn = f + 2 - 4 * y
    dn_ = f + 3 - 2 * x - 4 * y
    XN, YN, UP, DN, SIB = (xn, m), (yn, m), (f + 4, m), (f - 4, m), (f, 1 - m)
    cx, cy, cd, c0 = xn - 4 * z, yn - 4 * z, dn_ - 4 * z, f - 4 * z
    z_inner = jnp.logical_and(z > 0, z < 3).astype(jnp.int32)
    z_high = (z >= 2).astype(jnp.int32)

    def near(i):
        swap = (i == 0).astype(jnp.int32) - (i == 1).astype(jnp.int32)
        low = i + z_inner * swap
        return low + z_high * (3 - 2 * low)

    def far(i):
        return near(3 - i)

    def each_plane(order, body):
        def step(i, carry):
            body(order(i))
            return carry

        lax.fori_loop(0, 4, step, 0)

    def row_of(b):
        return pl.ds(pl.multiple_of(b * blk, 16), blk)

    def w_block(w, b):
        return PK.at[m, row_of(b)] if w == PACK else W.at[w, row_of(b)]

    def g_block(w, b):
        return GP.at[row_of(b)] if w == PACK else G.at[w, row_of(b)]

    def r_block(w, s):
        return RP.at[s] if w == PACK else R.at[w, s]

    def remote(src, dst, send, recv, dev):
        return pltpu.make_async_remote_copy(
            src_ref=src, dst_ref=dst, send_sem=send, recv_sem=recv, device_id=dev, device_id_type=MESH
        )

    def ag_push(w, b, dev):
        ref = w_block(w, b)
        remote(ref, ref, ag_send.at[w], ag_recv.at[w, b], dev).start()

    def ag_await(w, b):
        ref = w_block(w, b)
        remote(ref, ref, ag_send.at[w], ag_recv.at[w, b], XN).wait_recv()

    mcols = pl.ds(pl.multiple_of(m * half, 128), half)

    def own_copy(w):
        if w == PACK:
            src = pack.at[m]
        elif w == IN2:
            src = in2.at[:, mcols]
        elif w in (WQ, WK, WV):
            src = qkv.at[w - WQ]
        else:
            src = {WOUT: out_t, WUP: up, WDOWN: down_t}[w]
        return pltpu.make_async_copy(src, w_block(w, f), lsem.at[w])

    def ag_own(w):
        own_copy(w).wait()

        @pl.when(z < 3)
        def _():
            ag_push(w, f, UP)

        @pl.when(z > 0)
        def _():
            ag_push(w, f, DN)

        ag_push(w, f, XN)
        ag_push(w, f, YN)

    def ag_chain(w):
        for d in (1, 2, 3):

            @pl.when(z >= d)
            def _():
                b = f - 4 * d
                ag_await(w, b)

                @pl.when(z < 3)
                def _():
                    ag_push(w, b, UP)

                ag_push(w, b, XN)
                ag_push(w, b, YN)

            @pl.when(z + d <= 3)
            def _():
                b = f + 4 * d
                ag_await(w, b)

                @pl.when(z > 0)
                def _():
                    ag_push(w, b, DN)

                ag_push(w, b, XN)
                ag_push(w, b, YN)

    def ag_plane(w):
        def body(zb):
            even = lax.rem(zb, 2) == 0
            ag_await(w, 4 * zb + cx)

            @pl.when(even)
            def _():
                ag_push(w, 4 * zb + cx, YN)

            ag_await(w, 4 * zb + cy)

            @pl.when(jnp.logical_not(even))
            def _():
                ag_push(w, 4 * zb + cy, XN)

        each_plane(near, body)

    def ag_last(w):
        each_plane(near, lambda zb: ag_await(w, 4 * zb + cd))

    def rs_push(w, src, slot, dev):
        remote(src, r_block(w, slot), rs_send.at[w], rs_recv.at[w, slot], dev).start()

    def rs_await(w, slot):
        ref = r_block(w, slot)
        remote(ref, ref, rs_send.at[w], rs_recv.at[w, slot], XN).wait_recv()

    def rs_start(w):
        def body(zb):
            even = lax.rem(zb, 2) == 0

            @pl.when(even)
            def _():
                rs_push(w, g_block(w, 4 * zb + cd), SLOT_A + zb, YN)
                rs_push(w, g_block(w, 4 * zb + cy), SLOT_Y + zb, YN)

            @pl.when(jnp.logical_not(even))
            def _():
                rs_push(w, g_block(w, 4 * zb + cd), SLOT_A + zb, XN)
                rs_push(w, g_block(w, 4 * zb + cx), SLOT_X + zb, XN)

        each_plane(far, body)

    def rs_turn(w):
        def body(zb):
            even = lax.rem(zb, 2) == 0
            rs_await(w, SLOT_A + zb)
            ref = r_block(w, SLOT_A + zb)

            @pl.when(even)
            def _():
                own = g_block(w, 4 * zb + cx)
                ref[...] = (ref[...].astype(f32) + own[...].astype(f32)).astype(bf16)
                rs_push(w, ref, SLOT_X + zb, XN)

            @pl.when(jnp.logical_not(even))
            def _():
                own = g_block(w, 4 * zb + cy)
                ref[...] = (ref[...].astype(f32) + own[...].astype(f32)).astype(bf16)
                rs_push(w, ref, SLOT_Y + zb, YN)

        each_plane(far, body)

    def rs_chain(w, final):
        total = accp if w == PACK else acc

        def body(zb):
            rs_await(w, SLOT_X + zb)
            rs_await(w, SLOT_Y + zb)
            total[...] = (
                g_block(w, 4 * zb + c0)[...].astype(f32)
                + r_block(w, SLOT_X + zb)[...].astype(f32)
                + r_block(w, SLOT_Y + zb)[...].astype(f32)
            )

            def take(slot):
                rs_await(w, slot)
                total[...] += r_block(w, slot)[...].astype(f32)

            upward = zb > z
            downward = zb < z

            @pl.when(jnp.logical_or(jnp.logical_and(upward, z > 0), jnp.logical_and(zb <= z, z < 3)))
            def _():
                take(SLOT_V + zb)

            ref = r_block(w, SLOT_X + zb)

            @pl.when(upward)
            def _():
                ref[...] = total[...].astype(bf16)

                @pl.when(z + 1 == zb)
                def _():
                    rs_push(w, ref, SLOT_V2, UP)

                @pl.when(z + 1 != zb)
                def _():
                    rs_push(w, ref, SLOT_V + zb, UP)

            @pl.when(downward)
            def _():
                ref[...] = total[...].astype(bf16)
                rs_push(w, ref, SLOT_V + zb, DN)

            @pl.when(jnp.logical_and(zb == z, z > 0))
            def _():
                take(SLOT_V2)

        each_plane(far, body)
        final[...] = total[...]

    def exchange(i, src, dst):
        return remote(src, dst, ex_send.at[i], ex_recv.at[i], SIB)

    def by_rows(step, body):
        def one(i, carry):
            body(pl.ds(pl.multiple_of(i * step, step), step))
            return carry

        lax.fori_loop(0, rows // step, one, 0)

    halves = (slice(0, half), slice(half, width))

    barrier = pltpu.get_barrier_semaphore()
    for dev in (XN, YN, SIB):
        pl.semaphore_signal(barrier, inc=1, device_id=dev, device_id_type=MESH)

    @pl.when(z < 3)
    def _():
        pl.semaphore_signal(barrier, inc=1, device_id=UP, device_id_type=MESH)

    @pl.when(z > 0)
    def _():
        pl.semaphore_signal(barrier, inc=1, device_id=DN, device_id_type=MESH)

    order = (PACK, IN2, WQ, WK, WV, WOUT, WUP, WDOWN)
    for w in order:
        own_copy(w).start()
    cot_copy = pltpu.make_async_copy(cot_hbm, cot, lsem.at[8])
    cot_copy.start()
    pl.semaphore_wait(barrier, 4 + z_inner)

    ag_own(PACK)
    ag_own(IN2)
    ag_own(WQ)

    lens = [lengths[s] for s in range(series)]

    def pad_of(slot):
        total = jnp.zeros(slot.shape, jnp.int32)
        for s in range(series):
            inside = jnp.logical_and(slot >= s * seq, slot < (s + 1) * seq)
            total = jnp.where(inside, (s + 1) * seq - lens[s], total)
        return total

    def series_of(slot):
        total = jnp.zeros(slot.shape, jnp.int32)
        for s in range(1, series):
            total = total + (slot >= s * seq).astype(jnp.int32)
        return total

    slot_col = lax.broadcasted_iota(jnp.int32, (rows, 1), 0)
    keep_col[...] = jnp.broadcast_to((slot_col >= pad_of(slot_col)).astype(f32), keep_col.shape)
    lane_i = lax.broadcasted_iota(jnp.int32, (rows, PL), 1)
    keep = keep_col[...]
    wide = jnp.concatenate([values[...].astype(f32), jnp.zeros((rows, PL - patch), f32)], 1)
    inx[...] = jnp.where(
        lane_i < patch,
        wide * keep,
        jnp.where(lane_i < 2 * patch, 1.0 - keep, (lane_i == 2 * patch).astype(f32)),
    ).astype(bf16)

    key_slot = lax.broadcasted_iota(jnp.int32, (1, rows), 1)
    key_ok = key_slot >= pad_of(key_slot)
    key_series = series_of(key_slot)

    def bias_rows(s):
        step = s.size
        a = lax.broadcasted_iota(jnp.int32, (step, 1), 0) + s.start
        a_all = jnp.broadcast_to(a, (step, rows))
        b_all = jnp.broadcast_to(key_slot, (step, rows))
        same = series_of(a_all) == jnp.broadcast_to(key_series, (step, rows))
        ok = jnp.logical_or(jnp.broadcast_to(key_ok.astype(jnp.int32), (step, rows)) == 1, a_all == b_all)
        allowed = jnp.logical_and(jnp.logical_and(same, b_all <= a_all), ok)
        bias[s, :] = jnp.where(allowed, 0.0, -1e30)

    by_rows(32, bias_rows)

    lane = lax.broadcasted_iota(jnp.int32, (1, half), 1).astype(f32)
    in_head = lane - HD * jnp.floor((lane + 0.5) / HD)
    first = in_head < HD // 2
    turn = jnp.where(first, in_head, in_head - HD // 2)
    frequency = jnp.exp(turn * (-2.0 * math.log(10000.0) / HD))

    def rope_rows(s):
        step = s.size
        slot = lax.broadcasted_iota(jnp.int32, (step, 1), 0) + s.start
        place = (slot - pad_of(slot)).astype(f32)
        angle = place * frequency
        rope_c[s, :] = jnp.cos(angle)
        sine = jnp.sin(angle)
        rope_s[s, :] = jnp.where(first, -sine, sine)

    by_rows(16, rope_rows)

    def rope(t, s, inverse):
        other = jnp.where(first, pltpu.roll(t, half - HD // 2, 1), pltpu.roll(t, HD // 2, 1))
        turned = other * rope_s[s, :]
        return t * rope_c[s, :] - turned if inverse else t * rope_c[s, :] + turned

    ag_chain(PACK)
    ag_own(WK)
    ag_plane(PACK)
    ag_last(PACK)
    pk_copy = exchange(0, PK.at[m], PK.at[m])
    pk_copy.start()
    pk_copy.wait()
    gain_lane = lax.broadcasted_iota(jnp.int32, (16, PL), 1)
    for i in range(2):
        pick = (gain_lane == 2 * patch + 1 + i).astype(bf16)
        gains[i] = dot(pick, PK[1], 1, 1)[0:8]

    def pre_act():
        for cols in halves:
            tmp[:, cols] = dot(inx[...], PK[0, cols, :], 1, 1)

    pre_act()

    def silu_rows(s):
        t = tmp[s, :]
        hid[s, :] = (t / (1.0 + jnp.exp(-t))).astype(bf16)

    by_rows(16, silu_rows)

    ag_chain(IN2)
    ag_own(WV)
    ag_chain(WQ)
    ag_plane(IN2)
    ag_last(IN2)
    R0[m] = dot(hid[...], W[IN2], 1, 0) + dot(inx[...], PK[1, mcols, :], 1, 1)
    r0_copy = exchange(1, R0.at[m], R0.at[m])
    r0_copy.start()
    ag_chain(WK)
    ag_own(WOUT)
    r0_copy.wait()

    def norm_rows(load, gain, out):
        def body(s):
            a, b = load(s)
            mean = (jnp.sum(a * a, -1, keepdims=True) + jnp.sum(b * b, -1, keepdims=True)) / width
            scale = lax.rsqrt(mean + 1e-06)
            out[s, halves[0]] = (a * scale * gain[0:1, halves[0]]).astype(bf16)
            out[s, halves[1]] = (b * scale * gain[0:1, halves[1]]).astype(bf16)

        by_rows(16, body)

    norm_rows(lambda s: (R0[0, s, :], R0[1, s, :]), gains.at[0], nrm)

    def project(w, out):
        tmp[:, halves[0]] = dot(nrm[...], W[w], 1, 0)

        def body(s):
            out[s, :] = rope(tmp[s, halves[0]], s, False).astype(bf16)

        by_rows(16, body)

    ag_plane(WQ)
    ag_last(WQ)
    project(WQ, q)
    ag_chain(WV)
    ag_own(WUP)
    ag_plane(WK)
    ag_last(WK)
    project(WK, k)
    ag_chain(WOUT)
    ag_own(WDOWN)
    ag_plane(WV)
    ag_last(WV)
    v[...] = dot(nrm[...], W[WV], 1, 0).astype(bf16)

    win = 256
    scale = HD ** (-0.5)
    win_lane = lax.broadcasted_iota(jnp.int32, (1, win), 1)

    def head_window(h):
        low = jnp.minimum(lax.div(h * HD, 128) * 128, half - win)
        inside = jnp.logical_and(win_lane >= h * HD - low, win_lane < h * HD - low + HD)
        return pl.ds(pl.multiple_of(low, 128), win), inside

    def only(inside, t):
        return jnp.where(inside, t.astype(f32), 0.0).astype(bf16)

    att[...] = jnp.zeros_like(att)

    def head_forward(h, carry):
        cols, inside = head_window(h)
        score = dot(only(inside, q[:, cols]), k[:, cols], 1, 1) * scale + bias[...]
        exponent = jnp.exp(score - jnp.max(score, -1, keepdims=True))
        p = exponent / jnp.sum(exponent, -1, keepdims=True)
        prob[h] = p
        mixed = dot(p.astype(bf16), v[:, cols], 1, 0)
        att[:, cols] = jnp.where(inside, mixed, att[:, cols].astype(f32)).astype(bf16)
        return carry

    lax.fori_loop(0, heads, head_forward, 0)

    ag_chain(WUP)
    ag_plane(WOUT)
    ag_last(WOUT)

    def widen(dst, terms):
        for cols in halves:
            total = None
            for left, w in terms:
                part = dot(left[...], W[w, cols, :], 1, 1)
                total = part if total is None else total + part
            dst[:, cols] = total.astype(dst.dtype)

    widen(S.at[0], [(att, WOUT)])
    e1 = exchange(2, S.at[0], X.at[0])
    e1.start()
    ag_chain(WDOWN)
    e1.wait()

    def resid1_rows(s):
        for i, cols in enumerate(halves):
            R1[s, cols] = R0[i, s, :] + (S[0, s, cols] + X[0, s, cols])

    by_rows(16, resid1_rows)
    norm_rows(lambda s: (R1[s, halves[0]], R1[s, halves[1]]), gains.at[1], nrm2)

    ag_plane(WUP)
    ag_last(WUP)
    tmp[:, halves[0]] = dot(nrm2[...], W[WUP], 1, 0)

    def gelu_rows(s):
        t = tmp[s, halves[0]]
        phi = 0.5 * (1.0 + lax.erf(t * (2.0 ** -0.5)))
        mlp[s, :] = (t * phi).astype(bf16)
        gprime[s, :] = phi + t * jnp.exp(-0.5 * t * t) * ((2.0 * math.pi) ** -0.5)

    by_rows(16, gelu_rows)

    def weight_grad(w, left, right):
        for r in halves:
            G[w, r, :] = dot(left[:, r], right, 0, 0).astype(bf16)

    cot_copy.wait()
    weight_grad(WDOWN, cot, mlp[...])
    rs_start(WDOWN)
    ag_plane(WDOWN)
    ag_last(WDOWN)
    tmp[:, halves[0]] = dot(cot[...], W[WDOWN], 1, 0)

    def dup_rows(s):
        dup[s, :] = (tmp[s, halves[0]] * gprime[s, :]).astype(bf16)

    by_rows(16, dup_rows)
    weight_grad(WUP, nrm2, dup[...])
    rs_start(WUP)
    widen(SB, [(mlp, WDOWN)])
    e2 = exchange(3, SB, XB)
    e2.start()
    widen(S.at[1], [(dup, WUP)])
    e3 = exchange(4, S.at[1], X.at[1])
    e3.start()
    rs_turn(WDOWN)
    e2.wait()

    def output_rows(s):
        o_out[s, :] = (R1[s, :] + (SB[s, :].astype(f32) + XB[s, :].astype(f32))).astype(bf16)

    by_rows(16, output_rows)
    e3.wait()

    def norm_grad(load, partial, gain, base, out, keep_sum):
        def body(i, carry):
            s = pl.ds(pl.multiple_of(i * 16, 16), 16)
            xs = load(s)
            mean = sum(jnp.sum(t * t, -1, keepdims=True) for t in xs) / width
            r = lax.rsqrt(mean + 1e-06)
            n1 = [t * r for t in xs]
            dn = [partial[0][s, c] + partial[1][s, c] for c in halves]
            gd = [gain[0:1, c] * t for c, t in zip(halves, dn)]
            inner = sum(jnp.sum(a * b, -1, keepdims=True) for a, b in zip(gd, n1)) / width
            for c, a, b in zip(halves, gd, n1):
                out(s, c, base(s, c) + r * (a - b * inner))
            for c, a, b in zip(halves, dn, n1):
                prod = a * b
                accg[:, c] += prod[0:8] + prod[8:16]
            return carry

        accg[...] = jnp.zeros_like(accg)
        lax.fori_loop(0, rows // 16, body, 0)
        total = accg[...]
        high = total.astype(bf16)
        keep_sum[...] = jnp.concatenate([high.astype(f32), total - high.astype(f32)], 0).astype(bf16)

    def out1(s, c, t):
        R1[s, c] = t
        nrm2[s, c] = t.astype(bf16)

    norm_grad(
        lambda s: [R1[s, c] for c in halves],
        (S.at[1], X.at[1]),
        gains.at[1],
        lambda s, c: cot[s, c].astype(f32),
        out1,
        dgs.at[1],
    )
    weight_grad(WOUT, nrm2, att[...])
    rs_start(WOUT)
    att[...] = dot(nrm2[...], W[WOUT], 1, 0).astype(bf16)
    rs_turn(WUP)

    def head_backward(h, carry):
        cols, inside = head_window(h)
        cols2 = pl.ds(pl.multiple_of(cols.start + half, 128), win)
        p = prob[h]
        da = only(inside, att[:, cols])
        dp = dot(da, v[:, cols], 1, 1)
        inner = jnp.sum(dp * p, -1, keepdims=True)
        ds = (p * (dp - inner)).astype(bf16)
        dv_h = dot(p.astype(bf16), da, 0, 0)
        dq_h = dot(ds, k[:, cols], 1, 0) * scale
        dk_h = dot(ds, q[:, cols], 0, 0) * scale
        dv[:, cols] = jnp.where(inside, dv_h, dv[:, cols].astype(f32)).astype(bf16)
        tmp[:, cols] = jnp.where(inside, dq_h, tmp[:, cols])
        tmp[:, cols2] = jnp.where(inside, dk_h, tmp[:, cols2])
        return carry

    dv[...] = jnp.zeros_like(dv)
    tmp[...] = jnp.zeros_like(tmp)
    lax.fori_loop(0, heads, head_backward, 0)

    def unrope_rows(s):
        dq[s, :] = rope(tmp[s, halves[0]], s, True).astype(bf16)
        dk[s, :] = rope(tmp[s, halves[1]], s, True).astype(bf16)

    by_rows(16, unrope_rows)
    for w, g in ((WQ, dq), (WK, dk), (WV, dv)):
        weight_grad(w, nrm, g[...])
        rs_start(w)
    widen(S.at[0], [(dq, WQ), (dk, WK), (dv, WV)])
    e4 = exchange(5, S.at[0], X.at[0])
    e4.start()
    rs_turn(WOUT)
    rs_chain(WDOWN, o_down)
    e4.wait()

    def out0(s, c, t):
        dr0[s, c] = t.astype(bf16)

    norm_grad(
        lambda s: [R0[i, s, :] for i in range(2)],
        (S.at[0], X.at[0]),
        gains.at[0],
        lambda s, c: R1[s, c],
        out0,
        dgs.at[0],
    )

    weight_grad(IN2, hid, dr0[:, mcols])
    rs_start(IN2)
    for c in halves:
        S[1, :, c] = dot(dr0[:, mcols], W[IN2, c, :], 1, 1)
    e5 = exchange(6, S.at[1], X.at[1])
    e5.start()
    for w in (WQ, WK, WV):
        rs_turn(w)
    pre_act()
    e5.wait()

    def dpre_rows(s):
        t = tmp[s, :]
        sig = 1.0 / (1.0 + jnp.exp(-t))
        grad = (S[1, s, :] + X[1, s, :]) * (sig * (1.0 + t * (1.0 - sig)))
        nrm[s, :] = grad.astype(bf16)

    by_rows(16, dpre_rows)
    dval = dot(nrm[...], PK[0], 1, 0) + dot(dr0[...], PK[1], 1, 0)
    o_dval[...] = (dval * keep_col[...])[:, 0:patch]

    @pl.when(m == 0)
    def _():
        for r in halves:
            GP[r, :] = dot(nrm[:, r], inx[...], 0, 0).astype(bf16)

    @pl.when(m == 1)
    def _():
        for r in halves:
            total = dot(dr0[:, r], inx[...], 0, 0)
            for i in range(2):
                pick = (gain_lane == 2 * patch + 1 + i).astype(bf16)
                total = total + dot(dgs[i, :, r], pick, 0, 0)
            GP[r, :] = total.astype(bf16)

    rs_start(PACK)
    rs_chain(WUP, o_up)
    rs_turn(IN2)
    rs_chain(WOUT, o_wout)
    rs_turn(PACK)
    for i, w in enumerate((WQ, WK, WV)):
        rs_chain(w, o_qkv.at[i])
    rs_chain(IN2, fin_in2.at[m])
    e6 = exchange(7, fin_in2.at[m], fin_in2.at[m])
    e6.start()
    rs_chain(PACK, fin_pack.at[m])
    e7 = exchange(8, fin_pack.at[m], fin_pack.at[m])
    e7.start()
    e6.wait()
    for i, c in enumerate(halves):
        o_in2[:, c] = fin_in2[i]
    e7.wait()
    o_pack[...] = fin_pack[...]

    def drain(w, ref_of, sem, blocks):
        ref = ref_of(blocks)
        remote(ref, ref, sem.at[w], sem.at[w], XN).wait_send()

    for w in order:
        if w == PACK:
            view = lambda n: PK.at[m, pl.ds(0, n * blk)]
            rview = lambda n: RP.at[pl.ds(0, n)]
        else:
            view = lambda n, w=w: W.at[w, pl.ds(0, n * blk)]
            rview = lambda n, w=w: R.at[w, pl.ds(0, n)]

        drain(w, view, ag_send, 13)

        @pl.when(z_inner == 1)
        def _():
            drain(w, view, ag_send, 4)

        drain(w, rview, rs_send, 15)


def rotate(vectors, places):
    half_width = vectors.shape[-1] // 2
    frequency = 10000.0 ** (-2.0 * jnp.arange(half_width, dtype=jnp.float32) / vectors.shape[-1])
    angles = places[:, :, None, None] * frequency
    cosine = jnp.cos(angles)
    sine_val = jnp.sin(angles)
    first_half = vectors[..., :half_width]
    second_half = vectors[..., half_width:]
    return jnp.concatenate(
        [
            first_half * cosine - second_half * sine_val,
            second_half * cosine + first_half * sine_val,
        ],
        -1,
    )


def rms_norm(resid_rows, gain_vec):
    return (
        resid_rows
        * lax.rsqrt(jnp.mean(resid_rows * resid_rows, -1, keepdims=True) + 1e-06)
        * gain_vec
    )


def activate(up_rows):
    return jax.nn.gelu(up_rows, approximate=False)


def general_device(
    values,
    lengths,
    w_in1,
    b_in1,
    w_in2,
    b_in2,
    w_res,
    g_attn,
    w_qkv,
    w_out,
    g_mlp,
    w_up,
    w_down,
    cotangent,
):
    f32 = jnp.float32
    bf16 = jnp.bfloat16
    gathered = (
        lax.all_gather(w_in1, "fsdp", axis=1, tiled=True),
        lax.all_gather(b_in1, "fsdp", axis=0, tiled=True),
        lax.all_gather(w_in2, "fsdp", axis=0, tiled=True),
        lax.all_gather(b_in2, "fsdp", axis=0, tiled=True),
        lax.all_gather(w_res, "fsdp", axis=1, tiled=True),
        lax.all_gather(g_attn, "fsdp", axis=0, tiled=True),
        lax.all_gather(w_qkv, "fsdp", axis=0, tiled=True),
        lax.all_gather(w_out, "fsdp", axis=1, tiled=True),
        lax.all_gather(g_mlp, "fsdp", axis=0, tiled=True),
        lax.all_gather(w_up, "fsdp", axis=0, tiled=True),
        lax.all_gather(w_down, "fsdp", axis=1, tiled=True),
    )
    (
        full_in1,
        full_b1,
        full_in2,
        full_b2,
        full_res,
        full_gattn,
        full_qkv,
        full_out,
        full_gmlp,
        full_up,
        full_down,
    ) = gathered
    series = lengths.shape[0]
    seq_len = values.shape[0] // series
    patch_len = values.shape[1]
    slot_ids = jnp.arange(seq_len, dtype=jnp.int32)
    pad_count = seq_len - lengths
    padded = slot_ids[None, :] < pad_count[:, None]
    places = (slot_ids[None, :] - pad_count[:, None]).astype(f32)
    keep_mask = (1.0 - padded.astype(f32)).reshape(-1, 1)
    inputs = jnp.concatenate(
        [values.astype(f32) * keep_mask, jnp.broadcast_to(1.0 - keep_mask, values.shape)], 1
    ).astype(bf16)
    pre_act = jnp.dot(inputs, full_in1, preferred_element_type=f32) + full_b1.astype(f32)
    hidden = jax.nn.silu(pre_act).astype(bf16)
    resid0 = (
        jnp.dot(hidden, full_in2, preferred_element_type=f32)
        + full_b2.astype(f32)
        + jnp.dot(inputs, full_res, preferred_element_type=f32)
    )
    gain_attn = full_gattn.astype(f32)
    normed = rms_norm(resid0, gain_attn).astype(bf16)
    projected = jnp.einsum("td,dch->tch", normed, full_qkv, preferred_element_type=f32)
    local_heads = projected.shape[2] // HD
    head_shape = (series, seq_len, local_heads, HD)
    queries = rotate(projected[:, 0].reshape(head_shape), places).astype(bf16)
    key_rows = rotate(projected[:, 1].reshape(head_shape), places).astype(bf16)
    value_heads = projected[:, 2].reshape(head_shape).astype(bf16)
    causal = slot_ids[None, :] <= slot_ids[:, None]
    diagonal = slot_ids[None, :] == slot_ids[:, None]
    allowed = (causal[None] & (jnp.logical_not(padded)[:, None, :] | diagonal[None]))[:, None]
    scale = HD ** (-0.5)

    def score_block():
        raw = jnp.einsum("sqhe,skhe->shqk", queries, key_rows, preferred_element_type=f32) * scale
        return jnp.where(allowed, raw, -1e30)

    scores = score_block()
    row_max = jnp.max(scores, -1, keepdims=True)
    exponent = jnp.exp(scores - row_max)
    row_total = jnp.sum(exponent, -1, keepdims=True)
    log_total = row_max + jnp.log(row_total)
    attn_probs = (exponent / row_total).astype(bf16)
    attended = (
        jnp.einsum("shqk,skhe->sqhe", attn_probs, value_heads, preferred_element_type=f32)
        .reshape(-1, local_heads * HD)
        .astype(bf16)
    )
    branch_one = lax.psum(jnp.dot(attended, full_out, preferred_element_type=f32), "mp")
    resid1 = resid0 + branch_one
    gain_mlp = full_gmlp.astype(f32)
    normed2 = rms_norm(resid1, gain_mlp).astype(bf16)
    up_rows = jnp.dot(normed2, full_up, preferred_element_type=f32)
    mlp_hidden = activate(up_rows).astype(bf16)
    branch_two = lax.psum(
        jnp.dot(mlp_hidden, full_down, preferred_element_type=f32).astype(jnp.bfloat16), "mp"
    ).astype(jnp.float32)
    result = (resid1 + branch_two).astype(bf16)
    again = (
        lax.all_gather(w_in1, "fsdp", axis=1, tiled=True),
        lax.all_gather(b_in1, "fsdp", axis=0, tiled=True),
        lax.all_gather(w_in2, "fsdp", axis=0, tiled=True),
        lax.all_gather(b_in2, "fsdp", axis=0, tiled=True),
        lax.all_gather(w_res, "fsdp", axis=1, tiled=True),
        lax.all_gather(g_attn, "fsdp", axis=0, tiled=True),
        lax.all_gather(w_qkv, "fsdp", axis=0, tiled=True),
        lax.all_gather(w_out, "fsdp", axis=1, tiled=True),
        lax.all_gather(g_mlp, "fsdp", axis=0, tiled=True),
        lax.all_gather(w_up, "fsdp", axis=0, tiled=True),
        lax.all_gather(w_down, "fsdp", axis=1, tiled=True),
    )
    (
        back_in1,
        back_b1,
        back_in2,
        back_b2,
        back_res,
        back_gattn,
        back_qkv,
        back_out,
        back_gmlp,
        back_up,
        back_down,
    ) = again
    cot_rows = cotangent.astype(f32)
    grad_down = jnp.einsum("tf,td->fd", mlp_hidden, cotangent, preferred_element_type=f32)
    grad_hidden = jnp.einsum("td,fd->tf", cotangent, back_down, preferred_element_type=f32)
    unused_one, pull_mlp = jax.vjp(activate, up_rows)
    grad_up_rows = pull_mlp(grad_hidden)[0].astype(bf16)
    grad_up = jnp.einsum("td,tf->df", normed2, grad_up_rows, preferred_element_type=f32)
    norm_part2 = jnp.einsum("tf,df->td", grad_up_rows, back_up, preferred_element_type=f32)
    norm_grad2 = lax.psum(norm_part2, "mp")
    unused_two, pull_norm2 = jax.vjp(rms_norm, resid1, back_gmlp.astype(f32))
    resid_part1, grad_gmlp = pull_norm2(norm_grad2)
    resid1_grad = cot_rows + resid_part1
    out_grad = resid1_grad.astype(bf16)
    grad_out = jnp.einsum("th,td->hd", attended, out_grad, preferred_element_type=f32)
    attended_grad = (
        jnp.einsum("td,hd->th", out_grad, back_out, preferred_element_type=f32)
        .astype(bf16)
        .reshape(head_shape)
    )
    scores = score_block()
    probs_full = jnp.exp(scores - log_total)
    value_grad = jnp.einsum(
        "shqk,sqhe->skhe", probs_full.astype(bf16), attended_grad, preferred_element_type=f32
    )
    prob_grad = jnp.einsum(
        "sqhe,skhe->shqk", attended_grad, value_heads, preferred_element_type=f32
    )
    score_grad = (
        probs_full * (prob_grad - jnp.sum(prob_grad * probs_full, -1, keepdims=True))
    ).astype(bf16)
    query_grad = (
        jnp.einsum("shqk,skhe->sqhe", score_grad, key_rows, preferred_element_type=f32) * scale
    )
    key_grad = (
        jnp.einsum("shqk,sqhe->skhe", score_grad, queries, preferred_element_type=f32) * scale
    )
    width_local = local_heads * HD
    qkv_rows = jnp.stack(
        [
            rotate(query_grad, -places).reshape(-1, width_local),
            rotate(key_grad, -places).reshape(-1, width_local),
            value_grad.reshape(-1, width_local),
        ],
        1,
    ).astype(bf16)
    grad_qkv = jnp.einsum("td,tch->dch", normed, qkv_rows, preferred_element_type=f32)
    norm_part1 = jnp.einsum("tch,dch->td", qkv_rows, back_qkv, preferred_element_type=f32)
    norm_grad1 = lax.psum(norm_part1, "mp")
    unused_three, pull_norm1 = jax.vjp(rms_norm, resid0, back_gattn.astype(f32))
    resid_part0, grad_gattn = pull_norm1(norm_grad1)
    resid0_grad = (resid1_grad + resid_part0).astype(bf16)
    grad_in2 = jnp.einsum("th,td->hd", hidden, resid0_grad, preferred_element_type=f32)
    grad_b2 = jnp.sum(resid0_grad.astype(f32), 0)
    grad_res = jnp.einsum("tp,td->pd", inputs, resid0_grad, preferred_element_type=f32)
    hidden_grad = jnp.einsum("td,hd->th", resid0_grad, back_in2, preferred_element_type=f32)
    unused_four, pull_silu = jax.vjp(jax.nn.silu, pre_act)
    pre_grad = pull_silu(hidden_grad)[0].astype(bf16)
    grad_in1 = jnp.einsum("tp,th->ph", inputs, pre_grad, preferred_element_type=f32)
    grad_b1 = jnp.sum(pre_grad.astype(f32), 0)
    input_grad = jnp.einsum(
        "th,ph->tp", pre_grad, back_in1, preferred_element_type=f32
    ) + jnp.einsum("td,pd->tp", resid0_grad, back_res, preferred_element_type=f32)
    values_grad = input_grad[:, :patch_len] * keep_mask
    shares = tuple(
        (
            lax.psum_scatter(grad_in1, "fsdp", scatter_dimension=1, tiled=True),
            lax.psum_scatter(grad_b1, "fsdp", scatter_dimension=0, tiled=True),
            lax.psum_scatter(grad_in2, "fsdp", scatter_dimension=0, tiled=True),
            lax.psum_scatter(grad_b2, "fsdp", scatter_dimension=0, tiled=True),
            lax.psum_scatter(grad_res, "fsdp", scatter_dimension=1, tiled=True),
            lax.psum_scatter(grad_gattn, "fsdp", scatter_dimension=0, tiled=True),
            lax.psum_scatter(grad_qkv, "fsdp", scatter_dimension=0, tiled=True),
            lax.psum_scatter(grad_out, "fsdp", scatter_dimension=1, tiled=True),
            lax.psum_scatter(grad_gmlp, "fsdp", scatter_dimension=0, tiled=True),
            lax.psum_scatter(grad_up, "fsdp", scatter_dimension=0, tiled=True),
            lax.psum_scatter(grad_down, "fsdp", scatter_dimension=1, tiled=True),
        )
    )
    return (result, values_grad) + shares


def fused_device(
    values,
    lengths,
    w_in1,
    b_in1,
    w_in2,
    b_in2,
    w_res,
    g_attn,
    w_qkv,
    w_out,
    g_mlp,
    w_up,
    w_down,
    cotangent,
):
    rows, width = cotangent.shape
    half = w_out.shape[0]
    blk = w_in2.shape[0]
    patch = values.shape[1]
    tok_in = w_in1.shape[0]
    heads = half // HD

    def column(vec):
        return vec[:, None]

    def lanes(parts):
        used = sum(p.shape[1] for p in parts)
        return jnp.concatenate(parts + [jnp.zeros((blk, PL - used), bf16)], 1)

    pack = jnp.stack(
        [
            lanes([w_in1.T, column(b_in1)]),
            lanes([w_res.T, column(b_in2), column(g_attn), column(g_mlp)]),
        ]
    )
    vmem = pl.BlockSpec(memory_space=pltpu.VMEM)
    hbm = pl.BlockSpec(memory_space=pl.ANY)
    out_shape = (
        jax.ShapeDtypeStruct((rows, width), bf16),
        jax.ShapeDtypeStruct((rows, patch), f32),
        jax.ShapeDtypeStruct((2, blk, PL), f32),
        jax.ShapeDtypeStruct((blk, width), f32),
        jax.ShapeDtypeStruct((3, blk, half), f32),
        jax.ShapeDtypeStruct((blk, half), f32),
        jax.ShapeDtypeStruct((blk, half), f32),
        jax.ShapeDtypeStruct((blk, half), f32),
    )
    V = pltpu.VMEM
    scratch = [
        V((NW, width, half), bf16),
        V((2, width, PL), bf16),
        V((NW, width, half), bf16),
        V((width, PL), bf16),
        V((NW, SLOTS, blk, half), bf16),
        V((SLOTS, blk, PL), bf16),
        V((2, rows, half), f32),
        V((rows, width), f32),
        V((2, rows, width), f32),
        V((2, rows, width), f32),
        V((rows, width), bf16),
        V((rows, width), bf16),
        V((rows, width), bf16),
        V((rows, width), bf16),
        V((rows, width), bf16),
        V((rows, half), bf16),
        V((rows, half), bf16),
        V((rows, half), bf16),
        V((heads, rows, rows), f32),
        V((rows, half), bf16),
        V((rows, half), f32),
        V((rows, half), bf16),
        V((rows, width), bf16),
        V((rows, half), bf16),
        V((rows, half), bf16),
        V((rows, half), bf16),
        V((rows, half), bf16),
        V((rows, width), f32),
        V((rows, width), bf16),
        V((rows, half), f32),
        V((rows, half), f32),
        V((rows, rows), f32),
        V((rows, PL), bf16),
        V((2, 8, width), f32),
        V((2, 16, width), bf16),
        V((8, width), f32),
        V((rows, PL), f32),
        V((blk, half), f32),
        V((blk, PL), f32),
        V((2, blk, half), f32),
        V((2, blk, PL), f32),
        pltpu.SemaphoreType.DMA((8,)),
        pltpu.SemaphoreType.DMA((8, 16)),
        pltpu.SemaphoreType.DMA((8,)),
        pltpu.SemaphoreType.DMA((8, SLOTS)),
        pltpu.SemaphoreType.DMA((9,)),
        pltpu.SemaphoreType.DMA((9,)),
        pltpu.SemaphoreType.DMA((9,)),
    ]
    out, d_values, d_pack, d_in2, d_qkv, d_out_t, d_up, d_down_t = pl.pallas_call(
        fused_kernel,
        name="layer",
        out_shape=out_shape,
        in_specs=[pl.BlockSpec(memory_space=pltpu.SMEM), vmem] + [hbm] * 7,
        out_specs=(vmem,) * len(out_shape),
        scratch_shapes=scratch,
        compiler_params=pltpu.CompilerParams(
            collective_id=0, has_side_effects=True, vmem_limit_bytes=VMEM_BYTES
        ),
    )(
        lengths,
        values,
        pack,
        w_in2,
        jnp.transpose(w_qkv, (1, 0, 2)),
        w_out.T,
        w_up,
        w_down.T,
        cotangent,
    )
    return (
        out,
        d_values,
        d_pack[0, :, :tok_in].T,
        d_pack[0, :, tok_in],
        d_in2,
        d_pack[1, :, tok_in],
        d_pack[1, :, :tok_in].T,
        d_pack[1, :, tok_in + 1],
        jnp.transpose(d_qkv, (1, 0, 2)),
        d_out_t.T,
        d_pack[1, :, tok_in + 2],
        d_up,
        d_down_t.T,
    )


def on_device(*args):
    blk, width = args[4].shape
    half = args[9].shape[0]
    shards = width // blk
    series = args[1].shape[0]
    fits = (
        shards == 16
        and 2 * half == width
        and blk % 16 == 0
        and half % 128 == 0
        and args[0].shape[0] % 64 == 0
        and series <= 8
    )
    return (fused_device if fits else general_device)(*args)


def solution(mesh):
    in_specs = (
        P("fsdp", None),
        P("fsdp"),
        P(None, "fsdp"),
        P("fsdp"),
        P("fsdp", None),
        P("fsdp"),
        P(None, "fsdp"),
        P("fsdp"),
        P("fsdp", None, "mp"),
        P("mp", "fsdp"),
        P("fsdp"),
        P("fsdp", "mp"),
        P("mp", "fsdp"),
        P("fsdp", None),
    )
    out_specs = (
        P("fsdp", None),
        P("fsdp", None),
        P(None, "fsdp"),
        P("fsdp"),
        P("fsdp", None),
        P("fsdp"),
        P(None, "fsdp"),
        P("fsdp"),
        P("fsdp", None, "mp"),
        P("mp", "fsdp"),
        P("fsdp"),
        P("fsdp", "mp"),
        P("mp", "fsdp"),
    )
    return jax.shard_map(
        on_device, mesh=mesh, in_specs=in_specs, out_specs=out_specs, check_vma=False
    )
```

```python
import functools
import math

import jax
import jax.numpy as jnp
from jax import lax
from jax.experimental import pallas as pl
from jax.experimental.pallas import tpu as pltpu
from jax.sharding import PartitionSpec as P

HD = 80
MESH = pl.DeviceIdType.MESH
VMEM_BYTES = 63 * 2**20
f32 = jnp.float32
bf16 = jnp.bfloat16

IN2, WQ, WK, WV, WOUT, WUP, WDOWN, PACK = range(8)
NW = 7
PL = 128
PLANE_FIRST = ()
Z_FIRST = ()
CHAIN_LAST = tuple(w for w in range(NW) if w not in Z_FIRST)
SLOT_A, SLOT_X, SLOT_Y, SLOT_V, SLOTS = 0, 4, 8, 12, 16
Z_RELAY, Z_NEAR, Z_FAR, Z_A, Z_X, Z_Y, Z_SLOTS = 0, 8, 12, 16, 17, 18, 19


def dot(left, right, left_dim, right_dim):
    return lax.dot_general(
        left, right, (((left_dim,), (right_dim,)), ((), ())), preferred_element_type=f32
    )


def layer_kernel(
    lengths,
    values_t,
    w_in1,
    w_res,
    b_in1,
    b_in2,
    g_attn,
    g_mlp,
    in2,
    qkv,
    out_t,
    up,
    down_t,
    cot_hbm,
    o_out,
    o_dval,
    o_in1,
    o_b1,
    o_in2,
    o_b2,
    o_res,
    o_gattn,
    o_qkv,
    o_wout,
    o_gmlp,
    o_up,
    o_down,
    W,
    PK,
    G,
    GP,
    R,
    RZ,
    RP,
    R0,
    R1,
    S,
    X,
    SB,
    XB,
    hid,
    nrm,
    nrm2,
    q,
    k,
    v,
    prob,
    att,
    gprime,
    mlp,
    cot,
    dup,
    dq,
    dk,
    dv,
    tmp,
    dr0,
    rope_c,
    rope_s,
    bias,
    inx,
    gains,
    dgs,
    accg,
    keep_col,
    fin_in2,
    fin_pack,
    ag_send,
    ag_recv,
    rs_send,
    rs_recv,
    ex_send,
    ex_recv,
    lsem,
):
    rows, width = cot.shape
    half = W.shape[2]
    blk = in2.shape[0]
    series = lengths.shape[0]
    seq = rows // series
    heads = half // HD
    patch = values_t.shape[0]

    f = lax.axis_index("fsdp")
    m = lax.axis_index("mp")
    x = lax.rem(f, 2)
    y = lax.rem(lax.div(f, 2), 2)
    z = lax.div(f, 4)
    c0 = f - 4 * z
    cx = c0 + 1 - 2 * x
    cy = c0 + 2 - 4 * y
    cd = 3 - c0
    XN, YN, SIB = (4 * z + cx, m), (4 * z + cy, m), (f, 1 - m)
    z_high = (z >= 2).astype(jnp.int32)
    inner = jnp.logical_and(z > 0, z < 3)
    z_inner = inner.astype(jnp.int32)
    z_near = z + 1 - 2 * lax.rem(z, 2)
    z_far = 2 - z_high
    z_even = lax.rem(z, 2) == 0

    def plane(zb):
        return (4 * zb + c0, m)

    def near(i):
        swap = (i == 0).astype(jnp.int32) - (i == 1).astype(jnp.int32)
        low = i + z_inner * swap
        return low + z_high * (3 - 2 * low)

    def far(i):
        return near(3 - i)

    def each_plane(order, body, start=0):
        def step(i, carry):
            body(order(i))
            return carry

        lax.fori_loop(start, 4, step, 0)

    def each_other_plane(body):
        each_plane(near, body, 1)

    def row_of(b):
        return pl.ds(pl.multiple_of(b * blk, 16), blk)

    def w_block(w, b):
        return PK.at[m, row_of(b)] if w == PACK else W.at[w, row_of(b)]

    def g_block(w, b):
        return GP.at[row_of(b)] if w == PACK else G.at[w, row_of(b)]

    def r_block(w, s):
        if w == PACK:
            return RP.at[s]
        if w in Z_FIRST:
            return RZ.at[Z_FIRST.index(w), s]
        return R.at[CHAIN_LAST.index(w), s]

    def remote(src, dst, send, recv, dev):
        return pltpu.make_async_remote_copy(
            src_ref=src, dst_ref=dst, send_sem=send, recv_sem=recv, device_id=dev, device_id_type=MESH
        )

    def ag_push(w, b, *devs):
        ref = w_block(w, b)
        for dev in devs:
            remote(ref, ref, ag_send.at[w], ag_recv.at[w, b], dev).start()

    def ag_await(w, b):
        ref = w_block(w, b)
        remote(ref, ref, ag_send.at[w], ag_recv.at[w, b], XN).wait_recv()

    mcols = pl.ds(pl.multiple_of(m * half, 128), half)

    def own_copy(w):
        if w == IN2:
            src = in2.at[:, mcols]
        elif w in (WQ, WK, WV):
            src = qkv.at[w - WQ]
        else:
            src = {WOUT: out_t, WUP: up, WDOWN: down_t}[w]
        return pltpu.make_async_copy(src, w_block(w, f), lsem.at[w])

    def ag_own(w):
        if w != PACK:
            own_copy(w).wait()
        ag_push(w, f, XN, YN)
        if w in PLANE_FIRST:
            ag_push(w, f, plane(z_near), plane(z_far))
        else:
            each_other_plane(lambda zb: ag_push(w, f, plane(zb)))

    def ag_column(w):
        def body(zb):
            b = 4 * zb + c0
            ag_await(w, b)
            ag_push(w, b, XN, YN)

        each_other_plane(body)

    def ag_pass(w, zb, even, *more):
        ag_await(w, 4 * zb + cx)

        @pl.when(even)
        def _():
            ag_push(w, 4 * zb + cx, YN)

        ag_push(w, 4 * zb + cx, *more)
        ag_await(w, 4 * zb + cy)

        @pl.when(jnp.logical_not(even))
        def _():
            ag_push(w, 4 * zb + cy, XN)

        ag_push(w, 4 * zb + cy, *more)

    def ag_plane(w):
        if w in PLANE_FIRST:
            to = (plane(z_near), plane(z_far))
            ag_pass(w, z, z_even, *to)
            ag_await(w, 4 * z + cd)
            ag_push(w, 4 * z + cd, *to)
        else:
            each_plane(near, lambda zb: ag_pass(w, zb, lax.rem(zb, 2) == 0))

    def ag_relay(w):
        @pl.when(inner)
        def _():
            for zb in (3 - z, 3 * (1 - z_high)):
                for c in (c0, cx, cy, cd):
                    ag_await(w, 4 * zb + c)
                    ag_push(w, 4 * zb + c, plane(3 * z_high))

    def ag_last(w):
        if w in PLANE_FIRST:
            for c in (c0, cx, cy, cd):
                ag_await(w, 4 * z_near + c)

            @pl.when(jnp.logical_not(inner))
            def _():
                for zb in (z_far, 3 - z):
                    for c in (c0, cx, cy, cd):
                        ag_await(w, 4 * zb + c)
        else:
            each_plane(near, lambda zb: ag_await(w, 4 * zb + cd))

    final_of = {
        IN2: lambda: fin_in2.at[m],
        WQ: lambda: o_qkv.at[0],
        WK: lambda: o_qkv.at[1],
        WV: lambda: o_qkv.at[2],
        WOUT: lambda: o_wout,
        WUP: lambda: o_up,
        WDOWN: lambda: o_down,
        PACK: lambda: fin_pack.at[m],
    }

    def rs_push(w, src, slot, dev):
        remote(src, r_block(w, slot), rs_send.at[w], rs_recv.at[w, slot], dev).start()

    def rs_await(w, slot):
        ref = r_block(w, slot)
        remote(ref, ref, rs_send.at[w], rs_recv.at[w, slot], XN).wait_recv()

    def add_to(ref, other):
        ref[...] = (ref[...].astype(f32) + other[...].astype(f32)).astype(bf16)

    def sum3(a, b, c):
        return a[...].astype(f32) + b[...].astype(f32) + c[...].astype(f32)

    def rs_start(w):
        if w in Z_FIRST:
            cs = (cd, cx, cy, c0)

            @pl.when(jnp.logical_not(inner))
            def _():
                for zb in (3 - z, z_far):
                    for c in cs:
                        slot = Z_RELAY + 4 * lax.rem(zb, 2) + c
                        rs_push(w, g_block(w, 4 * zb + c), slot, plane(1 + z_high))

            for c in cs:
                rs_push(w, g_block(w, 4 * z_near + c), Z_NEAR + c, plane(z_near))
            return

        def body(zb):
            even = lax.rem(zb, 2) == 0

            @pl.when(even)
            def _():
                rs_push(w, g_block(w, 4 * zb + cd), SLOT_A + zb, YN)
                rs_push(w, g_block(w, 4 * zb + cy), SLOT_Y + zb, YN)

            @pl.when(jnp.logical_not(even))
            def _():
                rs_push(w, g_block(w, 4 * zb + cd), SLOT_A + zb, XN)
                rs_push(w, g_block(w, 4 * zb + cx), SLOT_X + zb, XN)

        each_plane(far, body)

    def turn(w, slot_a, even, own_x, own_y, slot_x, slot_y):
        rs_await(w, slot_a)
        ref = r_block(w, slot_a)

        @pl.when(even)
        def _():
            add_to(ref, own_x)
            rs_push(w, ref, slot_x, XN)

        @pl.when(jnp.logical_not(even))
        def _():
            add_to(ref, own_y)
            rs_push(w, ref, slot_y, YN)

    def rs_turn(w):
        if w in Z_FIRST:
            turn(w, Z_A, z_even, r_block(w, Z_NEAR + cx), r_block(w, Z_NEAR + cy), Z_X, Z_Y)
            return
        each_plane(
            far,
            lambda zb: turn(
                w,
                SLOT_A + zb,
                lax.rem(zb, 2) == 0,
                g_block(w, 4 * zb + cx),
                g_block(w, 4 * zb + cy),
                SLOT_X + zb,
                SLOT_Y + zb,
            ),
        )

    def rs_relay(w):
        @pl.when(inner)
        def _():
            for zb in (3 * (1 - z_high), z_far):
                for c in (cd, cx, cy, c0):
                    slot = Z_RELAY + 4 * lax.rem(zb, 2) + c
                    rs_await(w, slot)
                    ref = r_block(w, slot)
                    add_to(ref, g_block(w, 4 * zb + c))
                    rs_push(w, ref, Z_FAR + c, plane(zb))

    def rs_zsum(w):
        for c in (cd, cx, cy, c0):
            rs_await(w, Z_NEAR + c)
            rs_await(w, Z_FAR + c)
            ref = r_block(w, Z_NEAR + c)
            total = sum3(ref, r_block(w, Z_FAR + c), g_block(w, 4 * z + c))
            if c is c0:
                final_of[w]()[...] = total
            else:
                ref[...] = total.astype(bf16)
            if c is cd:

                @pl.when(z_even)
                def _():
                    rs_push(w, ref, Z_A, YN)

                @pl.when(jnp.logical_not(z_even))
                def _():
                    rs_push(w, ref, Z_A, XN)

            if c is cx:

                @pl.when(jnp.logical_not(z_even))
                def _():
                    rs_push(w, ref, Z_X, XN)

            if c is cy:

                @pl.when(z_even)
                def _():
                    rs_push(w, ref, Z_Y, YN)

    def plane_sum(w, zb):
        rs_await(w, SLOT_X + zb)
        rs_await(w, SLOT_Y + zb)
        return sum3(g_block(w, 4 * zb + c0), r_block(w, SLOT_X + zb), r_block(w, SLOT_Y + zb))

    def rs_out(w):
        def body(zb):
            ref = r_block(w, SLOT_X + zb)
            ref[...] = plane_sum(w, zb).astype(bf16)
            rs_push(w, ref, SLOT_V + z, plane(zb))

        each_other_plane(body)
        final_of[w]()[...] = plane_sum(w, z)

    def rs_final(w):
        final = final_of[w]()
        if w in Z_FIRST:
            rs_await(w, Z_X)
            rs_await(w, Z_Y)
            final[...] = sum3(final, r_block(w, Z_X), r_block(w, Z_Y))
            return

        for i in (1, 2, 3):
            rs_await(w, SLOT_V + near(jnp.int32(i)))
        parts = [r_block(w, SLOT_V + near(jnp.int32(i)))[...].astype(f32) for i in (1, 2, 3)]
        final[...] = final[...] + (parts[0] + parts[1] + parts[2])

    def exchange(i):
        src, dst = {
            0: lambda: (PK.at[m], PK.at[m]),
            1: lambda: (R0.at[m], R0.at[m]),
            2: lambda: (S.at[0], X.at[0]),
            3: lambda: (SB, XB),
            4: lambda: (S.at[1], X.at[1]),
            5: lambda: (S.at[0], X.at[0]),
            6: lambda: (S.at[1], X.at[1]),
            7: lambda: (fin_in2.at[m], fin_in2.at[m]),
            8: lambda: (fin_pack.at[m], fin_pack.at[m]),
        }[i]()
        return remote(src, dst, ex_send.at[i], ex_recv.at[i], SIB)

    def swap_start(i):
        exchange(i).start()

    def swap_wait(i):
        exchange(i).wait()

    def by_rows(step, body, unroll=4):
        def one(i, carry):
            body(pl.ds(pl.multiple_of(i * step, step), step))
            return carry

        lax.fori_loop(0, rows // step, one, 0, unroll=unroll)

    halves = (slice(0, half), slice(half, width))

    lens = [lengths[s] for s in range(series)]

    def pad_of(slot):
        total = jnp.zeros(slot.shape, jnp.int32)
        for s in range(series):
            inside = jnp.logical_and(slot >= s * seq, slot < (s + 1) * seq)
            total = jnp.where(inside, (s + 1) * seq - lens[s], total)
        return total

    def series_of(slot):
        total = jnp.zeros(slot.shape, jnp.int32)
        for s in range(1, series):
            total = total + (slot >= s * seq).astype(jnp.int32)
        return total

    lane = lax.broadcasted_iota(jnp.int32, (1, half), 1).astype(f32)
    in_head = lane - HD * jnp.floor((lane + 0.5) / HD)
    first = in_head < HD // 2

    def prepare():
        slot_col = lax.broadcasted_iota(jnp.int32, (rows, 1), 0)
        keep = jnp.broadcast_to((slot_col >= pad_of(slot_col)).astype(f32), keep_col.shape)
        keep_col[...] = keep
        lane_i = lax.broadcasted_iota(jnp.int32, (rows, PL), 1)
        tall = jnp.concatenate([values_t[...].astype(f32), jnp.zeros((PL - patch, rows), f32)], 0)
        inx[...] = jnp.where(
            lane_i < patch,
            tall.T * keep,
            jnp.where(lane_i < 2 * patch, 1.0 - keep, (lane_i == 2 * patch).astype(f32)),
        ).astype(bf16)

        key_slot = lax.broadcasted_iota(jnp.int32, (1, rows), 1)
        key_ok = (key_slot >= pad_of(key_slot)).astype(jnp.int32)
        key_series = series_of(key_slot)

        def bias_rows(s):
            shape = (s.size, rows)
            a = lax.broadcasted_iota(jnp.int32, shape, 0) + s.start
            b = jnp.broadcast_to(key_slot, shape)
            same = series_of(a) == jnp.broadcast_to(key_series, shape)
            ok = jnp.logical_or(jnp.broadcast_to(key_ok, shape) == 1, a == b)
            allowed = jnp.logical_and(jnp.logical_and(same, b <= a), ok)
            bias[s, :] = jnp.where(allowed, 0.0, -1e30)

        by_rows(32, bias_rows, 1)
        turn_i = jnp.where(first, in_head, in_head - HD // 2)
        frequency = jnp.exp(turn_i * (-2.0 * math.log(10000.0) / HD))

        def rope_rows(s):
            slot = lax.broadcasted_iota(jnp.int32, (s.size, 1), 0) + s.start
            place = (slot - pad_of(slot)).astype(f32)
            angle = place * frequency
            rope_c[s, :] = jnp.cos(angle)
            sine = jnp.sin(angle)
            rope_s[s, :] = jnp.where(first, -sine, sine)

        by_rows(16, rope_rows, 1)

    def rope(t, s, inverse):
        other = jnp.where(first, pltpu.roll(t, half - HD // 2, 1), pltpu.roll(t, HD // 2, 1))
        turned = other * rope_s[s, :]
        return t * rope_c[s, :] - turned if inverse else t * rope_c[s, :] + turned

    gain_lane = lax.broadcasted_iota(jnp.int32, (16, PL), 1)

    def pre_act():
        for cols in halves:
            tmp[:, cols] = dot(inx[...], PK[0, cols, :], 1, 1)

    def token_hidden():
        for i in range(2):
            pick = (gain_lane == 2 * patch + 1 + i).astype(bf16)
            gains[i] = dot(pick, PK[1], 1, 1)[0:8]
        pre_act()

        def silu_rows(s):
            t = tmp[s, :]
            hid[s, :] = (t / (1.0 + jnp.exp(-t))).astype(bf16)

        by_rows(16, silu_rows)

    def token_out():
        R0[m] = dot(hid[...], W[IN2], 1, 0) + dot(inx[...], PK[1, mcols, :], 1, 1)

    def norm_rows(load, gain, out):
        def body(s):
            a, b = load(s)
            mean = (jnp.sum(a * a, -1, keepdims=True) + jnp.sum(b * b, -1, keepdims=True)) / width
            scale = lax.rsqrt(mean + 1e-06)
            out[s, halves[0]] = (a * scale * gain[0:1, halves[0]]).astype(bf16)
            out[s, halves[1]] = (b * scale * gain[0:1, halves[1]]).astype(bf16)

        by_rows(16, body)

    def norm_first():
        norm_rows(lambda s: (R0[0, s, :], R0[1, s, :]), gains.at[0], nrm)

    def project(w, out):
        tmp[:, halves[0]] = dot(nrm[...], W[w], 1, 0)

        def body(s):
            out[s, :] = rope(tmp[s, halves[0]], s, False).astype(bf16)

        by_rows(16, body)

    def project_v():
        v[...] = dot(nrm[...], W[WV], 1, 0).astype(bf16)

    win = 256
    scale = HD ** (-0.5)
    win_lane = lax.broadcasted_iota(jnp.int32, (1, win), 1)

    def head_window(h):
        low = jnp.minimum(lax.div(h * HD, 128) * 128, half - win)
        inside = jnp.logical_and(win_lane >= h * HD - low, win_lane < h * HD - low + HD)
        return pl.ds(pl.multiple_of(low, 128), win), inside

    def only(inside, t):
        return jnp.where(inside, t.astype(f32), 0.0).astype(bf16)

    def attend():
        att[...] = jnp.zeros_like(att)

        def one(h, carry):
            cols, inside = head_window(h)
            score = dot(only(inside, q[:, cols]), k[:, cols], 1, 1) * scale + bias[...]
            exponent = jnp.exp(score - jnp.max(score, -1, keepdims=True))
            p = exponent / jnp.sum(exponent, -1, keepdims=True)
            prob[h] = p
            mixed = dot(p.astype(bf16), v[:, cols], 1, 0)
            att[:, cols] = jnp.where(inside, mixed, att[:, cols].astype(f32)).astype(bf16)
            return carry

        lax.fori_loop(0, heads, one, 0, unroll=2)

    def widen(dst, terms):
        for cols in halves:
            total = None
            for left, w in terms:
                part = dot(left[...], W[w, cols, :], 1, 1)
                total = part if total is None else total + part
            dst[:, cols] = total.astype(dst.dtype)

    def attend_out():
        widen(S.at[0], [(att, WOUT)])

    def norm_second():
        def body(s):
            for i, cols in enumerate(halves):
                R1[s, cols] = R0[i, s, :] + (S[0, s, cols] + X[0, s, cols])

        by_rows(16, body)
        norm_rows(lambda s: (R1[s, halves[0]], R1[s, halves[1]]), gains.at[1], nrm2)

    def feed_up():
        tmp[:, halves[0]] = dot(nrm2[...], W[WUP], 1, 0)

        def gelu_rows(s):
            t = tmp[s, halves[0]]
            phi = 0.5 * (1.0 + lax.erf(t * (2.0**-0.5)))
            mlp[s, :] = (t * phi).astype(bf16)
            gprime[s, :] = phi + t * jnp.exp(-0.5 * t * t) * ((2.0 * math.pi) ** -0.5)

        by_rows(16, gelu_rows)

    def weight_grad(w, left, right):
        for r in halves:
            G[w, r, :] = dot(left[:, r], right, 0, 0).astype(bf16)

    def grad_down():
        cot_copy.wait()
        weight_grad(WDOWN, cot, mlp[...])

    def grad_hidden():
        tmp[:, halves[0]] = dot(cot[...], W[WDOWN], 1, 0)

        def dup_rows(s):
            dup[s, :] = (tmp[s, halves[0]] * gprime[s, :]).astype(bf16)

        by_rows(16, dup_rows)

    def grad_up():
        weight_grad(WUP, nrm2, dup[...])

    def feed_down():
        widen(SB, [(mlp, WDOWN)])

    def grad_norm2():
        widen(S.at[1], [(dup, WUP)])

    def write_output():
        def body(s):
            o_out[s, :] = (R1[s, :] + (SB[s, :].astype(f32) + XB[s, :].astype(f32))).astype(bf16)

        by_rows(16, body)

    def norm_grad(load, i_part, gain, base, out, keep_sum):
        def body(i, carry):
            s = pl.ds(pl.multiple_of(i * 16, 16), 16)
            xs = load(s)
            mean = sum(jnp.sum(t * t, -1, keepdims=True) for t in xs) / width
            r = lax.rsqrt(mean + 1e-06)
            n1 = [t * r for t in xs]
            dn = [S[i_part, s, c] + X[i_part, s, c] for c in halves]
            gd = [gain[0:1, c] * t for c, t in zip(halves, dn)]
            along = sum(jnp.sum(a * b, -1, keepdims=True) for a, b in zip(gd, n1)) / width
            for c, a, b in zip(halves, gd, n1):
                out(s, c, base(s, c) + r * (a - b * along))
            for c, a, b in zip(halves, dn, n1):
                prod = a * b
                accg[:, c] += prod[0:8] + prod[8:16]
            return carry

        accg[...] = jnp.zeros_like(accg)
        lax.fori_loop(0, rows // 16, body, 0, unroll=4)
        total = accg[...]
        high = total.astype(bf16)
        keep_sum[...] = jnp.concatenate([high.astype(f32), total - high.astype(f32)], 0).astype(bf16)

    def norm_grad2():
        def out(s, c, t):
            R1[s, c] = t
            nrm2[s, c] = t.astype(bf16)

        norm_grad(
            lambda s: [R1[s, c] for c in halves],
            1,
            gains.at[1],
            lambda s, c: cot[s, c].astype(f32),
            out,
            dgs.at[1],
        )

    def norm_grad1():
        def out(s, c, t):
            dr0[s, c] = t.astype(bf16)

        norm_grad(
            lambda s: [R0[i, s, :] for i in range(2)],
            0,
            gains.at[0],
            lambda s, c: R1[s, c],
            out,
            dgs.at[0],
        )

    def grad_out():
        weight_grad(WOUT, nrm2, att[...])

    def grad_attended():
        att[...] = dot(nrm2[...], W[WOUT], 1, 0).astype(bf16)

    def attend_back():
        dv[...] = jnp.zeros_like(dv)
        tmp[...] = jnp.zeros_like(tmp)

        def one(h, carry):
            cols, inside = head_window(h)
            cols2 = pl.ds(pl.multiple_of(cols.start + half, 128), win)
            p = prob[h]
            da = only(inside, att[:, cols])
            dp = dot(da, v[:, cols], 1, 1)
            ds = (p * (dp - jnp.sum(dp * p, -1, keepdims=True))).astype(bf16)
            dv_h = dot(p.astype(bf16), da, 0, 0)
            dq_h = dot(ds, k[:, cols], 1, 0) * scale
            dk_h = dot(ds, q[:, cols], 0, 0) * scale
            dv[:, cols] = jnp.where(inside, dv_h, dv[:, cols].astype(f32)).astype(bf16)
            tmp[:, cols] = jnp.where(inside, dq_h, tmp[:, cols])
            tmp[:, cols2] = jnp.where(inside, dk_h, tmp[:, cols2])
            return carry

        lax.fori_loop(0, heads, one, 0, unroll=2)

    def unrotate():
        def body(s):
            dq[s, :] = rope(tmp[s, halves[0]], s, True).astype(bf16)
            dk[s, :] = rope(tmp[s, halves[1]], s, True).astype(bf16)

        by_rows(16, body)

    def grad_norm1():
        widen(S.at[0], [(dq, WQ), (dk, WK), (dv, WV)])

    def grad_in2():
        weight_grad(IN2, hid, dr0[:, mcols])

    def grad_token():
        for c in halves:
            S[1, :, c] = dot(dr0[:, mcols], W[IN2, c, :], 1, 1)

    def grad_pre():
        def body(s):
            t = tmp[s, :]
            sig = 1.0 / (1.0 + jnp.exp(-t))
            grad = (S[1, s, :] + X[1, s, :]) * (sig * (1.0 + t * (1.0 - sig)))
            nrm[s, :] = grad.astype(bf16)

        by_rows(16, body)

    def grad_values():
        total = dot(nrm[...], PK[0], 1, 0) + dot(dr0[...], PK[1], 1, 0)
        o_dval[...] = (total * keep_col[...]).T[0:patch, :]

    def grad_pack():
        @pl.when(m == 0)
        def _():
            for r in halves:
                GP[r, :] = dot(nrm[:, r], inx[...], 0, 0).astype(bf16)

        @pl.when(m == 1)
        def _():
            for r in halves:
                total = dot(dr0[:, r], inx[...], 0, 0)
                for i in range(2):
                    pick = (gain_lane == 2 * patch + 1 + i).astype(bf16)
                    total = total + dot(dgs[i, :, r], pick, 0, 0)
                GP[r, :] = total.astype(bf16)

    def write_small():
        for i, c in enumerate(halves):
            o_in2[:, c] = fin_in2[i]
        tok_in = 2 * patch
        one, two = fin_pack[0].T, fin_pack[1].T
        o_in1[...] = one[0:tok_in]
        o_b1[...] = one[tok_in : tok_in + 1]
        o_res[...] = two[0:tok_in]
        o_b2[...] = two[tok_in : tok_in + 1]
        o_gattn[...] = two[tok_in + 1 : tok_in + 2]
        o_gmlp[...] = two[tok_in + 2 : tok_in + 3]

    barrier = pltpu.get_barrier_semaphore()
    for dev in (XN, YN, SIB):
        pl.semaphore_signal(barrier, inc=1, device_id=dev, device_id_type=MESH)
    each_other_plane(
        lambda zb: pl.semaphore_signal(barrier, inc=1, device_id=plane(zb), device_id_type=MESH)
    )
    order = (IN2, WQ, WK, WV, WOUT, WUP, WDOWN)
    for w in order:
        own_copy(w).start()
    cot_copy = pltpu.make_async_copy(cot_hbm, cot, lsem.at[8])
    cot_copy.start()

    @pl.when(m == 0)
    def _():
        pack_block(PK.at[0, row_of(f)], w_in1, [b_in1])

    @pl.when(m == 1)
    def _():
        pack_block(PK.at[1, row_of(f)], w_res, [b_in2, g_attn, g_mlp])

    pl.semaphore_wait(barrier, 6)

    ag_own(PACK)
    ag_own(IN2)
    ag_column(PACK)
    ag_own(WQ)
    ag_plane(PACK)
    ag_own(WK)
    ag_own(WDOWN)
    prepare()
    ag_own(WV)
    ag_column(IN2)
    ag_plane(IN2)
    ag_last(PACK)
    ag_column(WQ)
    swap_start(0)
    swap_wait(0)
    token_hidden()
    ag_last(IN2)
    ag_own(WUP)
    ag_own(WOUT)
    ag_plane(WQ)
    ag_column(WK)
    token_out()
    ag_column(WV)
    ag_plane(WV)
    ag_plane(WK)
    swap_start(1)
    swap_wait(1)
    norm_first()
    ag_last(WQ)
    ag_column(WOUT)
    ag_last(WV)
    project(WQ, q)
    ag_column(WUP)
    ag_plane(WOUT)
    ag_last(WK)
    ag_plane(WUP)
    project_v()
    project(WK, k)
    ag_column(WDOWN)
    ag_last(WOUT)
    attend()
    attend_out()
    swap_start(2)
    ag_last(WUP)
    swap_wait(2)
    norm_second()
    ag_plane(WDOWN)
    feed_up()
    grad_down()
    rs_start(WDOWN)
    ag_last(WDOWN)
    feed_down()
    grad_hidden()
    grad_norm2()
    swap_start(3)
    swap_wait(3)
    swap_start(4)
    grad_up()
    rs_start(WUP)
    write_output()
    swap_wait(4)
    norm_grad2()
    grad_out()
    rs_turn(WDOWN)
    grad_attended()
    rs_start(WOUT)
    attend_back()
    unrotate()
    weight_grad(WQ, nrm, dq[...])
    grad_norm1()
    pre_act()
    rs_out(WDOWN)
    rs_turn(WOUT)
    swap_start(5)
    rs_turn(WUP)
    swap_wait(5)
    rs_start(WQ)
    norm_grad1()
    rs_out(WOUT)
    rs_turn(WQ)
    weight_grad(WK, nrm, dk[...])
    grad_token()
    grad_in2()
    weight_grad(WV, nrm, dv[...])
    rs_start(WK)
    rs_out(WUP)
    rs_turn(WK)
    swap_start(6)
    rs_start(IN2)
    swap_wait(6)
    rs_out(WQ)
    rs_out(WK)
    rs_final(WUP)
    grad_pre()
    grad_pack()
    rs_turn(IN2)
    rs_start(PACK)
    rs_final(WDOWN)
    grad_values()
    rs_start(WV)
    rs_turn(PACK)
    rs_out(IN2)
    rs_final(WK)
    rs_final(WOUT)
    rs_turn(WV)
    rs_final(IN2)
    rs_out(PACK)
    rs_final(WQ)
    swap_start(7)
    rs_final(PACK)
    rs_out(WV)
    swap_start(8)
    swap_wait(7)
    swap_wait(8)
    rs_final(WV)
    write_small()

    def drain(ref, sem):
        remote(ref, ref, sem, sem, XN).wait_send()

    for w in (PACK,) + order:
        ref = PK.at[m] if w == PACK else W.at[w]
        drain(ref.at[pl.ds(0, (11 if w in PLANE_FIRST else 15) * blk)], ag_send.at[w])
        if w in PLANE_FIRST:

            @pl.when(inner)
            def _():
                drain(ref.at[pl.ds(0, 8 * blk)], ag_send.at[w])

        if w == PACK:
            ref = RP
        elif w in Z_FIRST:
            ref = RZ.at[Z_FIRST.index(w)]
        else:
            ref = R.at[CHAIN_LAST.index(w)]
        drain(ref.at[pl.ds(0, 15)], rs_send.at[w])


def pack_block(dst, matrix, vectors):
    tok_in, blk = matrix.shape
    parts = [matrix[...].astype(f32)] + [t[...].astype(f32) for t in vectors]
    parts.append(jnp.zeros((PL - tok_in - len(vectors), blk), f32))
    tall = jnp.concatenate(parts, 0)
    wide = jnp.concatenate([tall, jnp.zeros((PL, PL - blk), f32)], 1)
    dst[...] = wide.T[0:blk].astype(bf16)


def copy_kernel(count, *refs):
    sources, targets, held, sems = refs[:count], refs[count : 2 * count], refs[2 * count : -1], refs[-1]
    inward = [pltpu.make_async_copy(sources[i], held[i], sems.at[0, i]) for i in range(count)]
    outward = [pltpu.make_async_copy(held[i], targets[i], sems.at[1, i]) for i in range(count)]
    for c in inward:
        c.start()
    for a, b in zip(inward, outward):
        a.wait()
        b.start()
    for c in outward:
        c.wait()


def rotate(vectors, places):
    half_width = vectors.shape[-1] // 2
    frequency = 10000.0 ** (-2.0 * jnp.arange(half_width, dtype=jnp.float32) / vectors.shape[-1])
    angles = places[:, :, None, None] * frequency
    cosine = jnp.cos(angles)
    sine_val = jnp.sin(angles)
    first_half = vectors[..., :half_width]
    second_half = vectors[..., half_width:]
    return jnp.concatenate(
        [
            first_half * cosine - second_half * sine_val,
            second_half * cosine + first_half * sine_val,
        ],
        -1,
    )


def rms_norm(resid_rows, gain_vec):
    return (
        resid_rows
        * lax.rsqrt(jnp.mean(resid_rows * resid_rows, -1, keepdims=True) + 1e-06)
        * gain_vec
    )


def activate(up_rows):
    return jax.nn.gelu(up_rows, approximate=False)


def general_device(
    values,
    lengths,
    w_in1,
    b_in1,
    w_in2,
    b_in2,
    w_res,
    g_attn,
    w_qkv,
    w_out,
    g_mlp,
    w_up,
    w_down,
    cotangent,
):
    f32 = jnp.float32
    bf16 = jnp.bfloat16
    gathered = (
        lax.all_gather(w_in1, "fsdp", axis=1, tiled=True),
        lax.all_gather(b_in1, "fsdp", axis=0, tiled=True),
        lax.all_gather(w_in2, "fsdp", axis=0, tiled=True),
        lax.all_gather(b_in2, "fsdp", axis=0, tiled=True),
        lax.all_gather(w_res, "fsdp", axis=1, tiled=True),
        lax.all_gather(g_attn, "fsdp", axis=0, tiled=True),
        lax.all_gather(w_qkv, "fsdp", axis=0, tiled=True),
        lax.all_gather(w_out, "fsdp", axis=1, tiled=True),
        lax.all_gather(g_mlp, "fsdp", axis=0, tiled=True),
        lax.all_gather(w_up, "fsdp", axis=0, tiled=True),
        lax.all_gather(w_down, "fsdp", axis=1, tiled=True),
    )
    (
        full_in1,
        full_b1,
        full_in2,
        full_b2,
        full_res,
        full_gattn,
        full_qkv,
        full_out,
        full_gmlp,
        full_up,
        full_down,
    ) = gathered
    series = lengths.shape[0]
    seq_len = values.shape[0] // series
    patch_len = values.shape[1]
    slot_ids = jnp.arange(seq_len, dtype=jnp.int32)
    pad_count = seq_len - lengths
    padded = slot_ids[None, :] < pad_count[:, None]
    places = (slot_ids[None, :] - pad_count[:, None]).astype(f32)
    keep_mask = (1.0 - padded.astype(f32)).reshape(-1, 1)
    inputs = jnp.concatenate(
        [values.astype(f32) * keep_mask, jnp.broadcast_to(1.0 - keep_mask, values.shape)], 1
    ).astype(bf16)
    pre_act = jnp.dot(inputs, full_in1, preferred_element_type=f32) + full_b1.astype(f32)
    hidden = jax.nn.silu(pre_act).astype(bf16)
    resid0 = (
        jnp.dot(hidden, full_in2, preferred_element_type=f32)
        + full_b2.astype(f32)
        + jnp.dot(inputs, full_res, preferred_element_type=f32)
    )
    gain_attn = full_gattn.astype(f32)
    normed = rms_norm(resid0, gain_attn).astype(bf16)
    projected = jnp.einsum("td,dch->tch", normed, full_qkv, preferred_element_type=f32)
    local_heads = projected.shape[2] // HD
    head_shape = (series, seq_len, local_heads, HD)
    queries = rotate(projected[:, 0].reshape(head_shape), places).astype(bf16)
    key_rows = rotate(projected[:, 1].reshape(head_shape), places).astype(bf16)
    value_heads = projected[:, 2].reshape(head_shape).astype(bf16)
    causal = slot_ids[None, :] <= slot_ids[:, None]
    diagonal = slot_ids[None, :] == slot_ids[:, None]
    allowed = (causal[None] & (jnp.logical_not(padded)[:, None, :] | diagonal[None]))[:, None]
    scale = HD ** (-0.5)

    def score_block():
        raw = jnp.einsum("sqhe,skhe->shqk", queries, key_rows, preferred_element_type=f32) * scale
        return jnp.where(allowed, raw, -1e30)

    scores = score_block()
    row_max = jnp.max(scores, -1, keepdims=True)
    exponent = jnp.exp(scores - row_max)
    row_total = jnp.sum(exponent, -1, keepdims=True)
    log_total = row_max + jnp.log(row_total)
    attn_probs = (exponent / row_total).astype(bf16)
    attended = (
        jnp.einsum("shqk,skhe->sqhe", attn_probs, value_heads, preferred_element_type=f32)
        .reshape(-1, local_heads * HD)
        .astype(bf16)
    )
    branch_one = lax.psum(jnp.dot(attended, full_out, preferred_element_type=f32), "mp")
    resid1 = resid0 + branch_one
    gain_mlp = full_gmlp.astype(f32)
    normed2 = rms_norm(resid1, gain_mlp).astype(bf16)
    up_rows = jnp.dot(normed2, full_up, preferred_element_type=f32)
    mlp_hidden = activate(up_rows).astype(bf16)
    branch_two = lax.psum(
        jnp.dot(mlp_hidden, full_down, preferred_element_type=f32).astype(jnp.bfloat16), "mp"
    ).astype(jnp.float32)
    result = (resid1 + branch_two).astype(bf16)
    again = (
        lax.all_gather(w_in1, "fsdp", axis=1, tiled=True),
        lax.all_gather(b_in1, "fsdp", axis=0, tiled=True),
        lax.all_gather(w_in2, "fsdp", axis=0, tiled=True),
        lax.all_gather(b_in2, "fsdp", axis=0, tiled=True),
        lax.all_gather(w_res, "fsdp", axis=1, tiled=True),
        lax.all_gather(g_attn, "fsdp", axis=0, tiled=True),
        lax.all_gather(w_qkv, "fsdp", axis=0, tiled=True),
        lax.all_gather(w_out, "fsdp", axis=1, tiled=True),
        lax.all_gather(g_mlp, "fsdp", axis=0, tiled=True),
        lax.all_gather(w_up, "fsdp", axis=0, tiled=True),
        lax.all_gather(w_down, "fsdp", axis=1, tiled=True),
    )
    (
        back_in1,
        back_b1,
        back_in2,
        back_b2,
        back_res,
        back_gattn,
        back_qkv,
        back_out,
        back_gmlp,
        back_up,
        back_down,
    ) = again
    cot_rows = cotangent.astype(f32)
    grad_down = jnp.einsum("tf,td->fd", mlp_hidden, cotangent, preferred_element_type=f32)
    grad_hidden = jnp.einsum("td,fd->tf", cotangent, back_down, preferred_element_type=f32)
    unused_one, pull_mlp = jax.vjp(activate, up_rows)
    grad_up_rows = pull_mlp(grad_hidden)[0].astype(bf16)
    grad_up = jnp.einsum("td,tf->df", normed2, grad_up_rows, preferred_element_type=f32)
    norm_part2 = jnp.einsum("tf,df->td", grad_up_rows, back_up, preferred_element_type=f32)
    norm_grad2 = lax.psum(norm_part2, "mp")
    unused_two, pull_norm2 = jax.vjp(rms_norm, resid1, back_gmlp.astype(f32))
    resid_part1, grad_gmlp = pull_norm2(norm_grad2)
    resid1_grad = cot_rows + resid_part1
    out_grad = resid1_grad.astype(bf16)
    grad_out = jnp.einsum("th,td->hd", attended, out_grad, preferred_element_type=f32)
    attended_grad = (
        jnp.einsum("td,hd->th", out_grad, back_out, preferred_element_type=f32)
        .astype(bf16)
        .reshape(head_shape)
    )
    scores = score_block()
    probs_full = jnp.exp(scores - log_total)
    value_grad = jnp.einsum(
        "shqk,sqhe->skhe", probs_full.astype(bf16), attended_grad, preferred_element_type=f32
    )
    prob_grad = jnp.einsum(
        "sqhe,skhe->shqk", attended_grad, value_heads, preferred_element_type=f32
    )
    score_grad = (
        probs_full * (prob_grad - jnp.sum(prob_grad * probs_full, -1, keepdims=True))
    ).astype(bf16)
    query_grad = (
        jnp.einsum("shqk,skhe->sqhe", score_grad, key_rows, preferred_element_type=f32) * scale
    )
    key_grad = (
        jnp.einsum("shqk,sqhe->skhe", score_grad, queries, preferred_element_type=f32) * scale
    )
    width_local = local_heads * HD
    qkv_rows = jnp.stack(
        [
            rotate(query_grad, -places).reshape(-1, width_local),
            rotate(key_grad, -places).reshape(-1, width_local),
            value_grad.reshape(-1, width_local),
        ],
        1,
    ).astype(bf16)
    grad_qkv = jnp.einsum("td,tch->dch", normed, qkv_rows, preferred_element_type=f32)
    norm_part1 = jnp.einsum("tch,dch->td", qkv_rows, back_qkv, preferred_element_type=f32)
    norm_grad1 = lax.psum(norm_part1, "mp")
    unused_three, pull_norm1 = jax.vjp(rms_norm, resid0, back_gattn.astype(f32))
    resid_part0, grad_gattn = pull_norm1(norm_grad1)
    resid0_grad = (resid1_grad + resid_part0).astype(bf16)
    grad_in2 = jnp.einsum("th,td->hd", hidden, resid0_grad, preferred_element_type=f32)
    grad_b2 = jnp.sum(resid0_grad.astype(f32), 0)
    grad_res = jnp.einsum("tp,td->pd", inputs, resid0_grad, preferred_element_type=f32)
    hidden_grad = jnp.einsum("td,hd->th", resid0_grad, back_in2, preferred_element_type=f32)
    unused_four, pull_silu = jax.vjp(jax.nn.silu, pre_act)
    pre_grad = pull_silu(hidden_grad)[0].astype(bf16)
    grad_in1 = jnp.einsum("tp,th->ph", inputs, pre_grad, preferred_element_type=f32)
    grad_b1 = jnp.sum(pre_grad.astype(f32), 0)
    input_grad = jnp.einsum(
        "th,ph->tp", pre_grad, back_in1, preferred_element_type=f32
    ) + jnp.einsum("td,pd->tp", resid0_grad, back_res, preferred_element_type=f32)
    values_grad = input_grad[:, :patch_len] * keep_mask
    shares = tuple(
        (
            lax.psum_scatter(grad_in1, "fsdp", scatter_dimension=1, tiled=True),
            lax.psum_scatter(grad_b1, "fsdp", scatter_dimension=0, tiled=True),
            lax.psum_scatter(grad_in2, "fsdp", scatter_dimension=0, tiled=True),
            lax.psum_scatter(grad_b2, "fsdp", scatter_dimension=0, tiled=True),
            lax.psum_scatter(grad_res, "fsdp", scatter_dimension=1, tiled=True),
            lax.psum_scatter(grad_gattn, "fsdp", scatter_dimension=0, tiled=True),
            lax.psum_scatter(grad_qkv, "fsdp", scatter_dimension=0, tiled=True),
            lax.psum_scatter(grad_out, "fsdp", scatter_dimension=1, tiled=True),
            lax.psum_scatter(grad_gmlp, "fsdp", scatter_dimension=0, tiled=True),
            lax.psum_scatter(grad_up, "fsdp", scatter_dimension=0, tiled=True),
            lax.psum_scatter(grad_down, "fsdp", scatter_dimension=1, tiled=True),
        )
    )
    return (result, values_grad) + shares


def fused_device(
    values,
    lengths,
    w_in1,
    b_in1,
    w_in2,
    b_in2,
    w_res,
    g_attn,
    w_qkv,
    w_out,
    g_mlp,
    w_up,
    w_down,
    cotangent,
):
    rows, width = cotangent.shape
    half = w_out.shape[0]
    blk = w_in2.shape[0]
    patch = values.shape[1]
    tok_in = w_in1.shape[0]
    heads = half // HD
    vmem = pl.BlockSpec(memory_space=pltpu.VMEM)
    hbm = pl.BlockSpec(memory_space=pl.ANY)

    def shape(*dims, dtype=f32):
        return jax.ShapeDtypeStruct(dims, dtype)

    out_shape = (
        shape(rows, width, dtype=bf16),
        shape(patch, rows),
        shape(tok_in, blk),
        shape(1, blk),
        shape(blk, width),
        shape(1, blk),
        shape(tok_in, blk),
        shape(1, blk),
        shape(3, blk, half),
        shape(blk, half),
        shape(1, blk),
        shape(blk, half),
        shape(blk, half),
    )
    V = pltpu.VMEM
    scratch = [
        V((NW, width, half), bf16),
        V((2, width, PL), bf16),
        V((NW, width, half), bf16),
        V((width, PL), bf16),
        V((len(CHAIN_LAST), SLOTS, blk, half), bf16),
        V((max(1, len(Z_FIRST)), Z_SLOTS, blk, half), bf16),
        V((SLOTS, blk, PL), bf16),
        V((2, rows, half), f32),
        V((rows, width), f32),
        V((2, rows, width), f32),
        V((2, rows, width), f32),
        V((rows, width), bf16),
        V((rows, width), bf16),
        V((rows, width), bf16),
        V((rows, width), bf16),
        V((rows, width), bf16),
        V((rows, half), bf16),
        V((rows, half), bf16),
        V((rows, half), bf16),
        V((heads, rows, rows), f32),
        V((rows, half), bf16),
        V((rows, half), f32),
        V((rows, half), bf16),
        V((rows, width), bf16),
        V((rows, half), bf16),
        V((rows, half), bf16),
        V((rows, half), bf16),
        V((rows, half), bf16),
        V((rows, width), f32),
        V((rows, width), bf16),
        V((rows, half), f32),
        V((rows, half), f32),
        V((rows, rows), f32),
        V((rows, PL), bf16),
        V((2, 8, width), f32),
        V((2, 16, width), bf16),
        V((8, width), f32),
        V((rows, PL), f32),
        V((2, blk, half), f32),
        V((2, blk, PL), f32),
        pltpu.SemaphoreType.DMA((8,)),
        pltpu.SemaphoreType.DMA((8, 16)),
        pltpu.SemaphoreType.DMA((8,)),
        pltpu.SemaphoreType.DMA((8, Z_SLOTS)),
        pltpu.SemaphoreType.DMA((9,)),
        pltpu.SemaphoreType.DMA((9,)),
        pltpu.SemaphoreType.DMA((9,)),
    ]
    results = pl.pallas_call(
        layer_kernel,
        name="layer",
        out_shape=out_shape,
        in_specs=[pl.BlockSpec(memory_space=pltpu.SMEM)] + [vmem] * 7 + [hbm] * 6,
        out_specs=(vmem,) * len(out_shape),
        scratch_shapes=scratch,
        compiler_params=pltpu.CompilerParams(
            collective_id=0, has_side_effects=True, vmem_limit_bytes=VMEM_BYTES
        ),
    )(
        lengths,
        values.T,
        w_in1,
        w_res,
        b_in1[None],
        b_in2[None],
        g_attn[None],
        g_mlp[None],
        w_in2,
        jnp.transpose(w_qkv, (1, 0, 2)),
        w_out.T,
        w_up,
        w_down.T,
        cotangent,
    )
    (
        out,
        d_values,
        d_in1,
        d_b1,
        d_in2,
        d_b2,
        d_res,
        d_gattn,
        d_qkv,
        d_out,
        d_gmlp,
        d_up,
        d_down,
    ) = pl.pallas_call(
        functools.partial(copy_kernel, len(out_shape)),
        name="hand_over",
        out_shape=out_shape,
        in_specs=[hbm] * len(out_shape),
        out_specs=(hbm,) * len(out_shape),
        scratch_shapes=[V(s.shape, s.dtype) for s in out_shape]
        + [pltpu.SemaphoreType.DMA((2, len(out_shape)))],
    )(*results)
    return (
        out,
        d_values.T,
        d_in1,
        d_b1[0],
        d_in2,
        d_b2[0],
        d_res,
        d_gattn[0],
        jnp.transpose(d_qkv, (1, 0, 2)),
        d_out.T,
        d_gmlp[0],
        d_up,
        d_down.T,
    )


def on_device(*args):
    blk, width = args[4].shape
    half = args[9].shape[0]
    shards = width // blk
    series = args[1].shape[0]
    fits = (
        shards == 16
        and 2 * half == width
        and blk % 16 == 0
        and half % 128 == 0
        and args[0].shape[0] % 64 == 0
        and series <= 8
    )
    return (fused_device if fits else general_device)(*args)


def solution(mesh):
    in_specs = (
        P("fsdp", None),
        P("fsdp"),
        P(None, "fsdp"),
        P("fsdp"),
        P("fsdp", None),
        P("fsdp"),
        P(None, "fsdp"),
        P("fsdp"),
        P("fsdp", None, "mp"),
        P("mp", "fsdp"),
        P("fsdp"),
        P("fsdp", "mp"),
        P("mp", "fsdp"),
        P("fsdp", None),
    )
    out_specs = (
        P("fsdp", None),
        P("fsdp", None),
        P(None, "fsdp"),
        P("fsdp"),
        P("fsdp", None),
        P("fsdp"),
        P(None, "fsdp"),
        P("fsdp"),
        P("fsdp", None, "mp"),
        P("mp", "fsdp"),
        P("fsdp"),
        P("fsdp", "mp"),
        P("mp", "fsdp"),
    )
    return jax.shard_map(
        on_device, mesh=mesh, in_specs=in_specs, out_specs=out_specs, check_vma=False
    )
```

```python
import functools
import math

import jax
import jax.numpy as jnp
from jax import lax
from jax.experimental import pallas as pl
from jax.experimental.pallas import tpu as pltpu
from jax.sharding import PartitionSpec as P

HD = 80
MESH = pl.DeviceIdType.MESH
VMEM_BYTES = 63 * 2**20
f32 = jnp.float32
bf16 = jnp.bfloat16

IN2, WQ, WK, WV, WOUT, WUP, WDOWN, PACK = range(8)
NW = 7
PL = 128
PLANE_FIRST = (WUP,)
Z_FIRST = (WUP,)
CHAIN_LAST = tuple(w for w in range(NW) if w not in Z_FIRST)
SLOT_A, SLOT_X, SLOT_Y, SLOT_V, SLOTS = 0, 4, 8, 12, 16
Z_RELAY, Z_NEAR, Z_FAR, Z_A, Z_X, Z_Y, Z_SLOTS = 0, 8, 12, 16, 17, 18, 19


def dot(left, right, left_dim, right_dim):
    return lax.dot_general(
        left, right, (((left_dim,), (right_dim,)), ((), ())), preferred_element_type=f32
    )


def layer_kernel(
    lengths,
    values_t,
    w_in1,
    w_res,
    b_in1,
    b_in2,
    g_attn,
    g_mlp,
    in2,
    qkv,
    out_t,
    up,
    down_t,
    cot_hbm,
    o_out,
    o_dval,
    o_in1,
    o_b1,
    o_in2,
    o_b2,
    o_res,
    o_gattn,
    o_qkv,
    o_wout,
    o_gmlp,
    o_up,
    o_down,
    W,
    PK,
    G,
    GP,
    R,
    RZ,
    RP,
    R0,
    R1,
    S,
    X,
    SB,
    XB,
    hid,
    nrm,
    nrm2,
    q,
    k,
    v,
    prob,
    att,
    gprime,
    mlp,
    cot,
    dup,
    dq,
    dk,
    dv,
    tmp,
    dr0,
    rope_c,
    rope_s,
    bias,
    inx,
    gains,
    dgs,
    accg,
    keep_col,
    fin_in2,
    fin_pack,
    ag_send,
    ag_recv,
    rs_send,
    rs_recv,
    ex_send,
    ex_recv,
    lsem,
):
    rows, width = cot.shape
    half = W.shape[2]
    blk = in2.shape[0]
    series = lengths.shape[0]
    seq = rows // series
    heads = half // HD
    patch = values_t.shape[0]

    f = lax.axis_index("fsdp")
    m = lax.axis_index("mp")
    x = lax.rem(f, 2)
    y = lax.rem(lax.div(f, 2), 2)
    z = lax.div(f, 4)
    c0 = f - 4 * z
    cx = c0 + 1 - 2 * x
    cy = c0 + 2 - 4 * y
    cd = 3 - c0
    XN, YN, SIB = (4 * z + cx, m), (4 * z + cy, m), (f, 1 - m)
    z_high = (z >= 2).astype(jnp.int32)
    inner = jnp.logical_and(z > 0, z < 3)
    z_inner = inner.astype(jnp.int32)
    z_near = z + 1 - 2 * lax.rem(z, 2)
    z_far = 2 - z_high
    z_even = lax.rem(z, 2) == 0

    def plane(zb):
        return (4 * zb + c0, m)

    def near(i):
        swap = (i == 0).astype(jnp.int32) - (i == 1).astype(jnp.int32)
        low = i + z_inner * swap
        return low + z_high * (3 - 2 * low)

    def far(i):
        return near(3 - i)

    def each_plane(order, body, start=0):
        def step(i, carry):
            body(order(i))
            return carry

        lax.fori_loop(start, 4, step, 0)

    def each_other_plane(body):
        each_plane(near, body, 1)

    def row_of(b):
        return pl.ds(pl.multiple_of(b * blk, 16), blk)

    def w_block(w, b):
        return PK.at[m, row_of(b)] if w == PACK else W.at[w, row_of(b)]

    def g_block(w, b):
        return GP.at[row_of(b)] if w == PACK else G.at[w, row_of(b)]

    def r_block(w, s):
        if w == PACK:
            return RP.at[s]
        if w in Z_FIRST:
            return RZ.at[Z_FIRST.index(w), s]
        return R.at[CHAIN_LAST.index(w), s]

    def remote(src, dst, send, recv, dev):
        return pltpu.make_async_remote_copy(
            src_ref=src, dst_ref=dst, send_sem=send, recv_sem=recv, device_id=dev, device_id_type=MESH
        )

    def ag_push(w, b, *devs):
        ref = w_block(w, b)
        for dev in devs:
            remote(ref, ref, ag_send.at[w], ag_recv.at[w, b], dev).start()

    def ag_await(w, b):
        ref = w_block(w, b)
        remote(ref, ref, ag_send.at[w], ag_recv.at[w, b], XN).wait_recv()

    mcols = pl.ds(pl.multiple_of(m * half, 128), half)

    def own_copy(w):
        if w == IN2:
            src = in2.at[:, mcols]
        elif w in (WQ, WK, WV):
            src = qkv.at[w - WQ]
        else:
            src = {WOUT: out_t, WUP: up, WDOWN: down_t}[w]
        return pltpu.make_async_copy(src, w_block(w, f), lsem.at[w])

    def ag_own(w):
        if w != PACK:
            own_copy(w).wait()
        ag_push(w, f, XN, YN)
        if w in PLANE_FIRST:
            ag_push(w, f, plane(z_near), plane(z_far))
        else:
            each_other_plane(lambda zb: ag_push(w, f, plane(zb)))

    def ag_column(w):
        def body(zb):
            b = 4 * zb + c0
            ag_await(w, b)
            ag_push(w, b, XN, YN)

        each_other_plane(body)

    def ag_pass(w, zb, even, *more):
        ag_await(w, 4 * zb + cx)

        @pl.when(even)
        def _():
            ag_push(w, 4 * zb + cx, YN)

        ag_push(w, 4 * zb + cx, *more)
        ag_await(w, 4 * zb + cy)

        @pl.when(jnp.logical_not(even))
        def _():
            ag_push(w, 4 * zb + cy, XN)

        ag_push(w, 4 * zb + cy, *more)

    def ag_plane(w):
        if w in PLANE_FIRST:
            to = (plane(z_near), plane(z_far))
            ag_pass(w, z, z_even, *to)
            ag_await(w, 4 * z + cd)
            ag_push(w, 4 * z + cd, *to)
        else:
            each_plane(near, lambda zb: ag_pass(w, zb, lax.rem(zb, 2) == 0))

    def ag_relay(w):
        @pl.when(inner)
        def _():
            for zb in (3 - z, 3 * (1 - z_high)):
                for c in (c0, cx, cy, cd):
                    ag_await(w, 4 * zb + c)
                    ag_push(w, 4 * zb + c, plane(3 * z_high))

    def ag_last(w):
        if w in PLANE_FIRST:
            for c in (c0, cx, cy, cd):
                ag_await(w, 4 * z_near + c)

            @pl.when(jnp.logical_not(inner))
            def _():
                for zb in (z_far, 3 - z):
                    for c in (c0, cx, cy, cd):
                        ag_await(w, 4 * zb + c)
        else:
            each_plane(near, lambda zb: ag_await(w, 4 * zb + cd))

    final_of = {
        IN2: lambda: fin_in2.at[m],
        WQ: lambda: o_qkv.at[0],
        WK: lambda: o_qkv.at[1],
        WV: lambda: o_qkv.at[2],
        WOUT: lambda: o_wout,
        WUP: lambda: o_up,
        WDOWN: lambda: o_down,
        PACK: lambda: fin_pack.at[m],
    }

    def rs_push(w, src, slot, dev):
        remote(src, r_block(w, slot), rs_send.at[w], rs_recv.at[w, slot], dev).start()

    def rs_await(w, slot):
        ref = r_block(w, slot)
        remote(ref, ref, rs_send.at[w], rs_recv.at[w, slot], XN).wait_recv()

    def add_to(ref, other):
        ref[...] = (ref[...].astype(f32) + other[...].astype(f32)).astype(bf16)

    def sum3(a, b, c):
        return a[...].astype(f32) + b[...].astype(f32) + c[...].astype(f32)

    def rs_start(w):
        if w in Z_FIRST:
            cs = (cd, cx, cy, c0)

            @pl.when(jnp.logical_not(inner))
            def _():
                for zb in (3 - z, z_far):
                    for c in cs:
                        slot = Z_RELAY + 4 * lax.rem(zb, 2) + c
                        rs_push(w, g_block(w, 4 * zb + c), slot, plane(1 + z_high))

            for c in cs:
                rs_push(w, g_block(w, 4 * z_near + c), Z_NEAR + c, plane(z_near))
            return

        def body(zb):
            even = lax.rem(zb, 2) == 0

            @pl.when(even)
            def _():
                rs_push(w, g_block(w, 4 * zb + cd), SLOT_A + zb, YN)
                rs_push(w, g_block(w, 4 * zb + cy), SLOT_Y + zb, YN)

            @pl.when(jnp.logical_not(even))
            def _():
                rs_push(w, g_block(w, 4 * zb + cd), SLOT_A + zb, XN)
                rs_push(w, g_block(w, 4 * zb + cx), SLOT_X + zb, XN)

        each_plane(far, body)

    def turn(w, slot_a, even, own_x, own_y, slot_x, slot_y):
        rs_await(w, slot_a)
        ref = r_block(w, slot_a)

        @pl.when(even)
        def _():
            add_to(ref, own_x)
            rs_push(w, ref, slot_x, XN)

        @pl.when(jnp.logical_not(even))
        def _():
            add_to(ref, own_y)
            rs_push(w, ref, slot_y, YN)

    def rs_turn(w):
        if w in Z_FIRST:
            turn(w, Z_A, z_even, r_block(w, Z_NEAR + cx), r_block(w, Z_NEAR + cy), Z_X, Z_Y)
            return
        each_plane(
            far,
            lambda zb: turn(
                w,
                SLOT_A + zb,
                lax.rem(zb, 2) == 0,
                g_block(w, 4 * zb + cx),
                g_block(w, 4 * zb + cy),
                SLOT_X + zb,
                SLOT_Y + zb,
            ),
        )

    def rs_relay(w):
        @pl.when(inner)
        def _():
            for zb in (3 * (1 - z_high), z_far):
                for c in (cd, cx, cy, c0):
                    slot = Z_RELAY + 4 * lax.rem(zb, 2) + c
                    rs_await(w, slot)
                    ref = r_block(w, slot)
                    add_to(ref, g_block(w, 4 * zb + c))
                    rs_push(w, ref, Z_FAR + c, plane(zb))

    def rs_zsum(w):
        for c in (cd, cx, cy, c0):
            rs_await(w, Z_NEAR + c)
            rs_await(w, Z_FAR + c)
            ref = r_block(w, Z_NEAR + c)
            total = sum3(ref, r_block(w, Z_FAR + c), g_block(w, 4 * z + c))
            if c is c0:
                final_of[w]()[...] = total
            else:
                ref[...] = total.astype(bf16)
            if c is cd:

                @pl.when(z_even)
                def _():
                    rs_push(w, ref, Z_A, YN)

                @pl.when(jnp.logical_not(z_even))
                def _():
                    rs_push(w, ref, Z_A, XN)

            if c is cx:

                @pl.when(jnp.logical_not(z_even))
                def _():
                    rs_push(w, ref, Z_X, XN)

            if c is cy:

                @pl.when(z_even)
                def _():
                    rs_push(w, ref, Z_Y, YN)

    def plane_sum(w, zb):
        rs_await(w, SLOT_X + zb)
        rs_await(w, SLOT_Y + zb)
        return sum3(g_block(w, 4 * zb + c0), r_block(w, SLOT_X + zb), r_block(w, SLOT_Y + zb))

    def rs_out(w):
        def body(zb):
            ref = r_block(w, SLOT_X + zb)
            ref[...] = plane_sum(w, zb).astype(bf16)
            rs_push(w, ref, SLOT_V + z, plane(zb))

        each_other_plane(body)
        final_of[w]()[...] = plane_sum(w, z)

    def rs_final(w):
        final = final_of[w]()
        if w in Z_FIRST:
            rs_await(w, Z_X)
            rs_await(w, Z_Y)
            final[...] = sum3(final, r_block(w, Z_X), r_block(w, Z_Y))
            return

        for i in (1, 2, 3):
            rs_await(w, SLOT_V + near(jnp.int32(i)))
        parts = [r_block(w, SLOT_V + near(jnp.int32(i)))[...].astype(f32) for i in (1, 2, 3)]
        final[...] = final[...] + (parts[0] + parts[1] + parts[2])

    def exchange(i):
        src, dst = {
            0: lambda: (PK.at[m], PK.at[m]),
            1: lambda: (R0.at[m], R0.at[m]),
            2: lambda: (S.at[0], X.at[0]),
            3: lambda: (SB, XB),
            4: lambda: (S.at[1], X.at[1]),
            5: lambda: (S.at[0], X.at[0]),
            6: lambda: (S.at[1], X.at[1]),
            7: lambda: (fin_in2.at[m], fin_in2.at[m]),
            8: lambda: (fin_pack.at[m], fin_pack.at[m]),
        }[i]()
        return remote(src, dst, ex_send.at[i], ex_recv.at[i], SIB)

    def swap_start(i):
        exchange(i).start()

    def swap_wait(i):
        exchange(i).wait()

    def by_rows(step, body, unroll=4):
        def one(i, carry):
            body(pl.ds(pl.multiple_of(i * step, step), step))
            return carry

        lax.fori_loop(0, rows // step, one, 0, unroll=unroll)

    halves = (slice(0, half), slice(half, width))

    lens = [lengths[s] for s in range(series)]

    def pad_of(slot):
        total = jnp.zeros(slot.shape, jnp.int32)
        for s in range(series):
            inside = jnp.logical_and(slot >= s * seq, slot < (s + 1) * seq)
            total = jnp.where(inside, (s + 1) * seq - lens[s], total)
        return total

    def series_of(slot):
        total = jnp.zeros(slot.shape, jnp.int32)
        for s in range(1, series):
            total = total + (slot >= s * seq).astype(jnp.int32)
        return total

    lane = lax.broadcasted_iota(jnp.int32, (1, half), 1).astype(f32)
    in_head = lane - HD * jnp.floor((lane + 0.5) / HD)
    first = in_head < HD // 2

    def prepare():
        slot_col = lax.broadcasted_iota(jnp.int32, (rows, 1), 0)
        keep = jnp.broadcast_to((slot_col >= pad_of(slot_col)).astype(f32), keep_col.shape)
        keep_col[...] = keep
        lane_i = lax.broadcasted_iota(jnp.int32, (rows, PL), 1)
        tall = jnp.concatenate([values_t[...].astype(f32), jnp.zeros((PL - patch, rows), f32)], 0)
        inx[...] = jnp.where(
            lane_i < patch,
            tall.T * keep,
            jnp.where(lane_i < 2 * patch, 1.0 - keep, (lane_i == 2 * patch).astype(f32)),
        ).astype(bf16)

        key_slot = lax.broadcasted_iota(jnp.int32, (1, rows), 1)
        key_ok = (key_slot >= pad_of(key_slot)).astype(jnp.int32)
        key_series = series_of(key_slot)

        def bias_rows(s):
            shape = (s.size, rows)
            a = lax.broadcasted_iota(jnp.int32, shape, 0) + s.start
            b = jnp.broadcast_to(key_slot, shape)
            same = series_of(a) == jnp.broadcast_to(key_series, shape)
            ok = jnp.logical_or(jnp.broadcast_to(key_ok, shape) == 1, a == b)
            allowed = jnp.logical_and(jnp.logical_and(same, b <= a), ok)
            bias[s, :] = jnp.where(allowed, 0.0, -1e30)

        by_rows(32, bias_rows, 1)
        turn_i = jnp.where(first, in_head, in_head - HD // 2)
        frequency = jnp.exp(turn_i * (-2.0 * math.log(10000.0) / HD))

        def rope_rows(s):
            slot = lax.broadcasted_iota(jnp.int32, (s.size, 1), 0) + s.start
            place = (slot - pad_of(slot)).astype(f32)
            angle = place * frequency
            rope_c[s, :] = jnp.cos(angle)
            sine = jnp.sin(angle)
            rope_s[s, :] = jnp.where(first, -sine, sine)

        by_rows(16, rope_rows, 1)

    def rope(t, s, inverse):
        other = jnp.where(first, pltpu.roll(t, half - HD // 2, 1), pltpu.roll(t, HD // 2, 1))
        turned = other * rope_s[s, :]
        return t * rope_c[s, :] - turned if inverse else t * rope_c[s, :] + turned

    gain_lane = lax.broadcasted_iota(jnp.int32, (16, PL), 1)

    def pre_act():
        for cols in halves:
            tmp[:, cols] = dot(inx[...], PK[0, cols, :], 1, 1)

    def token_hidden():
        for i in range(2):
            pick = (gain_lane == 2 * patch + 1 + i).astype(bf16)
            gains[i] = dot(pick, PK[1], 1, 1)[0:8]
        pre_act()

        def silu_rows(s):
            t = tmp[s, :]
            hid[s, :] = (t / (1.0 + jnp.exp(-t))).astype(bf16)

        by_rows(16, silu_rows)

    def token_out():
        R0[m] = dot(hid[...], W[IN2], 1, 0) + dot(inx[...], PK[1, mcols, :], 1, 1)

    def norm_rows(load, gain, out):
        def body(s):
            a, b = load(s)
            mean = (jnp.sum(a * a, -1, keepdims=True) + jnp.sum(b * b, -1, keepdims=True)) / width
            scale = lax.rsqrt(mean + 1e-06)
            out[s, halves[0]] = (a * scale * gain[0:1, halves[0]]).astype(bf16)
            out[s, halves[1]] = (b * scale * gain[0:1, halves[1]]).astype(bf16)

        by_rows(16, body)

    def norm_first():
        norm_rows(lambda s: (R0[0, s, :], R0[1, s, :]), gains.at[0], nrm)

    def project(w, out):
        tmp[:, halves[0]] = dot(nrm[...], W[w], 1, 0)

        def body(s):
            out[s, :] = rope(tmp[s, halves[0]], s, False).astype(bf16)

        by_rows(16, body)

    def project_v():
        v[...] = dot(nrm[...], W[WV], 1, 0).astype(bf16)

    win = 256
    scale = HD ** (-0.5)
    win_lane = lax.broadcasted_iota(jnp.int32, (1, win), 1)

    def head_window(h):
        low = jnp.minimum(lax.div(h * HD, 128) * 128, half - win)
        inside = jnp.logical_and(win_lane >= h * HD - low, win_lane < h * HD - low + HD)
        return pl.ds(pl.multiple_of(low, 128), win), inside

    def only(inside, t):
        return jnp.where(inside, t.astype(f32), 0.0).astype(bf16)

    def attend():
        att[...] = jnp.zeros_like(att)

        def one(h, carry):
            cols, inside = head_window(h)
            score = dot(only(inside, q[:, cols]), k[:, cols], 1, 1) * scale + bias[...]
            exponent = jnp.exp(score - jnp.max(score, -1, keepdims=True))
            p = exponent / jnp.sum(exponent, -1, keepdims=True)
            prob[h] = p
            mixed = dot(p.astype(bf16), v[:, cols], 1, 0)
            att[:, cols] = jnp.where(inside, mixed, att[:, cols].astype(f32)).astype(bf16)
            return carry

        lax.fori_loop(0, heads, one, 0, unroll=2)

    def widen(dst, terms):
        for cols in halves:
            total = None
            for left, w in terms:
                part = dot(left[...], W[w, cols, :], 1, 1)
                total = part if total is None else total + part
            dst[:, cols] = total.astype(dst.dtype)

    def attend_out():
        widen(S.at[0], [(att, WOUT)])

    def norm_second():
        def body(s):
            for i, cols in enumerate(halves):
                R1[s, cols] = R0[i, s, :] + (S[0, s, cols] + X[0, s, cols])

        by_rows(16, body)
        norm_rows(lambda s: (R1[s, halves[0]], R1[s, halves[1]]), gains.at[1], nrm2)

    def feed_up():
        tmp[:, halves[0]] = dot(nrm2[...], W[WUP], 1, 0)

        def gelu_rows(s):
            t = tmp[s, halves[0]]
            phi = 0.5 * (1.0 + lax.erf(t * (2.0**-0.5)))
            mlp[s, :] = (t * phi).astype(bf16)
            gprime[s, :] = phi + t * jnp.exp(-0.5 * t * t) * ((2.0 * math.pi) ** -0.5)

        by_rows(16, gelu_rows)

    def weight_grad(w, left, right):
        for r in halves:
            G[w, r, :] = dot(left[:, r], right, 0, 0).astype(bf16)

    def grad_down():
        cot_copy.wait()
        weight_grad(WDOWN, cot, mlp[...])

    def grad_hidden():
        tmp[:, halves[0]] = dot(cot[...], W[WDOWN], 1, 0)

        def dup_rows(s):
            dup[s, :] = (tmp[s, halves[0]] * gprime[s, :]).astype(bf16)

        by_rows(16, dup_rows)

    def grad_up():
        weight_grad(WUP, nrm2, dup[...])

    def feed_down():
        widen(SB, [(mlp, WDOWN)])

    def grad_norm2():
        widen(S.at[1], [(dup, WUP)])

    def write_output():
        def body(s):
            o_out[s, :] = (R1[s, :] + (SB[s, :].astype(f32) + XB[s, :].astype(f32))).astype(bf16)

        by_rows(16, body)

    def norm_grad(load, i_part, gain, base, out, keep_sum):
        def body(i, carry):
            s = pl.ds(pl.multiple_of(i * 16, 16), 16)
            xs = load(s)
            mean = sum(jnp.sum(t * t, -1, keepdims=True) for t in xs) / width
            r = lax.rsqrt(mean + 1e-06)
            n1 = [t * r for t in xs]
            dn = [S[i_part, s, c] + X[i_part, s, c] for c in halves]
            gd = [gain[0:1, c] * t for c, t in zip(halves, dn)]
            along = sum(jnp.sum(a * b, -1, keepdims=True) for a, b in zip(gd, n1)) / width
            for c, a, b in zip(halves, gd, n1):
                out(s, c, base(s, c) + r * (a - b * along))
            for c, a, b in zip(halves, dn, n1):
                prod = a * b
                accg[:, c] += prod[0:8] + prod[8:16]
            return carry

        accg[...] = jnp.zeros_like(accg)
        lax.fori_loop(0, rows // 16, body, 0, unroll=4)
        total = accg[...]
        high = total.astype(bf16)
        keep_sum[...] = jnp.concatenate([high.astype(f32), total - high.astype(f32)], 0).astype(bf16)

    def norm_grad2():
        def out(s, c, t):
            R1[s, c] = t
            nrm2[s, c] = t.astype(bf16)

        norm_grad(
            lambda s: [R1[s, c] for c in halves],
            1,
            gains.at[1],
            lambda s, c: cot[s, c].astype(f32),
            out,
            dgs.at[1],
        )

    def norm_grad1():
        def out(s, c, t):
            dr0[s, c] = t.astype(bf16)

        norm_grad(
            lambda s: [R0[i, s, :] for i in range(2)],
            0,
            gains.at[0],
            lambda s, c: R1[s, c],
            out,
            dgs.at[0],
        )

    def grad_out():
        weight_grad(WOUT, nrm2, att[...])

    def grad_attended():
        att[...] = dot(nrm2[...], W[WOUT], 1, 0).astype(bf16)

    def attend_back():
        dv[...] = jnp.zeros_like(dv)
        tmp[...] = jnp.zeros_like(tmp)

        def one(h, carry):
            cols, inside = head_window(h)
            cols2 = pl.ds(pl.multiple_of(cols.start + half, 128), win)
            p = prob[h]
            da = only(inside, att[:, cols])
            dp = dot(da, v[:, cols], 1, 1)
            ds = (p * (dp - jnp.sum(dp * p, -1, keepdims=True))).astype(bf16)
            dv_h = dot(p.astype(bf16), da, 0, 0)
            dq_h = dot(ds, k[:, cols], 1, 0) * scale
            dk_h = dot(ds, q[:, cols], 0, 0) * scale
            dv[:, cols] = jnp.where(inside, dv_h, dv[:, cols].astype(f32)).astype(bf16)
            tmp[:, cols] = jnp.where(inside, dq_h, tmp[:, cols])
            tmp[:, cols2] = jnp.where(inside, dk_h, tmp[:, cols2])
            return carry

        lax.fori_loop(0, heads, one, 0, unroll=2)

    def unrotate():
        def body(s):
            dq[s, :] = rope(tmp[s, halves[0]], s, True).astype(bf16)
            dk[s, :] = rope(tmp[s, halves[1]], s, True).astype(bf16)

        by_rows(16, body)

    def grad_norm1():
        widen(S.at[0], [(dq, WQ), (dk, WK), (dv, WV)])

    def grad_in2():
        weight_grad(IN2, hid, dr0[:, mcols])

    def grad_token():
        for c in halves:
            S[1, :, c] = dot(dr0[:, mcols], W[IN2, c, :], 1, 1)

    def grad_pre():
        def body(s):
            t = tmp[s, :]
            sig = 1.0 / (1.0 + jnp.exp(-t))
            grad = (S[1, s, :] + X[1, s, :]) * (sig * (1.0 + t * (1.0 - sig)))
            nrm[s, :] = grad.astype(bf16)

        by_rows(16, body)

    def grad_values():
        total = dot(nrm[...], PK[0], 1, 0) + dot(dr0[...], PK[1], 1, 0)
        o_dval[...] = (total * keep_col[...]).T[0:patch, :]

    def grad_pack():
        @pl.when(m == 0)
        def _():
            for r in halves:
                GP[r, :] = dot(nrm[:, r], inx[...], 0, 0).astype(bf16)

        @pl.when(m == 1)
        def _():
            for r in halves:
                total = dot(dr0[:, r], inx[...], 0, 0)
                for i in range(2):
                    pick = (gain_lane == 2 * patch + 1 + i).astype(bf16)
                    total = total + dot(dgs[i, :, r], pick, 0, 0)
                GP[r, :] = total.astype(bf16)

    def write_small():
        for i, c in enumerate(halves):
            o_in2[:, c] = fin_in2[i]
        tok_in = 2 * patch
        one, two = fin_pack[0].T, fin_pack[1].T
        o_in1[...] = one[0:tok_in]
        o_b1[...] = one[tok_in : tok_in + 1]
        o_res[...] = two[0:tok_in]
        o_b2[...] = two[tok_in : tok_in + 1]
        o_gattn[...] = two[tok_in + 1 : tok_in + 2]
        o_gmlp[...] = two[tok_in + 2 : tok_in + 3]

    barrier = pltpu.get_barrier_semaphore()
    for dev in (XN, YN, SIB):
        pl.semaphore_signal(barrier, inc=1, device_id=dev, device_id_type=MESH)
    each_other_plane(
        lambda zb: pl.semaphore_signal(barrier, inc=1, device_id=plane(zb), device_id_type=MESH)
    )
    order = (IN2, WQ, WK, WV, WOUT, WUP, WDOWN)
    for w in order:
        own_copy(w).start()
    cot_copy = pltpu.make_async_copy(cot_hbm, cot, lsem.at[8])
    cot_copy.start()

    @pl.when(m == 0)
    def _():
        pack_block(PK.at[0, row_of(f)], w_in1, [b_in1])

    @pl.when(m == 1)
    def _():
        pack_block(PK.at[1, row_of(f)], w_res, [b_in2, g_attn, g_mlp])

    pl.semaphore_wait(barrier, 6)

    ag_own(PACK)
    ag_own(WQ)
    ag_own(WK)
    ag_own(WOUT)
    ag_own(IN2)
    ag_own(WUP)
    ag_column(PACK)
    ag_column(WQ)
    ag_own(WV)
    ag_plane(PACK)
    ag_column(WK)
    ag_last(PACK)
    swap_start(0)
    ag_plane(WQ)
    prepare()
    ag_plane(WK)
    swap_wait(0)
    ag_column(IN2)
    token_hidden()
    ag_plane(IN2)
    ag_own(WDOWN)
    ag_last(WK)
    ag_plane(WUP)
    ag_column(WV)
    ag_last(IN2)
    ag_column(WOUT)
    token_out()
    ag_last(WQ)
    ag_plane(WV)
    swap_start(1)
    swap_wait(1)
    norm_first()
    project(WK, k)
    ag_plane(WOUT)
    project(WQ, q)
    ag_relay(WUP)
    ag_column(WDOWN)
    ag_last(WV)
    project_v()
    attend()
    ag_last(WOUT)
    attend_out()
    swap_start(2)
    ag_plane(WDOWN)
    swap_wait(2)
    norm_second()
    ag_last(WUP)
    feed_up()
    ag_last(WDOWN)
    grad_down()
    rs_start(WDOWN)
    feed_down()
    swap_start(3)
    grad_hidden()
    grad_norm2()
    swap_start(4)
    swap_wait(3)
    grad_up()
    rs_start(WUP)
    write_output()
    swap_wait(4)
    norm_grad2()
    grad_out()
    rs_start(WOUT)
    rs_turn(WDOWN)
    grad_attended()
    attend_back()
    unrotate()
    rs_turn(WOUT)
    weight_grad(WQ, nrm, dq[...])
    weight_grad(WK, nrm, dk[...])
    rs_start(WK)
    rs_relay(WUP)
    rs_out(WOUT)
    grad_norm1()
    swap_start(5)
    rs_start(WQ)
    rs_turn(WQ)
    rs_out(WDOWN)
    swap_wait(5)
    pre_act()
    norm_grad1()
    rs_turn(WK)
    rs_final(WOUT)
    grad_in2()
    rs_start(IN2)
    grad_token()
    swap_start(6)
    swap_wait(6)
    rs_out(WK)
    rs_turn(IN2)
    rs_out(WQ)
    weight_grad(WV, nrm, dv[...])
    rs_start(WV)
    grad_pre()
    grad_pack()
    rs_start(PACK)
    rs_out(IN2)
    rs_final(WQ)
    rs_turn(PACK)
    rs_turn(WV)
    grad_values()
    rs_out(PACK)
    rs_zsum(WUP)
    rs_out(WV)
    rs_final(IN2)
    swap_start(7)
    rs_turn(WUP)
    rs_final(PACK)
    rs_final(WK)
    swap_wait(7)
    swap_start(8)
    rs_final(WDOWN)
    swap_wait(8)
    rs_final(WUP)
    rs_final(WV)
    write_small()

    def drain(ref, sem):
        remote(ref, ref, sem, sem, XN).wait_send()

    for w in (PACK,) + order:
        ref = PK.at[m] if w == PACK else W.at[w]
        drain(ref.at[pl.ds(0, (11 if w in PLANE_FIRST else 15) * blk)], ag_send.at[w])
        if w in PLANE_FIRST:

            @pl.when(inner)
            def _():
                drain(ref.at[pl.ds(0, 8 * blk)], ag_send.at[w])

        if w == PACK:
            ref = RP
        elif w in Z_FIRST:
            ref = RZ.at[Z_FIRST.index(w)]
        else:
            ref = R.at[CHAIN_LAST.index(w)]
        drain(ref.at[pl.ds(0, 15)], rs_send.at[w])


def pack_block(dst, matrix, vectors):
    tok_in, blk = matrix.shape
    parts = [matrix[...].astype(f32)] + [t[...].astype(f32) for t in vectors]
    parts.append(jnp.zeros((PL - tok_in - len(vectors), blk), f32))
    tall = jnp.concatenate(parts, 0)
    wide = jnp.concatenate([tall, jnp.zeros((PL, PL - blk), f32)], 1)
    dst[...] = wide.T[0:blk].astype(bf16)


def copy_kernel(count, *refs):
    sources, targets, held, sems = refs[:count], refs[count : 2 * count], refs[2 * count : -1], refs[-1]
    inward = [pltpu.make_async_copy(sources[i], held[i], sems.at[0, i]) for i in range(count)]
    outward = [pltpu.make_async_copy(held[i], targets[i], sems.at[1, i]) for i in range(count)]
    for c in inward:
        c.start()
    for a, b in zip(inward, outward):
        a.wait()
        b.start()
    for c in outward:
        c.wait()


def rotate(vectors, places):
    half_width = vectors.shape[-1] // 2
    frequency = 10000.0 ** (-2.0 * jnp.arange(half_width, dtype=jnp.float32) / vectors.shape[-1])
    angles = places[:, :, None, None] * frequency
    cosine = jnp.cos(angles)
    sine_val = jnp.sin(angles)
    first_half = vectors[..., :half_width]
    second_half = vectors[..., half_width:]
    return jnp.concatenate(
        [
            first_half * cosine - second_half * sine_val,
            second_half * cosine + first_half * sine_val,
        ],
        -1,
    )


def rms_norm(resid_rows, gain_vec):
    return (
        resid_rows
        * lax.rsqrt(jnp.mean(resid_rows * resid_rows, -1, keepdims=True) + 1e-06)
        * gain_vec
    )


def activate(up_rows):
    return jax.nn.gelu(up_rows, approximate=False)


def general_device(
    values,
    lengths,
    w_in1,
    b_in1,
    w_in2,
    b_in2,
    w_res,
    g_attn,
    w_qkv,
    w_out,
    g_mlp,
    w_up,
    w_down,
    cotangent,
):
    f32 = jnp.float32
    bf16 = jnp.bfloat16
    gathered = (
        lax.all_gather(w_in1, "fsdp", axis=1, tiled=True),
        lax.all_gather(b_in1, "fsdp", axis=0, tiled=True),
        lax.all_gather(w_in2, "fsdp", axis=0, tiled=True),
        lax.all_gather(b_in2, "fsdp", axis=0, tiled=True),
        lax.all_gather(w_res, "fsdp", axis=1, tiled=True),
        lax.all_gather(g_attn, "fsdp", axis=0, tiled=True),
        lax.all_gather(w_qkv, "fsdp", axis=0, tiled=True),
        lax.all_gather(w_out, "fsdp", axis=1, tiled=True),
        lax.all_gather(g_mlp, "fsdp", axis=0, tiled=True),
        lax.all_gather(w_up, "fsdp", axis=0, tiled=True),
        lax.all_gather(w_down, "fsdp", axis=1, tiled=True),
    )
    (
        full_in1,
        full_b1,
        full_in2,
        full_b2,
        full_res,
        full_gattn,
        full_qkv,
        full_out,
        full_gmlp,
        full_up,
        full_down,
    ) = gathered
    series = lengths.shape[0]
    seq_len = values.shape[0] // series
    patch_len = values.shape[1]
    slot_ids = jnp.arange(seq_len, dtype=jnp.int32)
    pad_count = seq_len - lengths
    padded = slot_ids[None, :] < pad_count[:, None]
    places = (slot_ids[None, :] - pad_count[:, None]).astype(f32)
    keep_mask = (1.0 - padded.astype(f32)).reshape(-1, 1)
    inputs = jnp.concatenate(
        [values.astype(f32) * keep_mask, jnp.broadcast_to(1.0 - keep_mask, values.shape)], 1
    ).astype(bf16)
    pre_act = jnp.dot(inputs, full_in1, preferred_element_type=f32) + full_b1.astype(f32)
    hidden = jax.nn.silu(pre_act).astype(bf16)
    resid0 = (
        jnp.dot(hidden, full_in2, preferred_element_type=f32)
        + full_b2.astype(f32)
        + jnp.dot(inputs, full_res, preferred_element_type=f32)
    )
    gain_attn = full_gattn.astype(f32)
    normed = rms_norm(resid0, gain_attn).astype(bf16)
    projected = jnp.einsum("td,dch->tch", normed, full_qkv, preferred_element_type=f32)
    local_heads = projected.shape[2] // HD
    head_shape = (series, seq_len, local_heads, HD)
    queries = rotate(projected[:, 0].reshape(head_shape), places).astype(bf16)
    key_rows = rotate(projected[:, 1].reshape(head_shape), places).astype(bf16)
    value_heads = projected[:, 2].reshape(head_shape).astype(bf16)
    causal = slot_ids[None, :] <= slot_ids[:, None]
    diagonal = slot_ids[None, :] == slot_ids[:, None]
    allowed = (causal[None] & (jnp.logical_not(padded)[:, None, :] | diagonal[None]))[:, None]
    scale = HD ** (-0.5)

    def score_block():
        raw = jnp.einsum("sqhe,skhe->shqk", queries, key_rows, preferred_element_type=f32) * scale
        return jnp.where(allowed, raw, -1e30)

    scores = score_block()
    row_max = jnp.max(scores, -1, keepdims=True)
    exponent = jnp.exp(scores - row_max)
    row_total = jnp.sum(exponent, -1, keepdims=True)
    log_total = row_max + jnp.log(row_total)
    attn_probs = (exponent / row_total).astype(bf16)
    attended = (
        jnp.einsum("shqk,skhe->sqhe", attn_probs, value_heads, preferred_element_type=f32)
        .reshape(-1, local_heads * HD)
        .astype(bf16)
    )
    branch_one = lax.psum(jnp.dot(attended, full_out, preferred_element_type=f32), "mp")
    resid1 = resid0 + branch_one
    gain_mlp = full_gmlp.astype(f32)
    normed2 = rms_norm(resid1, gain_mlp).astype(bf16)
    up_rows = jnp.dot(normed2, full_up, preferred_element_type=f32)
    mlp_hidden = activate(up_rows).astype(bf16)
    branch_two = lax.psum(
        jnp.dot(mlp_hidden, full_down, preferred_element_type=f32).astype(jnp.bfloat16), "mp"
    ).astype(jnp.float32)
    result = (resid1 + branch_two).astype(bf16)
    again = (
        lax.all_gather(w_in1, "fsdp", axis=1, tiled=True),
        lax.all_gather(b_in1, "fsdp", axis=0, tiled=True),
        lax.all_gather(w_in2, "fsdp", axis=0, tiled=True),
        lax.all_gather(b_in2, "fsdp", axis=0, tiled=True),
        lax.all_gather(w_res, "fsdp", axis=1, tiled=True),
        lax.all_gather(g_attn, "fsdp", axis=0, tiled=True),
        lax.all_gather(w_qkv, "fsdp", axis=0, tiled=True),
        lax.all_gather(w_out, "fsdp", axis=1, tiled=True),
        lax.all_gather(g_mlp, "fsdp", axis=0, tiled=True),
        lax.all_gather(w_up, "fsdp", axis=0, tiled=True),
        lax.all_gather(w_down, "fsdp", axis=1, tiled=True),
    )
    (
        back_in1,
        back_b1,
        back_in2,
        back_b2,
        back_res,
        back_gattn,
        back_qkv,
        back_out,
        back_gmlp,
        back_up,
        back_down,
    ) = again
    cot_rows = cotangent.astype(f32)
    grad_down = jnp.einsum("tf,td->fd", mlp_hidden, cotangent, preferred_element_type=f32)
    grad_hidden = jnp.einsum("td,fd->tf", cotangent, back_down, preferred_element_type=f32)
    unused_one, pull_mlp = jax.vjp(activate, up_rows)
    grad_up_rows = pull_mlp(grad_hidden)[0].astype(bf16)
    grad_up = jnp.einsum("td,tf->df", normed2, grad_up_rows, preferred_element_type=f32)
    norm_part2 = jnp.einsum("tf,df->td", grad_up_rows, back_up, preferred_element_type=f32)
    norm_grad2 = lax.psum(norm_part2, "mp")
    unused_two, pull_norm2 = jax.vjp(rms_norm, resid1, back_gmlp.astype(f32))
    resid_part1, grad_gmlp = pull_norm2(norm_grad2)
    resid1_grad = cot_rows + resid_part1
    out_grad = resid1_grad.astype(bf16)
    grad_out = jnp.einsum("th,td->hd", attended, out_grad, preferred_element_type=f32)
    attended_grad = (
        jnp.einsum("td,hd->th", out_grad, back_out, preferred_element_type=f32)
        .astype(bf16)
        .reshape(head_shape)
    )
    scores = score_block()
    probs_full = jnp.exp(scores - log_total)
    value_grad = jnp.einsum(
        "shqk,sqhe->skhe", probs_full.astype(bf16), attended_grad, preferred_element_type=f32
    )
    prob_grad = jnp.einsum(
        "sqhe,skhe->shqk", attended_grad, value_heads, preferred_element_type=f32
    )
    score_grad = (
        probs_full * (prob_grad - jnp.sum(prob_grad * probs_full, -1, keepdims=True))
    ).astype(bf16)
    query_grad = (
        jnp.einsum("shqk,skhe->sqhe", score_grad, key_rows, preferred_element_type=f32) * scale
    )
    key_grad = (
        jnp.einsum("shqk,sqhe->skhe", score_grad, queries, preferred_element_type=f32) * scale
    )
    width_local = local_heads * HD
    qkv_rows = jnp.stack(
        [
            rotate(query_grad, -places).reshape(-1, width_local),
            rotate(key_grad, -places).reshape(-1, width_local),
            value_grad.reshape(-1, width_local),
        ],
        1,
    ).astype(bf16)
    grad_qkv = jnp.einsum("td,tch->dch", normed, qkv_rows, preferred_element_type=f32)
    norm_part1 = jnp.einsum("tch,dch->td", qkv_rows, back_qkv, preferred_element_type=f32)
    norm_grad1 = lax.psum(norm_part1, "mp")
    unused_three, pull_norm1 = jax.vjp(rms_norm, resid0, back_gattn.astype(f32))
    resid_part0, grad_gattn = pull_norm1(norm_grad1)
    resid0_grad = (resid1_grad + resid_part0).astype(bf16)
    grad_in2 = jnp.einsum("th,td->hd", hidden, resid0_grad, preferred_element_type=f32)
    grad_b2 = jnp.sum(resid0_grad.astype(f32), 0)
    grad_res = jnp.einsum("tp,td->pd", inputs, resid0_grad, preferred_element_type=f32)
    hidden_grad = jnp.einsum("td,hd->th", resid0_grad, back_in2, preferred_element_type=f32)
    unused_four, pull_silu = jax.vjp(jax.nn.silu, pre_act)
    pre_grad = pull_silu(hidden_grad)[0].astype(bf16)
    grad_in1 = jnp.einsum("tp,th->ph", inputs, pre_grad, preferred_element_type=f32)
    grad_b1 = jnp.sum(pre_grad.astype(f32), 0)
    input_grad = jnp.einsum(
        "th,ph->tp", pre_grad, back_in1, preferred_element_type=f32
    ) + jnp.einsum("td,pd->tp", resid0_grad, back_res, preferred_element_type=f32)
    values_grad = input_grad[:, :patch_len] * keep_mask
    shares = tuple(
        (
            lax.psum_scatter(grad_in1, "fsdp", scatter_dimension=1, tiled=True),
            lax.psum_scatter(grad_b1, "fsdp", scatter_dimension=0, tiled=True),
            lax.psum_scatter(grad_in2, "fsdp", scatter_dimension=0, tiled=True),
            lax.psum_scatter(grad_b2, "fsdp", scatter_dimension=0, tiled=True),
            lax.psum_scatter(grad_res, "fsdp", scatter_dimension=1, tiled=True),
            lax.psum_scatter(grad_gattn, "fsdp", scatter_dimension=0, tiled=True),
            lax.psum_scatter(grad_qkv, "fsdp", scatter_dimension=0, tiled=True),
            lax.psum_scatter(grad_out, "fsdp", scatter_dimension=1, tiled=True),
            lax.psum_scatter(grad_gmlp, "fsdp", scatter_dimension=0, tiled=True),
            lax.psum_scatter(grad_up, "fsdp", scatter_dimension=0, tiled=True),
            lax.psum_scatter(grad_down, "fsdp", scatter_dimension=1, tiled=True),
        )
    )
    return (result, values_grad) + shares


def fused_device(
    values,
    lengths,
    w_in1,
    b_in1,
    w_in2,
    b_in2,
    w_res,
    g_attn,
    w_qkv,
    w_out,
    g_mlp,
    w_up,
    w_down,
    cotangent,
):
    rows, width = cotangent.shape
    half = w_out.shape[0]
    blk = w_in2.shape[0]
    patch = values.shape[1]
    tok_in = w_in1.shape[0]
    heads = half // HD
    vmem = pl.BlockSpec(memory_space=pltpu.VMEM)
    hbm = pl.BlockSpec(memory_space=pl.ANY)

    def shape(*dims, dtype=f32):
        return jax.ShapeDtypeStruct(dims, dtype)

    out_shape = (
        shape(rows, width, dtype=bf16),
        shape(patch, rows),
        shape(tok_in, blk),
        shape(1, blk),
        shape(blk, width),
        shape(1, blk),
        shape(tok_in, blk),
        shape(1, blk),
        shape(3, blk, half),
        shape(blk, half),
        shape(1, blk),
        shape(blk, half),
        shape(blk, half),
    )
    V = pltpu.VMEM
    scratch = [
        V((NW, width, half), bf16),
        V((2, width, PL), bf16),
        V((NW, width, half), bf16),
        V((width, PL), bf16),
        V((len(CHAIN_LAST), SLOTS, blk, half), bf16),
        V((max(1, len(Z_FIRST)), Z_SLOTS, blk, half), bf16),
        V((SLOTS, blk, PL), bf16),
        V((2, rows, half), f32),
        V((rows, width), f32),
        V((2, rows, width), f32),
        V((2, rows, width), f32),
        V((rows, width), bf16),
        V((rows, width), bf16),
        V((rows, width), bf16),
        V((rows, width), bf16),
        V((rows, width), bf16),
        V((rows, half), bf16),
        V((rows, half), bf16),
        V((rows, half), bf16),
        V((heads, rows, rows), f32),
        V((rows, half), bf16),
        V((rows, half), f32),
        V((rows, half), bf16),
        V((rows, width), bf16),
        V((rows, half), bf16),
        V((rows, half), bf16),
        V((rows, half), bf16),
        V((rows, half), bf16),
        V((rows, width), f32),
        V((rows, width), bf16),
        V((rows, half), f32),
        V((rows, half), f32),
        V((rows, rows), f32),
        V((rows, PL), bf16),
        V((2, 8, width), f32),
        V((2, 16, width), bf16),
        V((8, width), f32),
        V((rows, PL), f32),
        V((2, blk, half), f32),
        V((2, blk, PL), f32),
        pltpu.SemaphoreType.DMA((8,)),
        pltpu.SemaphoreType.DMA((8, 16)),
        pltpu.SemaphoreType.DMA((8,)),
        pltpu.SemaphoreType.DMA((8, Z_SLOTS)),
        pltpu.SemaphoreType.DMA((9,)),
        pltpu.SemaphoreType.DMA((9,)),
        pltpu.SemaphoreType.DMA((9,)),
    ]
    results = pl.pallas_call(
        layer_kernel,
        name="layer",
        out_shape=out_shape,
        in_specs=[pl.BlockSpec(memory_space=pltpu.SMEM)] + [vmem] * 7 + [hbm] * 6,
        out_specs=(vmem,) * len(out_shape),
        scratch_shapes=scratch,
        compiler_params=pltpu.CompilerParams(
            collective_id=0, has_side_effects=True, vmem_limit_bytes=VMEM_BYTES
        ),
    )(
        lengths,
        values.T,
        w_in1,
        w_res,
        b_in1[None],
        b_in2[None],
        g_attn[None],
        g_mlp[None],
        w_in2,
        jnp.transpose(w_qkv, (1, 0, 2)),
        w_out.T,
        w_up,
        w_down.T,
        cotangent,
    )
    (
        out,
        d_values,
        d_in1,
        d_b1,
        d_in2,
        d_b2,
        d_res,
        d_gattn,
        d_qkv,
        d_out,
        d_gmlp,
        d_up,
        d_down,
    ) = pl.pallas_call(
        functools.partial(copy_kernel, len(out_shape)),
        name="hand_over",
        out_shape=out_shape,
        in_specs=[hbm] * len(out_shape),
        out_specs=(hbm,) * len(out_shape),
        scratch_shapes=[V(s.shape, s.dtype) for s in out_shape]
        + [pltpu.SemaphoreType.DMA((2, len(out_shape)))],
    )(*results)
    return (
        out,
        d_values.T,
        d_in1,
        d_b1[0],
        d_in2,
        d_b2[0],
        d_res,
        d_gattn[0],
        jnp.transpose(d_qkv, (1, 0, 2)),
        d_out.T,
        d_gmlp[0],
        d_up,
        d_down.T,
    )


def on_device(*args):
    blk, width = args[4].shape
    half = args[9].shape[0]
    shards = width // blk
    series = args[1].shape[0]
    fits = (
        shards == 16
        and 2 * half == width
        and blk % 16 == 0
        and half % 128 == 0
        and args[0].shape[0] % 64 == 0
        and series <= 8
    )
    return (fused_device if fits else general_device)(*args)


def solution(mesh):
    in_specs = (
        P("fsdp", None),
        P("fsdp"),
        P(None, "fsdp"),
        P("fsdp"),
        P("fsdp", None),
        P("fsdp"),
        P(None, "fsdp"),
        P("fsdp"),
        P("fsdp", None, "mp"),
        P("mp", "fsdp"),
        P("fsdp"),
        P("fsdp", "mp"),
        P("mp", "fsdp"),
        P("fsdp", None),
    )
    out_specs = (
        P("fsdp", None),
        P("fsdp", None),
        P(None, "fsdp"),
        P("fsdp"),
        P("fsdp", None),
        P("fsdp"),
        P(None, "fsdp"),
        P("fsdp"),
        P("fsdp", None, "mp"),
        P("mp", "fsdp"),
        P("fsdp"),
        P("fsdp", "mp"),
        P("mp", "fsdp"),
    )
    return jax.shard_map(
        on_device, mesh=mesh, in_specs=in_specs, out_specs=out_specs, check_vma=False
    )
```

```python
import functools
import math

import jax
import jax.numpy as jnp
from jax import lax
from jax.experimental import pallas as pl
from jax.experimental.pallas import tpu as pltpu
from jax.sharding import PartitionSpec as P

HD = 80
MESH = pl.DeviceIdType.MESH
VMEM_BYTES = 63 * 2**20
f32 = jnp.float32
bf16 = jnp.bfloat16

IN2, WQ, WK, WV, WOUT, WUP, WDOWN, PACK, XTRA = range(9)
NW = 7
PL = 128
SPLIT, CUT = WQ, 384
ITEMS = (PACK, IN2, WQ, WK, WV, WOUT, WUP, WDOWN) + (() if SPLIT is None else (XTRA,))
PLANE_FIRST = (WUP, XTRA)
Z_FIRST = (WUP, XTRA)


def cols_of(w, half):
    if SPLIT is None or w not in (SPLIT, XTRA):
        return 0, PL if w == PACK else half
    return (0, CUT) if w == SPLIT else (CUT, half)


SLOT_A, SLOT_X, SLOT_Y, SLOT_V, SLOTS = 0, 4, 8, 12, 16
Z_RELAY, Z_NEAR, Z_FAR, Z_A, Z_X, Z_Y, Z_SLOTS = 0, 8, 12, 16, 17, 18, 19


def dot(left, right, left_dim, right_dim):
    return lax.dot_general(
        left, right, (((left_dim,), (right_dim,)), ((), ())), preferred_element_type=f32
    )


def layer_kernel(
    lengths,
    values_t,
    w_in1,
    w_res,
    b_in1,
    b_in2,
    g_attn,
    g_mlp,
    in2,
    qkv,
    out_t,
    up,
    down_t,
    cot_hbm,
    o_out,
    o_dval,
    o_in1,
    o_b1,
    o_in2,
    o_b2,
    o_res,
    o_gattn,
    o_qkv,
    o_wout,
    o_gmlp,
    o_up,
    o_down,
    W,
    PK,
    G,
    GP,
    recv,
    R0,
    R1,
    S,
    X,
    SB,
    XB,
    hid,
    nrm,
    nrm2,
    q,
    k,
    v,
    prob,
    att,
    gprime,
    mlp,
    cot,
    dup,
    dq,
    dk,
    dv,
    tmp,
    dr0,
    rope_c,
    rope_s,
    bias,
    inx,
    gains,
    dgs,
    accg,
    keep_col,
    fin,
    fin_in2,
    fin_pack,
    out_rows,
    in2_rows,
    ag_send,
    ag_recv,
    rs_send,
    rs_recv,
    ex_send,
    ex_recv,
    lsem,
    out_sem,
):
    rows, width = cot.shape
    half = W.shape[2]
    blk = in2.shape[0]
    series = lengths.shape[0]
    seq = rows // series
    heads = half // HD
    patch = values_t.shape[0]

    f = lax.axis_index("fsdp")
    m = lax.axis_index("mp")
    x = lax.rem(f, 2)
    y = lax.rem(lax.div(f, 2), 2)
    z = lax.div(f, 4)
    c0 = f - 4 * z
    cx = c0 + 1 - 2 * x
    cy = c0 + 2 - 4 * y
    cd = 3 - c0
    XN, YN, SIB = (4 * z + cx, m), (4 * z + cy, m), (f, 1 - m)
    z_high = (z >= 2).astype(jnp.int32)
    inner = jnp.logical_and(z > 0, z < 3)
    z_inner = inner.astype(jnp.int32)
    z_near = z + 1 - 2 * lax.rem(z, 2)
    z_far = 2 - z_high
    z_even = lax.rem(z, 2) == 0

    def plane(zb):
        return (4 * zb + c0, m)

    def near(i):
        swap = (i == 0).astype(jnp.int32) - (i == 1).astype(jnp.int32)
        low = i + z_inner * swap
        return low + z_high * (3 - 2 * low)

    def each_plane(order, body, start=0):
        def step(i, carry):
            body(order(i))
            return carry

        lax.fori_loop(start, 4, step, 0)

    def each_other_plane(body):
        each_plane(near, body, 1)

    nearest = [near(jnp.int32(i)) for i in range(4)]

    def row_of(b):
        return pl.ds(pl.multiple_of(b * blk, 16), blk)

    def whole(w):
        return SPLIT if w == XTRA else w

    def part(ref, w, *index):
        low, high = cols_of(w, half)
        return ref.at[(*index, slice(low, high))]

    def w_rows(w, r):
        return PK.at[m, r] if w == PACK else part(W, w, whole(w), r)

    def w_block(w, b):
        return w_rows(w, row_of(b))

    def g_block(w, b):
        return GP.at[row_of(b)] if w == PACK else part(G, w, whole(w), row_of(b))

    def r_block(w, s):
        return recv[w].at[s]

    def remote(src, dst, send, recv, dev):
        return pltpu.make_async_remote_copy(
            src_ref=src, dst_ref=dst, send_sem=send, recv_sem=recv, device_id=dev, device_id_type=MESH
        )

    def ag_push(w, b, *devs):
        ref = w_block(w, b)
        for dev in devs:
            remote(ref, ref, ag_send.at[w], ag_recv.at[w, b], dev).start()

    def ag_await(w, b):
        ref = w_block(w, b)
        remote(ref, ref, ag_send.at[w], ag_recv.at[w, b], XN).wait_recv()

    mcols = pl.ds(pl.multiple_of(m * half, 128), half)

    def own_copy(w):
        if w == IN2:
            src = in2.at[:, mcols]
        elif whole(w) in (WQ, WK, WV):
            src = part(qkv, w, whole(w) - WQ, slice(None))
        else:
            src = part({WOUT: out_t, WUP: up, WDOWN: down_t}[whole(w)], w, slice(None))
        return pltpu.make_async_copy(src, w_block(w, f), lsem.at[w])

    def ag_ready(w):
        own_copy(w).wait()

    def ag_own_xy(w):
        ag_push(w, f, XN, YN)

    def ag_own_z(w):
        if w in PLANE_FIRST:
            ag_push(w, f, plane(z_near), plane(z_far))
        else:
            each_other_plane(lambda zb: ag_push(w, f, plane(zb)))

    def ag_column(w, i):
        b = 4 * nearest[i] + c0
        ag_await(w, b)
        ag_push(w, b, XN, YN)

    def ag_from_x(w, zb, even):
        ag_await(w, 4 * zb + cx)

        @pl.when(even)
        def _():
            ag_push(w, 4 * zb + cx, YN)

    def ag_from_y(w, zb, even):
        ag_await(w, 4 * zb + cy)

        @pl.when(jnp.logical_not(even))
        def _():
            ag_push(w, 4 * zb + cy, XN)

    def ag_plane(w, i):
        even = lax.rem(nearest[i], 2) == 0
        ag_from_x(w, nearest[i], even)
        ag_from_y(w, nearest[i], even)

    def ag_first_x(w):
        ag_from_x(w, z, z_even)
        ag_push(w, 4 * z + cx, plane(z_near), plane(z_far))

    def ag_first_y(w):
        ag_from_y(w, z, z_even)
        ag_push(w, 4 * z + cy, plane(z_near), plane(z_far))

    def ag_first_d(w):
        ag_await(w, 4 * z + cd)
        ag_push(w, 4 * z + cd, plane(z_near), plane(z_far))

    def ag_relay(w, i):
        @pl.when(inner)
        def _():
            zb = (3 - z, 3 * (1 - z_high))[i]
            for c in (c0, cx, cy, cd):
                ag_await(w, 4 * zb + c)
                ag_push(w, 4 * zb + c, plane(3 * z_high))

    def ag_last(w):
        if w in PLANE_FIRST:
            for c in (c0, cx, cy, cd):
                ag_await(w, 4 * z_near + c)

            @pl.when(jnp.logical_not(inner))
            def _():
                for zb in (z_far, 3 - z):
                    for c in (c0, cx, cy, cd):
                        ag_await(w, 4 * zb + c)
        else:
            each_plane(near, lambda zb: ag_await(w, 4 * zb + cd))

    def final_of(w):
        if w == PACK:
            return fin_pack.at[m]
        if w == IN2:
            return fin_in2.at[m]
        return part(fin, w, whole(w) - WQ, slice(None))

    targets = [o_qkv.at[0], o_qkv.at[1], o_qkv.at[2], o_wout, o_up, o_down]

    def hand_out(w):
        target = part(targets[whole(w) - WQ], w, slice(None))
        return pltpu.make_async_copy(final_of(w), target, out_sem.at[w])

    def rs_push(w, src, slot, dev):
        remote(src, r_block(w, slot), rs_send.at[w], rs_recv.at[w, slot], dev).start()

    def rs_await(w, slot):
        ref = r_block(w, slot)
        remote(ref, ref, rs_send.at[w], rs_recv.at[w, slot], XN).wait_recv()

    def add_to(ref, other):
        ref[...] = (ref[...].astype(f32) + other[...].astype(f32)).astype(bf16)

    def sum3(a, b, c):
        return a[...].astype(f32) + b[...].astype(f32) + c[...].astype(f32)

    def rs_start(w, i):
        zb = nearest[3 - i]
        even = lax.rem(zb, 2) == 0

        @pl.when(even)
        def _():
            rs_push(w, g_block(w, 4 * zb + cd), SLOT_A + zb, YN)
            rs_push(w, g_block(w, 4 * zb + cy), SLOT_Y + zb, YN)

        @pl.when(jnp.logical_not(even))
        def _():
            rs_push(w, g_block(w, 4 * zb + cd), SLOT_A + zb, XN)
            rs_push(w, g_block(w, 4 * zb + cx), SLOT_X + zb, XN)

    def turn(w, slot_a, even, own_x, own_y, slot_x, slot_y):
        rs_await(w, slot_a)
        ref = r_block(w, slot_a)

        @pl.when(even)
        def _():
            add_to(ref, own_x)
            rs_push(w, ref, slot_x, XN)

        @pl.when(jnp.logical_not(even))
        def _():
            add_to(ref, own_y)
            rs_push(w, ref, slot_y, YN)

    def rs_turn(w, i):
        zb = nearest[3 - i]
        own_x, own_y = g_block(w, 4 * zb + cx), g_block(w, 4 * zb + cy)
        turn(w, SLOT_A + zb, lax.rem(zb, 2) == 0, own_x, own_y, SLOT_X + zb, SLOT_Y + zb)

    def rs_out(w, i):
        zb = nearest[i]
        rs_await(w, SLOT_X + zb)
        rs_await(w, SLOT_Y + zb)
        ref = r_block(w, SLOT_X + zb)
        total = sum3(g_block(w, 4 * zb + c0), ref, r_block(w, SLOT_Y + zb))
        if i == 0:
            final_of(w)[...] = total
        else:
            ref[...] = total.astype(bf16)
            rs_push(w, ref, SLOT_V + z, plane(zb))

    def rs_first_far(w, i):
        @pl.when(jnp.logical_not(inner))
        def _():
            zb = (3 - z, z_far)[i]
            for c in (cd, cx, cy, c0):
                slot = Z_RELAY + 4 * lax.rem(zb, 2) + c
                rs_push(w, g_block(w, 4 * zb + c), slot, plane(1 + z_high))

    def rs_first_near(w):
        for c in (cd, cx, cy, c0):
            rs_push(w, g_block(w, 4 * z_near + c), Z_NEAR + c, plane(z_near))

    def rs_relay(w, i):
        @pl.when(inner)
        def _():
            zb = (3 * (1 - z_high), z_far)[i]
            for c in (cd, cx, cy, c0):
                slot = Z_RELAY + 4 * lax.rem(zb, 2) + c
                rs_await(w, slot)
                ref = r_block(w, slot)
                add_to(ref, g_block(w, 4 * zb + c))
                rs_push(w, ref, Z_FAR + c, plane(zb))

    def rs_zsum(w, i):
        c = (cd, cx, cy, c0)[i]
        rs_await(w, Z_NEAR + c)
        rs_await(w, Z_FAR + c)
        ref = r_block(w, Z_NEAR + c)
        total = sum3(ref, r_block(w, Z_FAR + c), g_block(w, 4 * z + c))
        if i == 3:
            final_of(w)[...] = total
            return
        ref[...] = total.astype(bf16)
        if i in (0, 2):

            @pl.when(z_even)
            def _():
                rs_push(w, ref, Z_A if i == 0 else Z_Y, YN)

        if i in (0, 1):

            @pl.when(jnp.logical_not(z_even))
            def _():
                rs_push(w, ref, Z_A if i == 0 else Z_X, XN)

    def rs_first_turn(w):
        turn(w, Z_A, z_even, r_block(w, Z_NEAR + cx), r_block(w, Z_NEAR + cy), Z_X, Z_Y)

    def rs_final(w):
        final = final_of(w)
        if w in Z_FIRST:
            rs_await(w, Z_X)
            rs_await(w, Z_Y)
            final[...] = sum3(final, r_block(w, Z_X), r_block(w, Z_Y))
        else:
            for i in (1, 2, 3):
                rs_await(w, SLOT_V + nearest[i])
            parts = [r_block(w, SLOT_V + nearest[i])[...].astype(f32) for i in (1, 2, 3)]
            final[...] = final[...] + (parts[0] + parts[1] + parts[2])
        if w not in (IN2, PACK):
            hand_out(w).start()

    def exchange(i):
        src, dst = {
            0: lambda: (PK.at[m], PK.at[m]),
            1: lambda: (R0.at[m], R0.at[m]),
            2: lambda: (S.at[0], X.at[0]),
            3: lambda: (SB, XB),
            4: lambda: (S.at[1], X.at[1]),
            5: lambda: (S.at[0], X.at[0]),
            6: lambda: (S.at[1], X.at[1]),
            7: lambda: (fin_in2.at[m], fin_in2.at[m]),
            8: lambda: (fin_pack.at[m], fin_pack.at[m]),
        }[i]()
        return remote(src, dst, ex_send.at[i], ex_recv.at[i], SIB)

    def swap_start(i):
        exchange(i).start()

    def swap_wait(i):
        exchange(i).wait()

    def by_rows(step, body, unroll=4):
        def one(i, carry):
            body(pl.ds(pl.multiple_of(i * step, step), step))
            return carry

        lax.fori_loop(0, rows // step, one, 0, unroll=unroll)

    halves = (slice(0, half), slice(half, width))

    lens = [lengths[s] for s in range(series)]

    def pad_of(slot):
        total = jnp.zeros(slot.shape, jnp.int32)
        for s in range(series):
            inside = jnp.logical_and(slot >= s * seq, slot < (s + 1) * seq)
            total = jnp.where(inside, (s + 1) * seq - lens[s], total)
        return total

    def series_of(slot):
        total = jnp.zeros(slot.shape, jnp.int32)
        for s in range(1, series):
            total = total + (slot >= s * seq).astype(jnp.int32)
        return total

    lane = lax.broadcasted_iota(jnp.int32, (1, half), 1).astype(f32)
    in_head = lane - HD * jnp.floor((lane + 0.5) / HD)
    first = in_head < HD // 2

    def prepare():
        slot_col = lax.broadcasted_iota(jnp.int32, (rows, 1), 0)
        keep = jnp.broadcast_to((slot_col >= pad_of(slot_col)).astype(f32), keep_col.shape)
        keep_col[...] = keep
        lane_i = lax.broadcasted_iota(jnp.int32, (rows, PL), 1)
        tall = jnp.concatenate([values_t[...].astype(f32), jnp.zeros((PL - patch, rows), f32)], 0)
        inx[...] = jnp.where(
            lane_i < patch,
            tall.T * keep,
            jnp.where(lane_i < 2 * patch, 1.0 - keep, (lane_i == 2 * patch).astype(f32)),
        ).astype(bf16)

        key_slot = lax.broadcasted_iota(jnp.int32, (1, rows), 1)
        key_ok = (key_slot >= pad_of(key_slot)).astype(jnp.int32)
        key_series = series_of(key_slot)

        def bias_rows(s):
            shape = (s.size, rows)
            a = lax.broadcasted_iota(jnp.int32, shape, 0) + s.start
            b = jnp.broadcast_to(key_slot, shape)
            same = series_of(a) == jnp.broadcast_to(key_series, shape)
            ok = jnp.logical_or(jnp.broadcast_to(key_ok, shape) == 1, a == b)
            allowed = jnp.logical_and(jnp.logical_and(same, b <= a), ok)
            bias[s, :] = jnp.where(allowed, 0.0, -1e30)

        by_rows(32, bias_rows, 1)
        turn_i = jnp.where(first, in_head, in_head - HD // 2)
        frequency = jnp.exp(turn_i * (-2.0 * math.log(10000.0) / HD))

        def rope_rows(s):
            slot = lax.broadcasted_iota(jnp.int32, (s.size, 1), 0) + s.start
            place = (slot - pad_of(slot)).astype(f32)
            angle = place * frequency
            rope_c[s, :] = jnp.cos(angle)
            sine = jnp.sin(angle)
            rope_s[s, :] = jnp.where(first, -sine, sine)

        by_rows(16, rope_rows, 1)

    def rope(t, s, inverse):
        other = jnp.where(first, pltpu.roll(t, half - HD // 2, 1), pltpu.roll(t, HD // 2, 1))
        turned = other * rope_s[s, :]
        return t * rope_c[s, :] - turned if inverse else t * rope_c[s, :] + turned

    gain_lane = lax.broadcasted_iota(jnp.int32, (16, PL), 1)

    def pre_act():
        for cols in halves:
            tmp[:, cols] = dot(inx[...], PK[0, cols, :], 1, 1)

    def token_hidden():
        for i in range(2):
            pick = (gain_lane == 2 * patch + 1 + i).astype(bf16)
            gains[i] = dot(pick, PK[1], 1, 1)[0:8]
        pre_act()

        def silu_rows(s):
            t = tmp[s, :]
            hid[s, :] = (t / (1.0 + jnp.exp(-t))).astype(bf16)

        by_rows(16, silu_rows)

    def token_out():
        R0[m] = dot(hid[...], W[IN2], 1, 0) + dot(inx[...], PK[1, mcols, :], 1, 1)

    def norm_rows(load, gain, out):
        def body(s):
            a, b = load(s)
            mean = (jnp.sum(a * a, -1, keepdims=True) + jnp.sum(b * b, -1, keepdims=True)) / width
            scale = lax.rsqrt(mean + 1e-06)
            out[s, halves[0]] = (a * scale * gain[0:1, halves[0]]).astype(bf16)
            out[s, halves[1]] = (b * scale * gain[0:1, halves[1]]).astype(bf16)

        by_rows(16, body)

    def norm_first():
        norm_rows(lambda s: (R0[0, s, :], R0[1, s, :]), gains.at[0], nrm)

    def project(w, out):
        tmp[:, halves[0]] = dot(nrm[...], W[w], 1, 0)

        def body(s):
            out[s, :] = rope(tmp[s, halves[0]], s, False).astype(bf16)

        by_rows(16, body)

    def project_v():
        v[...] = dot(nrm[...], W[WV], 1, 0).astype(bf16)

    win = 256
    scale = HD ** (-0.5)
    win_lane = lax.broadcasted_iota(jnp.int32, (1, win), 1)

    def head_window(h):
        low = jnp.minimum(lax.div(h * HD, 128) * 128, half - win)
        inside = jnp.logical_and(win_lane >= h * HD - low, win_lane < h * HD - low + HD)
        return pl.ds(pl.multiple_of(low, 128), win), inside

    def only(inside, t):
        return jnp.where(inside, t.astype(f32), 0.0).astype(bf16)

    def attend():
        att[...] = jnp.zeros_like(att)

        def one(h, carry):
            cols, inside = head_window(h)
            score = dot(only(inside, q[:, cols]), k[:, cols], 1, 1) * scale + bias[...]
            exponent = jnp.exp(score - jnp.max(score, -1, keepdims=True))
            p = exponent / jnp.sum(exponent, -1, keepdims=True)
            prob[h] = p
            mixed = dot(p.astype(bf16), v[:, cols], 1, 0)
            att[:, cols] = jnp.where(inside, mixed, att[:, cols].astype(f32)).astype(bf16)
            return carry

        lax.fori_loop(0, heads, one, 0, unroll=2)

    def widen(dst, terms):
        for cols in halves:
            total = None
            for left, w in terms:
                part = dot(left[...], W[w, cols, :], 1, 1)
                total = part if total is None else total + part
            dst[:, cols] = total.astype(dst.dtype)

    def attend_out():
        widen(S.at[0], [(att, WOUT)])

    def norm_second():
        def body(s):
            for i, cols in enumerate(halves):
                R1[s, cols] = R0[i, s, :] + (S[0, s, cols] + X[0, s, cols])

        by_rows(16, body)
        norm_rows(lambda s: (R1[s, halves[0]], R1[s, halves[1]]), gains.at[1], nrm2)

    def feed_up():
        tmp[:, halves[0]] = dot(nrm2[...], W[WUP], 1, 0)

        def gelu_rows(s):
            t = tmp[s, halves[0]]
            phi = 0.5 * (1.0 + lax.erf(t * (2.0**-0.5)))
            mlp[s, :] = (t * phi).astype(bf16)
            gprime[s, :] = phi + t * jnp.exp(-0.5 * t * t) * ((2.0 * math.pi) ** -0.5)

        by_rows(16, gelu_rows)

    def weight_grad(w, left, right):
        for r in halves:
            G[w, r, :] = dot(left[:, r], right, 0, 0).astype(bf16)

    def grad_down():
        cot_copy.wait()
        weight_grad(WDOWN, cot, mlp[...])

    def grad_hidden():
        tmp[:, halves[0]] = dot(cot[...], W[WDOWN], 1, 0)

        def dup_rows(s):
            dup[s, :] = (tmp[s, halves[0]] * gprime[s, :]).astype(bf16)

        by_rows(16, dup_rows)

    def grad_up():
        weight_grad(WUP, nrm2, dup[...])

    def feed_down():
        widen(SB, [(mlp, WDOWN)])

    def grad_norm2():
        widen(S.at[1], [(dup, WUP)])

    out_copy = pltpu.make_async_copy(out_rows, o_out, out_sem.at[PACK])
    in2_copy = pltpu.make_async_copy(in2_rows, o_in2, out_sem.at[IN2])

    def write_output():
        def body(s):
            out_rows[s, :] = (R1[s, :] + (SB[s, :].astype(f32) + XB[s, :].astype(f32))).astype(bf16)

        by_rows(16, body)
        out_copy.start()

    def norm_grad(load, i_part, gain, base, out, keep_sum):
        def body(i, carry):
            s = pl.ds(pl.multiple_of(i * 16, 16), 16)
            xs = load(s)
            mean = sum(jnp.sum(t * t, -1, keepdims=True) for t in xs) / width
            r = lax.rsqrt(mean + 1e-06)
            n1 = [t * r for t in xs]
            dn = [S[i_part, s, c] + X[i_part, s, c] for c in halves]
            gd = [gain[0:1, c] * t for c, t in zip(halves, dn)]
            along = sum(jnp.sum(a * b, -1, keepdims=True) for a, b in zip(gd, n1)) / width
            for c, a, b in zip(halves, gd, n1):
                out(s, c, base(s, c) + r * (a - b * along))
            for c, a, b in zip(halves, dn, n1):
                prod = a * b
                accg[:, c] += prod[0:8] + prod[8:16]
            return carry

        accg[...] = jnp.zeros_like(accg)
        lax.fori_loop(0, rows // 16, body, 0, unroll=4)
        total = accg[...]
        high = total.astype(bf16)
        keep_sum[...] = jnp.concatenate([high.astype(f32), total - high.astype(f32)], 0).astype(bf16)

    def norm_grad2():
        def out(s, c, t):
            R1[s, c] = t
            nrm2[s, c] = t.astype(bf16)

        norm_grad(
            lambda s: [R1[s, c] for c in halves],
            1,
            gains.at[1],
            lambda s, c: cot[s, c].astype(f32),
            out,
            dgs.at[1],
        )

    def norm_grad1():
        def out(s, c, t):
            dr0[s, c] = t.astype(bf16)

        norm_grad(
            lambda s: [R0[i, s, :] for i in range(2)],
            0,
            gains.at[0],
            lambda s, c: R1[s, c],
            out,
            dgs.at[0],
        )

    def grad_out():
        weight_grad(WOUT, nrm2, att[...])

    def grad_attended():
        att[...] = dot(nrm2[...], W[WOUT], 1, 0).astype(bf16)

    def attend_back():
        dv[...] = jnp.zeros_like(dv)
        tmp[...] = jnp.zeros_like(tmp)

        def one(h, carry):
            cols, inside = head_window(h)
            cols2 = pl.ds(pl.multiple_of(cols.start + half, 128), win)
            p = prob[h]
            da = only(inside, att[:, cols])
            dp = dot(da, v[:, cols], 1, 1)
            ds = (p * (dp - jnp.sum(dp * p, -1, keepdims=True))).astype(bf16)
            dv_h = dot(p.astype(bf16), da, 0, 0)
            dq_h = dot(ds, k[:, cols], 1, 0) * scale
            dk_h = dot(ds, q[:, cols], 0, 0) * scale
            dv[:, cols] = jnp.where(inside, dv_h, dv[:, cols].astype(f32)).astype(bf16)
            tmp[:, cols] = jnp.where(inside, dq_h, tmp[:, cols])
            tmp[:, cols2] = jnp.where(inside, dk_h, tmp[:, cols2])
            return carry

        lax.fori_loop(0, heads, one, 0, unroll=2)

    def unrotate():
        def body(s):
            dq[s, :] = rope(tmp[s, halves[0]], s, True).astype(bf16)
            dk[s, :] = rope(tmp[s, halves[1]], s, True).astype(bf16)

        by_rows(16, body)

    def grad_norm1():
        widen(S.at[0], [(dq, WQ), (dk, WK), (dv, WV)])

    def grad_in2():
        weight_grad(IN2, hid, dr0[:, mcols])

    def grad_token():
        for c in halves:
            S[1, :, c] = dot(dr0[:, mcols], W[IN2, c, :], 1, 1)

    def grad_pre():
        def body(s):
            t = tmp[s, :]
            sig = 1.0 / (1.0 + jnp.exp(-t))
            grad = (S[1, s, :] + X[1, s, :]) * (sig * (1.0 + t * (1.0 - sig)))
            nrm[s, :] = grad.astype(bf16)

        by_rows(16, body)

    def grad_values():
        total = dot(nrm[...], PK[0], 1, 0) + dot(dr0[...], PK[1], 1, 0)
        o_dval[...] = (total * keep_col[...]).T[0:patch, :]

    def grad_pack():
        @pl.when(m == 0)
        def _():
            for r in halves:
                GP[r, :] = dot(nrm[:, r], inx[...], 0, 0).astype(bf16)

        @pl.when(m == 1)
        def _():
            for r in halves:
                total = dot(dr0[:, r], inx[...], 0, 0)
                for i in range(2):
                    pick = (gain_lane == 2 * patch + 1 + i).astype(bf16)
                    total = total + dot(dgs[i, :, r], pick, 0, 0)
                GP[r, :] = total.astype(bf16)

    def write_in2():
        for i, c in enumerate(halves):
            in2_rows[:, c] = fin_in2[i]
        in2_copy.start()

    def write_small():
        tok_in = 2 * patch
        one, two = fin_pack[0].T, fin_pack[1].T
        o_in1[...] = one[0:tok_in]
        o_b1[...] = one[tok_in : tok_in + 1]
        o_res[...] = two[0:tok_in]
        o_b2[...] = two[tok_in : tok_in + 1]
        o_gattn[...] = two[tok_in + 1 : tok_in + 2]
        o_gmlp[...] = two[tok_in + 2 : tok_in + 3]

    barrier = pltpu.get_barrier_semaphore()
    for dev in (XN, YN, SIB):
        pl.semaphore_signal(barrier, inc=1, device_id=dev, device_id_type=MESH)
    each_other_plane(
        lambda zb: pl.semaphore_signal(barrier, inc=1, device_id=plane(zb), device_id_type=MESH)
    )
    order = ITEMS[1:]
    for w in order:
        own_copy(w).start()
    cot_copy = pltpu.make_async_copy(cot_hbm, cot, lsem.at[PACK])
    cot_copy.start()

    @pl.when(m == 0)
    def _():
        pack_block(PK.at[0, row_of(f)], w_in1, [b_in1])

    @pl.when(m == 1)
    def _():
        pack_block(PK.at[1, row_of(f)], w_res, [b_in2, g_attn, g_mlp])

    pl.semaphore_wait(barrier, 6)

    ag_own_z(PACK)
    ag_ready(WV)
    ag_own_xy(WV)
    ag_ready(WQ)
    ag_own_z(WQ)
    ag_own_xy(PACK)
    ag_ready(IN2)
    ag_own_z(IN2)
    ag_column(PACK, 1)
    ag_ready(WK)
    ag_own_xy(WK)
    ag_ready(XTRA)
    ag_own_z(XTRA)
    ag_column(WQ, 1)
    ag_own_xy(XTRA)
    ag_column(WQ, 2)
    ag_plane(PACK, 0)
    ag_column(PACK, 3)
    ag_column(WQ, 3)
    ag_first_y(XTRA)
    ag_column(IN2, 1)
    ag_plane(PACK, 3)
    ag_column(PACK, 2)
    ag_own_z(WK)
    ag_ready(WUP)
    ag_own_xy(WUP)
    ag_column(IN2, 3)
    ag_column(IN2, 2)
    ag_ready(WDOWN)
    ag_own_xy(WDOWN)
    ag_ready(WOUT)
    ag_own_z(WOUT)
    ag_own_xy(WOUT)
    ag_column(WK, 1)
    prepare()
    ag_plane(IN2, 1)
    ag_plane(PACK, 1)
    ag_plane(PACK, 2)
    ag_first_x(XTRA)
    ag_column(WK, 2)
    ag_plane(IN2, 3)
    ag_last(PACK)
    ag_column(WK, 3)
    ag_plane(WK, 0)
    ag_own_xy(IN2)
    ag_plane(IN2, 2)
    ag_own_xy(WQ)
    ag_plane(WQ, 2)
    ag_first_d(XTRA)
    ag_plane(WK, 2)
    ag_plane(WQ, 1)
    swap_start(0)
    ag_plane(WOUT, 0)
    ag_plane(IN2, 0)
    ag_column(WOUT, 1)
    ag_relay(XTRA, 0)
    ag_own_z(WV)
    ag_plane(WQ, 3)
    ag_plane(WK, 1)
    ag_plane(WK, 3)
    ag_relay(XTRA, 1)
    ag_own_z(WDOWN)
    ag_column(WV, 1)
    ag_column(WOUT, 2)
    ag_plane(WV, 1)
    ag_first_x(WUP)
    ag_first_y(WUP)
    ag_plane(WQ, 0)
    ag_column(WV, 3)
    ag_column(WV, 2)
    ag_own_z(WUP)
    ag_last(WK)
    ag_plane(WOUT, 2)
    swap_wait(0)
    token_hidden()
    ag_plane(WV, 0)
    ag_first_d(WUP)
    ag_plane(WOUT, 1)
    ag_last(IN2)
    token_out()
    swap_start(1)
    ag_last(XTRA)
    swap_wait(1)
    ag_last(WQ)
    ag_column(WOUT, 3)
    norm_first()
    ag_plane(WV, 3)
    ag_plane(WV, 2)
    project(WK, k)
    ag_column(WDOWN, 3)
    project(WQ, q)
    ag_plane(WOUT, 3)
    ag_relay(WUP, 0)
    ag_column(WDOWN, 2)
    ag_column(WDOWN, 1)
    ag_plane(WDOWN, 0)
    ag_last(WV)
    project_v()
    attend()
    ag_last(WOUT)
    attend_out()
    swap_start(2)
    ag_plane(WDOWN, 3)
    ag_plane(WDOWN, 2)
    ag_relay(WUP, 1)
    ag_plane(WDOWN, 1)
    swap_wait(2)
    norm_second()
    ag_last(WUP)
    feed_up()
    grad_down()
    rs_start(WDOWN, 0)
    rs_start(WDOWN, 1)
    ag_last(WDOWN)
    grad_hidden()
    feed_down()
    swap_start(3)
    grad_up()
    rs_first_far(WUP, 0)
    grad_norm2()
    swap_start(4)
    rs_start(WDOWN, 3)
    rs_turn(WDOWN, 0)
    rs_first_far(WUP, 1)
    rs_turn(WDOWN, 1)
    swap_wait(3)
    write_output()
    rs_first_near(WUP)
    rs_start(WDOWN, 2)
    swap_wait(4)
    norm_grad2()
    grad_out()
    grad_attended()
    rs_start(WOUT, 1)
    rs_start(WOUT, 0)
    attend_back()
    rs_start(WOUT, 3)
    weight_grad(WV, nrm, dv[...])
    rs_start(WV, 1)
    rs_start(WV, 2)
    unrotate()
    rs_relay(WUP, 0)
    weight_grad(WK, nrm, dk[...])
    rs_turn(WOUT, 1)
    rs_start(WV, 0)
    rs_start(WK, 1)
    grad_norm1()
    rs_relay(WUP, 1)
    swap_start(5)
    weight_grad(WQ, nrm, dq[...])
    rs_start(WK, 3)
    pre_act()
    rs_turn(WV, 0)
    rs_out(WDOWN, 3)
    rs_out(WOUT, 2)
    rs_start(WK, 0)
    swap_wait(5)
    norm_grad1()
    rs_turn(WV, 1)
    rs_start(WOUT, 2)
    rs_turn(WV, 2)
    grad_token()
    grad_in2()
    rs_first_far(XTRA, 0)
    rs_start(IN2, 2)
    rs_turn(WK, 1)
    swap_start(6)
    rs_start(IN2, 3)
    rs_start(WQ, 2)
    swap_wait(6)
    rs_out(WDOWN, 2)
    grad_pre()
    rs_out(WV, 3)
    rs_turn(WOUT, 2)
    rs_first_near(XTRA)
    rs_start(IN2, 1)
    rs_out(WV, 2)
    grad_pack()
    rs_first_far(XTRA, 1)
    rs_out(WV, 1)
    rs_turn(WDOWN, 2)
    rs_start(IN2, 0)
    rs_turn(IN2, 1)
    rs_turn(WK, 0)
    rs_turn(WK, 3)
    rs_start(WV, 3)
    rs_relay(XTRA, 0)
    rs_start(PACK, 3)
    rs_turn(IN2, 3)
    rs_out(WK, 3)
    rs_turn(IN2, 0)
    rs_start(PACK, 1)
    rs_start(PACK, 2)
    rs_start(PACK, 0)
    rs_out(WOUT, 1)
    rs_relay(XTRA, 1)
    rs_turn(WOUT, 0)
    rs_out(IN2, 2)
    rs_turn(IN2, 2)
    rs_turn(WOUT, 3)
    rs_out(WDOWN, 1)
    rs_turn(WV, 3)
    rs_zsum(XTRA, 0)
    rs_turn(PACK, 0)
    rs_turn(PACK, 2)
    rs_start(WQ, 1)
    rs_turn(PACK, 3)
    rs_out(IN2, 3)
    rs_turn(WDOWN, 3)
    rs_out(IN2, 1)
    rs_turn(PACK, 1)
    rs_start(WK, 2)
    rs_turn(WQ, 2)
    rs_zsum(XTRA, 3)
    rs_turn(WQ, 1)
    rs_start(WQ, 3)
    rs_out(WOUT, 3)
    rs_zsum(WUP, 3)
    rs_out(WV, 0)
    rs_out(WK, 2)
    rs_out(WOUT, 0)
    rs_turn(WK, 2)
    rs_out(IN2, 0)
    rs_out(PACK, 0)
    rs_out(WQ, 1)
    rs_out(PACK, 3)
    rs_start(WQ, 0)
    rs_final(IN2)
    rs_final(WV)
    rs_zsum(WUP, 0)
    rs_out(PACK, 2)
    rs_turn(WQ, 3)
    rs_out(PACK, 1)
    rs_final(WOUT)
    rs_turn(WQ, 0)
    swap_start(7)
    rs_out(WK, 0)
    rs_zsum(WUP, 1)
    rs_out(WQ, 2)
    rs_zsum(WUP, 2)
    rs_out(WDOWN, 0)
    rs_out(WK, 1)
    rs_first_turn(WUP)
    rs_zsum(XTRA, 1)
    rs_out(WQ, 3)
    rs_zsum(XTRA, 2)
    rs_first_turn(XTRA)
    rs_final(PACK)
    swap_start(8)
    rs_final(WK)
    rs_final(WDOWN)
    swap_wait(7)
    write_in2()
    rs_out(WQ, 0)
    rs_final(XTRA)
    grad_values()
    rs_final(WUP)
    rs_final(WQ)
    swap_wait(8)
    write_small()

    for w in ITEMS:
        if w not in (IN2, PACK):
            hand_out(w).wait()
    out_copy.wait()
    in2_copy.wait()

    def drain(ref, sem):
        remote(ref, ref, sem, sem, XN).wait_send()

    for w in ITEMS:
        drain(w_rows(w, pl.ds(0, (11 if w in PLANE_FIRST else 15) * blk)), ag_send.at[w])
        if w in PLANE_FIRST:

            @pl.when(inner)
            def _():
                drain(w_rows(w, pl.ds(0, 8 * blk)), ag_send.at[w])

        drain(recv[w].at[pl.ds(0, 15)], rs_send.at[w])


def pack_block(dst, matrix, vectors):
    tok_in, blk = matrix.shape
    parts = [matrix[...].astype(f32)] + [t[...].astype(f32) for t in vectors]
    parts.append(jnp.zeros((PL - tok_in - len(vectors), blk), f32))
    tall = jnp.concatenate(parts, 0)
    wide = jnp.concatenate([tall, jnp.zeros((PL, PL - blk), f32)], 1)
    dst[...] = wide.T[0:blk].astype(bf16)


def copy_kernel(count, *refs):
    sources, targets, held, sems = refs[:count], refs[count : 2 * count], refs[2 * count : -1], refs[-1]
    inward = [pltpu.make_async_copy(sources[i], held[i], sems.at[0, i]) for i in range(count)]
    outward = [pltpu.make_async_copy(held[i], targets[i], sems.at[1, i]) for i in range(count)]
    for c in inward:
        c.start()
    for a, b in zip(inward, outward):
        a.wait()
        b.start()
    for c in outward:
        c.wait()


def rotate(vectors, places):
    half_width = vectors.shape[-1] // 2
    frequency = 10000.0 ** (-2.0 * jnp.arange(half_width, dtype=jnp.float32) / vectors.shape[-1])
    angles = places[:, :, None, None] * frequency
    cosine = jnp.cos(angles)
    sine_val = jnp.sin(angles)
    first_half = vectors[..., :half_width]
    second_half = vectors[..., half_width:]
    return jnp.concatenate(
        [
            first_half * cosine - second_half * sine_val,
            second_half * cosine + first_half * sine_val,
        ],
        -1,
    )


def rms_norm(resid_rows, gain_vec):
    return (
        resid_rows
        * lax.rsqrt(jnp.mean(resid_rows * resid_rows, -1, keepdims=True) + 1e-06)
        * gain_vec
    )


def activate(up_rows):
    return jax.nn.gelu(up_rows, approximate=False)


def general_device(
    values,
    lengths,
    w_in1,
    b_in1,
    w_in2,
    b_in2,
    w_res,
    g_attn,
    w_qkv,
    w_out,
    g_mlp,
    w_up,
    w_down,
    cotangent,
):
    f32 = jnp.float32
    bf16 = jnp.bfloat16
    gathered = (
        lax.all_gather(w_in1, "fsdp", axis=1, tiled=True),
        lax.all_gather(b_in1, "fsdp", axis=0, tiled=True),
        lax.all_gather(w_in2, "fsdp", axis=0, tiled=True),
        lax.all_gather(b_in2, "fsdp", axis=0, tiled=True),
        lax.all_gather(w_res, "fsdp", axis=1, tiled=True),
        lax.all_gather(g_attn, "fsdp", axis=0, tiled=True),
        lax.all_gather(w_qkv, "fsdp", axis=0, tiled=True),
        lax.all_gather(w_out, "fsdp", axis=1, tiled=True),
        lax.all_gather(g_mlp, "fsdp", axis=0, tiled=True),
        lax.all_gather(w_up, "fsdp", axis=0, tiled=True),
        lax.all_gather(w_down, "fsdp", axis=1, tiled=True),
    )
    (
        full_in1,
        full_b1,
        full_in2,
        full_b2,
        full_res,
        full_gattn,
        full_qkv,
        full_out,
        full_gmlp,
        full_up,
        full_down,
    ) = gathered
    series = lengths.shape[0]
    seq_len = values.shape[0] // series
    patch_len = values.shape[1]
    slot_ids = jnp.arange(seq_len, dtype=jnp.int32)
    pad_count = seq_len - lengths
    padded = slot_ids[None, :] < pad_count[:, None]
    places = (slot_ids[None, :] - pad_count[:, None]).astype(f32)
    keep_mask = (1.0 - padded.astype(f32)).reshape(-1, 1)
    inputs = jnp.concatenate(
        [values.astype(f32) * keep_mask, jnp.broadcast_to(1.0 - keep_mask, values.shape)], 1
    ).astype(bf16)
    pre_act = jnp.dot(inputs, full_in1, preferred_element_type=f32) + full_b1.astype(f32)
    hidden = jax.nn.silu(pre_act).astype(bf16)
    resid0 = (
        jnp.dot(hidden, full_in2, preferred_element_type=f32)
        + full_b2.astype(f32)
        + jnp.dot(inputs, full_res, preferred_element_type=f32)
    )
    gain_attn = full_gattn.astype(f32)
    normed = rms_norm(resid0, gain_attn).astype(bf16)
    projected = jnp.einsum("td,dch->tch", normed, full_qkv, preferred_element_type=f32)
    local_heads = projected.shape[2] // HD
    head_shape = (series, seq_len, local_heads, HD)
    queries = rotate(projected[:, 0].reshape(head_shape), places).astype(bf16)
    key_rows = rotate(projected[:, 1].reshape(head_shape), places).astype(bf16)
    value_heads = projected[:, 2].reshape(head_shape).astype(bf16)
    causal = slot_ids[None, :] <= slot_ids[:, None]
    diagonal = slot_ids[None, :] == slot_ids[:, None]
    allowed = (causal[None] & (jnp.logical_not(padded)[:, None, :] | diagonal[None]))[:, None]
    scale = HD ** (-0.5)

    def score_block():
        raw = jnp.einsum("sqhe,skhe->shqk", queries, key_rows, preferred_element_type=f32) * scale
        return jnp.where(allowed, raw, -1e30)

    scores = score_block()
    row_max = jnp.max(scores, -1, keepdims=True)
    exponent = jnp.exp(scores - row_max)
    row_total = jnp.sum(exponent, -1, keepdims=True)
    log_total = row_max + jnp.log(row_total)
    attn_probs = (exponent / row_total).astype(bf16)
    attended = (
        jnp.einsum("shqk,skhe->sqhe", attn_probs, value_heads, preferred_element_type=f32)
        .reshape(-1, local_heads * HD)
        .astype(bf16)
    )
    branch_one = lax.psum(jnp.dot(attended, full_out, preferred_element_type=f32), "mp")
    resid1 = resid0 + branch_one
    gain_mlp = full_gmlp.astype(f32)
    normed2 = rms_norm(resid1, gain_mlp).astype(bf16)
    up_rows = jnp.dot(normed2, full_up, preferred_element_type=f32)
    mlp_hidden = activate(up_rows).astype(bf16)
    branch_two = lax.psum(
        jnp.dot(mlp_hidden, full_down, preferred_element_type=f32).astype(jnp.bfloat16), "mp"
    ).astype(jnp.float32)
    result = (resid1 + branch_two).astype(bf16)
    again = (
        lax.all_gather(w_in1, "fsdp", axis=1, tiled=True),
        lax.all_gather(b_in1, "fsdp", axis=0, tiled=True),
        lax.all_gather(w_in2, "fsdp", axis=0, tiled=True),
        lax.all_gather(b_in2, "fsdp", axis=0, tiled=True),
        lax.all_gather(w_res, "fsdp", axis=1, tiled=True),
        lax.all_gather(g_attn, "fsdp", axis=0, tiled=True),
        lax.all_gather(w_qkv, "fsdp", axis=0, tiled=True),
        lax.all_gather(w_out, "fsdp", axis=1, tiled=True),
        lax.all_gather(g_mlp, "fsdp", axis=0, tiled=True),
        lax.all_gather(w_up, "fsdp", axis=0, tiled=True),
        lax.all_gather(w_down, "fsdp", axis=1, tiled=True),
    )
    (
        back_in1,
        back_b1,
        back_in2,
        back_b2,
        back_res,
        back_gattn,
        back_qkv,
        back_out,
        back_gmlp,
        back_up,
        back_down,
    ) = again
    cot_rows = cotangent.astype(f32)
    grad_down = jnp.einsum("tf,td->fd", mlp_hidden, cotangent, preferred_element_type=f32)
    grad_hidden = jnp.einsum("td,fd->tf", cotangent, back_down, preferred_element_type=f32)
    unused_one, pull_mlp = jax.vjp(activate, up_rows)
    grad_up_rows = pull_mlp(grad_hidden)[0].astype(bf16)
    grad_up = jnp.einsum("td,tf->df", normed2, grad_up_rows, preferred_element_type=f32)
    norm_part2 = jnp.einsum("tf,df->td", grad_up_rows, back_up, preferred_element_type=f32)
    norm_grad2 = lax.psum(norm_part2, "mp")
    unused_two, pull_norm2 = jax.vjp(rms_norm, resid1, back_gmlp.astype(f32))
    resid_part1, grad_gmlp = pull_norm2(norm_grad2)
    resid1_grad = cot_rows + resid_part1
    out_grad = resid1_grad.astype(bf16)
    grad_out = jnp.einsum("th,td->hd", attended, out_grad, preferred_element_type=f32)
    attended_grad = (
        jnp.einsum("td,hd->th", out_grad, back_out, preferred_element_type=f32)
        .astype(bf16)
        .reshape(head_shape)
    )
    scores = score_block()
    probs_full = jnp.exp(scores - log_total)
    value_grad = jnp.einsum(
        "shqk,sqhe->skhe", probs_full.astype(bf16), attended_grad, preferred_element_type=f32
    )
    prob_grad = jnp.einsum(
        "sqhe,skhe->shqk", attended_grad, value_heads, preferred_element_type=f32
    )
    score_grad = (
        probs_full * (prob_grad - jnp.sum(prob_grad * probs_full, -1, keepdims=True))
    ).astype(bf16)
    query_grad = (
        jnp.einsum("shqk,skhe->sqhe", score_grad, key_rows, preferred_element_type=f32) * scale
    )
    key_grad = (
        jnp.einsum("shqk,sqhe->skhe", score_grad, queries, preferred_element_type=f32) * scale
    )
    width_local = local_heads * HD
    qkv_rows = jnp.stack(
        [
            rotate(query_grad, -places).reshape(-1, width_local),
            rotate(key_grad, -places).reshape(-1, width_local),
            value_grad.reshape(-1, width_local),
        ],
        1,
    ).astype(bf16)
    grad_qkv = jnp.einsum("td,tch->dch", normed, qkv_rows, preferred_element_type=f32)
    norm_part1 = jnp.einsum("tch,dch->td", qkv_rows, back_qkv, preferred_element_type=f32)
    norm_grad1 = lax.psum(norm_part1, "mp")
    unused_three, pull_norm1 = jax.vjp(rms_norm, resid0, back_gattn.astype(f32))
    resid_part0, grad_gattn = pull_norm1(norm_grad1)
    resid0_grad = (resid1_grad + resid_part0).astype(bf16)
    grad_in2 = jnp.einsum("th,td->hd", hidden, resid0_grad, preferred_element_type=f32)
    grad_b2 = jnp.sum(resid0_grad.astype(f32), 0)
    grad_res = jnp.einsum("tp,td->pd", inputs, resid0_grad, preferred_element_type=f32)
    hidden_grad = jnp.einsum("td,hd->th", resid0_grad, back_in2, preferred_element_type=f32)
    unused_four, pull_silu = jax.vjp(jax.nn.silu, pre_act)
    pre_grad = pull_silu(hidden_grad)[0].astype(bf16)
    grad_in1 = jnp.einsum("tp,th->ph", inputs, pre_grad, preferred_element_type=f32)
    grad_b1 = jnp.sum(pre_grad.astype(f32), 0)
    input_grad = jnp.einsum(
        "th,ph->tp", pre_grad, back_in1, preferred_element_type=f32
    ) + jnp.einsum("td,pd->tp", resid0_grad, back_res, preferred_element_type=f32)
    values_grad = input_grad[:, :patch_len] * keep_mask
    shares = tuple(
        (
            lax.psum_scatter(grad_in1, "fsdp", scatter_dimension=1, tiled=True),
            lax.psum_scatter(grad_b1, "fsdp", scatter_dimension=0, tiled=True),
            lax.psum_scatter(grad_in2, "fsdp", scatter_dimension=0, tiled=True),
            lax.psum_scatter(grad_b2, "fsdp", scatter_dimension=0, tiled=True),
            lax.psum_scatter(grad_res, "fsdp", scatter_dimension=1, tiled=True),
            lax.psum_scatter(grad_gattn, "fsdp", scatter_dimension=0, tiled=True),
            lax.psum_scatter(grad_qkv, "fsdp", scatter_dimension=0, tiled=True),
            lax.psum_scatter(grad_out, "fsdp", scatter_dimension=1, tiled=True),
            lax.psum_scatter(grad_gmlp, "fsdp", scatter_dimension=0, tiled=True),
            lax.psum_scatter(grad_up, "fsdp", scatter_dimension=0, tiled=True),
            lax.psum_scatter(grad_down, "fsdp", scatter_dimension=1, tiled=True),
        )
    )
    return (result, values_grad) + shares


def fused_device(
    values,
    lengths,
    w_in1,
    b_in1,
    w_in2,
    b_in2,
    w_res,
    g_attn,
    w_qkv,
    w_out,
    g_mlp,
    w_up,
    w_down,
    cotangent,
):
    rows, width = cotangent.shape
    half = w_out.shape[0]
    blk = w_in2.shape[0]
    patch = values.shape[1]
    tok_in = w_in1.shape[0]
    heads = half // HD
    vmem = pl.BlockSpec(memory_space=pltpu.VMEM)
    hbm = pl.BlockSpec(memory_space=pl.ANY)

    def shape(*dims, dtype=f32):
        return jax.ShapeDtypeStruct(dims, dtype)

    out_shape = (
        shape(rows, width, dtype=bf16),
        shape(patch, rows),
        shape(tok_in, blk),
        shape(1, blk),
        shape(blk, width),
        shape(1, blk),
        shape(tok_in, blk),
        shape(1, blk),
        shape(3, blk, half),
        shape(blk, half),
        shape(1, blk),
        shape(blk, half),
        shape(blk, half),
    )
    V = pltpu.VMEM
    scratch = [
        V((NW, width, half), bf16),
        V((2, width, PL), bf16),
        V((NW, width, half), bf16),
        V((width, PL), bf16),
        {
            w: V((Z_SLOTS if w in Z_FIRST else SLOTS, blk, cols_of(w, half)[1] - cols_of(w, half)[0]), bf16)
            for w in ITEMS
        },
        V((2, rows, half), f32),
        V((rows, width), f32),
        V((2, rows, width), f32),
        V((2, rows, width), f32),
        V((rows, width), bf16),
        V((rows, width), bf16),
        V((rows, width), bf16),
        V((rows, width), bf16),
        V((rows, width), bf16),
        V((rows, half), bf16),
        V((rows, half), bf16),
        V((rows, half), bf16),
        V((heads, rows, rows), f32),
        V((rows, half), bf16),
        V((rows, half), f32),
        V((rows, half), bf16),
        V((rows, width), bf16),
        V((rows, half), bf16),
        V((rows, half), bf16),
        V((rows, half), bf16),
        V((rows, half), bf16),
        V((rows, width), f32),
        V((rows, width), bf16),
        V((rows, half), f32),
        V((rows, half), f32),
        V((rows, rows), f32),
        V((rows, PL), bf16),
        V((2, 8, width), f32),
        V((2, 16, width), bf16),
        V((8, width), f32),
        V((rows, PL), f32),
        V((NW - 1, blk, half), f32),
        V((2, blk, half), f32),
        V((2, blk, PL), f32),
        V((rows, width), bf16),
        V((blk, width), f32),
        pltpu.SemaphoreType.DMA((9,)),
        pltpu.SemaphoreType.DMA((9, 16)),
        pltpu.SemaphoreType.DMA((9,)),
        pltpu.SemaphoreType.DMA((9, Z_SLOTS)),
        pltpu.SemaphoreType.DMA((9,)),
        pltpu.SemaphoreType.DMA((9,)),
        pltpu.SemaphoreType.DMA((9,)),
        pltpu.SemaphoreType.DMA((9,)),
    ]
    results = pl.pallas_call(
        layer_kernel,
        name="layer",
        out_shape=out_shape,
        in_specs=[pl.BlockSpec(memory_space=pltpu.SMEM)] + [vmem] * 7 + [hbm] * 6,
        out_specs=(hbm,) + (vmem,) * 3 + (hbm,) + (vmem,) * 3 + (hbm,) * 2 + (vmem,) + (hbm,) * 2,
        scratch_shapes=scratch,
        compiler_params=pltpu.CompilerParams(
            collective_id=0, has_side_effects=True, vmem_limit_bytes=VMEM_BYTES
        ),
    )(
        lengths,
        values.T,
        w_in1,
        w_res,
        b_in1[None],
        b_in2[None],
        g_attn[None],
        g_mlp[None],
        w_in2,
        jnp.transpose(w_qkv, (1, 0, 2)),
        w_out.T,
        w_up,
        w_down.T,
        cotangent,
    )
    (
        out,
        d_values,
        d_in1,
        d_b1,
        d_in2,
        d_b2,
        d_res,
        d_gattn,
        d_qkv,
        d_out,
        d_gmlp,
        d_up,
        d_down,
    ) = pl.pallas_call(
        functools.partial(copy_kernel, len(out_shape)),
        name="hand_over",
        out_shape=out_shape,
        in_specs=[hbm] * len(out_shape),
        out_specs=(hbm,) * len(out_shape),
        scratch_shapes=[V(s.shape, s.dtype) for s in out_shape]
        + [pltpu.SemaphoreType.DMA((2, len(out_shape)))],
    )(*results)
    return (
        out,
        d_values.T,
        d_in1,
        d_b1[0],
        d_in2,
        d_b2[0],
        d_res,
        d_gattn[0],
        jnp.transpose(d_qkv, (1, 0, 2)),
        d_out.T,
        d_gmlp[0],
        d_up,
        d_down.T,
    )


def on_device(*args):
    blk, width = args[4].shape
    half = args[9].shape[0]
    shards = width // blk
    series = args[1].shape[0]
    fits = (
        shards == 16
        and 2 * half == width
        and blk % 16 == 0
        and half % 128 == 0
        and args[0].shape[0] % 64 == 0
        and series <= 8
    )
    return (fused_device if fits else general_device)(*args)


def solution(mesh):
    in_specs = (
        P("fsdp", None),
        P("fsdp"),
        P(None, "fsdp"),
        P("fsdp"),
        P("fsdp", None),
        P("fsdp"),
        P(None, "fsdp"),
        P("fsdp"),
        P("fsdp", None, "mp"),
        P("mp", "fsdp"),
        P("fsdp"),
        P("fsdp", "mp"),
        P("mp", "fsdp"),
        P("fsdp", None),
    )
    out_specs = (
        P("fsdp", None),
        P("fsdp", None),
        P(None, "fsdp"),
        P("fsdp"),
        P("fsdp", None),
        P("fsdp"),
        P(None, "fsdp"),
        P("fsdp"),
        P("fsdp", None, "mp"),
        P("mp", "fsdp"),
        P("fsdp"),
        P("fsdp", "mp"),
        P("mp", "fsdp"),
    )
    return jax.shard_map(
        on_device, mesh=mesh, in_specs=in_specs, out_specs=out_specs, check_vma=False
    )
```

```python
import functools
import math

import jax
import jax.numpy as jnp
from jax import lax
from jax.experimental import pallas as pl
from jax.experimental.pallas import tpu as pltpu
from jax.sharding import PartitionSpec as P

HD = 80
MESH = pl.DeviceIdType.MESH
VMEM_BYTES = 63 * 2**20
f32 = jnp.float32
bf16 = jnp.bfloat16

IN2, WQ, WK, WV, WOUT, WUP, WDOWN, PACK, XTRA = range(9)
NW = 7
PL = 128
SPLIT, CUT = WQ, 384
ITEMS = (PACK, IN2, WQ, WK, WV, WOUT, WUP, WDOWN) + (() if SPLIT is None else (XTRA,))
PLANE_FIRST = (WUP, XTRA)
Z_FIRST = (WUP, XTRA)


def cols_of(w, half):
    if SPLIT is None or w not in (SPLIT, XTRA):
        return 0, PL if w == PACK else half
    return (0, CUT) if w == SPLIT else (CUT, half)


SLOT_A, SLOT_X, SLOT_Y, SLOT_V, SLOTS = 0, 4, 8, 12, 16
Z_RELAY, Z_NEAR, Z_FAR, Z_A, Z_X, Z_Y, Z_SLOTS = 0, 8, 12, 16, 17, 18, 19


def dot(left, right, left_dim, right_dim):
    return lax.dot_general(
        left, right, (((left_dim,), (right_dim,)), ((), ())), preferred_element_type=f32
    )


def layer_kernel(
    small_hbm,
    in2,
    qkv,
    out_t,
    up,
    down_t,
    cot_hbm,
    o_out,
    o_dval,
    o_in1,
    o_b1,
    o_in2,
    o_b2,
    o_res,
    o_gattn,
    o_qkv,
    o_wout,
    o_gmlp,
    o_up,
    o_down,
    small,
    W,
    PK,
    G,
    GP,
    recv,
    R0,
    R1,
    S,
    X,
    SB,
    XB,
    hid,
    nrm,
    nrm2,
    q,
    k,
    v,
    prob,
    att,
    gprime,
    mlp,
    cot,
    dup,
    dq,
    dk,
    dv,
    tmp,
    dr0,
    rope_c,
    rope_s,
    bias,
    inx,
    gains,
    dgs,
    accg,
    keep_col,
    fin,
    fin_in2,
    fin_pack,
    out_rows,
    in2_rows,
    ag_send,
    ag_recv,
    rs_send,
    rs_recv,
    ex_send,
    ex_recv,
    lsem,
    out_sem,
    small_sem,
):
    lengths, values_t, w_in1, w_res, b_in1, b_in2, g_attn, g_mlp = small
    rows, width = cot.shape
    half = W.shape[2]
    blk = in2.shape[0]
    series = lengths.shape[0]
    seq = rows // series
    heads = half // HD
    patch = values_t.shape[0]

    f = lax.axis_index("fsdp")
    m = lax.axis_index("mp")
    x = lax.rem(f, 2)
    y = lax.rem(lax.div(f, 2), 2)
    z = lax.div(f, 4)
    c0 = f - 4 * z
    cx = c0 + 1 - 2 * x
    cy = c0 + 2 - 4 * y
    cd = 3 - c0
    XN, YN, SIB = (4 * z + cx, m), (4 * z + cy, m), (f, 1 - m)
    z_high = (z >= 2).astype(jnp.int32)
    inner = jnp.logical_and(z > 0, z < 3)
    z_inner = inner.astype(jnp.int32)
    z_near = z + 1 - 2 * lax.rem(z, 2)
    z_far = 2 - z_high
    z_even = lax.rem(z, 2) == 0
    z_odd = jnp.logical_not(z_even)

    def plane(zb):
        return (4 * zb + c0, m)

    def near(i):
        swap = (i == 0).astype(jnp.int32) - (i == 1).astype(jnp.int32)
        low = i + z_inner * swap
        return low + z_high * (3 - 2 * low)

    def each_plane(order, body, start=0):
        def step(i, carry):
            body(order(i))
            return carry

        lax.fori_loop(start, 4, step, 0)

    def each_other_plane(body):
        each_plane(near, body, 1)

    nearest = [near(jnp.int32(i)) for i in range(4)]

    def row_of(b):
        return pl.ds(pl.multiple_of(b * blk, 16), blk)

    def whole(w):
        return SPLIT if w == XTRA else w

    def part(ref, w, *index):
        low, high = cols_of(w, half)
        return ref.at[(*index, slice(low, high))]

    def w_rows(w, r):
        return PK.at[m, r] if w == PACK else part(W, w, whole(w), r)

    def w_block(w, b):
        return w_rows(w, row_of(b))

    def g_block(w, b):
        return GP.at[row_of(b)] if w == PACK else part(G, w, whole(w), row_of(b))

    def r_block(w, s):
        return recv[w].at[s]

    def remote(src, dst, send, recv, dev):
        return pltpu.make_async_remote_copy(
            src_ref=src, dst_ref=dst, send_sem=send, recv_sem=recv, device_id=dev, device_id_type=MESH
        )

    def ag_push(w, b, *devs):
        ref = w_block(w, b)
        for dev in devs:
            remote(ref, ref, ag_send.at[w], ag_recv.at[w, b], dev).start()

    def ag_await(w, b):
        ref = w_block(w, b)
        remote(ref, ref, ag_send.at[w], ag_recv.at[w, b], XN).wait_recv()

    mcols = pl.ds(pl.multiple_of(m * half, 128), half)

    def own_copy(w):
        if w == IN2:
            src = in2.at[:, mcols]
        elif whole(w) in (WQ, WK, WV):
            src = part(qkv, w, whole(w) - WQ, slice(None))
        else:
            src = part({WOUT: out_t, WUP: up, WDOWN: down_t}[whole(w)], w, slice(None))
        return pltpu.make_async_copy(src, w_block(w, f), lsem.at[w])

    def ag_ready(w):
        own_copy(w).wait()

    def ag_own_xy(w):
        ag_push(w, f, XN, YN)

    def ag_own_z(w):
        if w in PLANE_FIRST:
            ag_push(w, f, plane(z_near), plane(z_far))
        else:
            each_other_plane(lambda zb: ag_push(w, f, plane(zb)))

    def ag_column(w, i):
        b = 4 * nearest[i] + c0
        ag_await(w, b)
        ag_push(w, b, XN, YN)

    def ag_from_x(w, zb, even):
        ag_await(w, 4 * zb + cx)

        @pl.when(even)
        def _():
            ag_push(w, 4 * zb + cx, YN)

    def ag_from_y(w, zb, even):
        ag_await(w, 4 * zb + cy)

        @pl.when(jnp.logical_not(even))
        def _():
            ag_push(w, 4 * zb + cy, XN)

    def ag_plane(w, i):
        even = lax.rem(nearest[i], 2) == 0
        ag_from_x(w, nearest[i], even)
        ag_from_y(w, nearest[i], even)

    def turns_y(w):
        return z_odd if w in (XTRA, PACK) else z_even

    def ag_first_x(w):
        ag_from_x(w, z, turns_y(w))
        ag_push(w, 4 * z + cx, plane(z_near), plane(z_far))

    def ag_first_y(w):
        ag_from_y(w, z, turns_y(w))
        ag_push(w, 4 * z + cy, plane(z_near), plane(z_far))

    def ag_first_d(w):
        ag_await(w, 4 * z + cd)
        ag_push(w, 4 * z + cd, plane(z_near), plane(z_far))

    def ag_relay(w, i):
        @pl.when(inner)
        def _():
            zb = (3 - z, 3 * (1 - z_high))[i]
            for c in (c0, cx, cy, cd):
                ag_await(w, 4 * zb + c)
                ag_push(w, 4 * zb + c, plane(3 * z_high))

    def ag_last(w):
        if w in PLANE_FIRST:
            for c in (c0, cx, cy, cd):
                ag_await(w, 4 * z_near + c)

            @pl.when(jnp.logical_not(inner))
            def _():
                for zb in (z_far, 3 - z):
                    for c in (c0, cx, cy, cd):
                        ag_await(w, 4 * zb + c)
        else:
            each_plane(near, lambda zb: ag_await(w, 4 * zb + cd))

    def final_of(w):
        if w == PACK:
            return fin_pack.at[m]
        if w == IN2:
            return fin_in2.at[m]
        return part(fin, w, whole(w) - WQ, slice(None))

    targets = [o_qkv.at[0], o_qkv.at[1], o_qkv.at[2], o_wout, o_up, o_down]

    def hand_out(w):
        target = part(targets[whole(w) - WQ], w, slice(None))
        return pltpu.make_async_copy(final_of(w), target, out_sem.at[w])

    def rs_push(w, src, slot, dev):
        remote(src, r_block(w, slot), rs_send.at[w], rs_recv.at[w, slot], dev).start()

    def rs_await(w, slot):
        ref = r_block(w, slot)
        remote(ref, ref, rs_send.at[w], rs_recv.at[w, slot], XN).wait_recv()

    def add_to(ref, other):
        ref[...] = (ref[...].astype(f32) + other[...].astype(f32)).astype(bf16)

    def sum3(a, b, c):
        return a[...].astype(f32) + b[...].astype(f32) + c[...].astype(f32)

    def rs_start(w, i):
        zb = nearest[3 - i]
        even = lax.rem(zb, 2) == 0

        @pl.when(even)
        def _():
            rs_push(w, g_block(w, 4 * zb + cd), SLOT_A + zb, YN)
            rs_push(w, g_block(w, 4 * zb + cy), SLOT_Y + zb, YN)

        @pl.when(jnp.logical_not(even))
        def _():
            rs_push(w, g_block(w, 4 * zb + cd), SLOT_A + zb, XN)
            rs_push(w, g_block(w, 4 * zb + cx), SLOT_X + zb, XN)

    def turn(w, slot_a, even, own_x, own_y, slot_x, slot_y):
        rs_await(w, slot_a)
        ref = r_block(w, slot_a)

        @pl.when(even)
        def _():
            add_to(ref, own_x)
            rs_push(w, ref, slot_x, XN)

        @pl.when(jnp.logical_not(even))
        def _():
            add_to(ref, own_y)
            rs_push(w, ref, slot_y, YN)

    def rs_turn(w, i):
        zb = nearest[3 - i]
        own_x, own_y = g_block(w, 4 * zb + cx), g_block(w, 4 * zb + cy)
        turn(w, SLOT_A + zb, lax.rem(zb, 2) == 0, own_x, own_y, SLOT_X + zb, SLOT_Y + zb)

    def rs_out(w, i):
        zb = nearest[i]
        rs_await(w, SLOT_X + zb)
        rs_await(w, SLOT_Y + zb)
        ref = r_block(w, SLOT_X + zb)
        total = sum3(g_block(w, 4 * zb + c0), ref, r_block(w, SLOT_Y + zb))
        if i == 0:
            final_of(w)[...] = total
        else:
            ref[...] = total.astype(bf16)
            rs_push(w, ref, SLOT_V + z, plane(zb))

    def rs_first_far(w, i):
        @pl.when(jnp.logical_not(inner))
        def _():
            zb = (3 - z, z_far)[i]
            for c in (cd, cx, cy, c0):
                slot = Z_RELAY + 4 * lax.rem(zb, 2) + c
                rs_push(w, g_block(w, 4 * zb + c), slot, plane(1 + z_high))

    def rs_first_near(w):
        for c in (cd, cx, cy, c0):
            rs_push(w, g_block(w, 4 * z_near + c), Z_NEAR + c, plane(z_near))

    def rs_relay(w, i):
        @pl.when(inner)
        def _():
            zb = (3 * (1 - z_high), z_far)[i]
            for c in (cd, cx, cy, c0):
                slot = Z_RELAY + 4 * lax.rem(zb, 2) + c
                rs_await(w, slot)
                ref = r_block(w, slot)
                add_to(ref, g_block(w, 4 * zb + c))
                rs_push(w, ref, Z_FAR + c, plane(zb))

    def rs_zsum(w, i):
        c = (cd, cx, cy, c0)[i]
        rs_await(w, Z_NEAR + c)
        rs_await(w, Z_FAR + c)
        ref = r_block(w, Z_NEAR + c)
        total = sum3(ref, r_block(w, Z_FAR + c), g_block(w, 4 * z + c))
        if i == 3:
            final_of(w)[...] = total
            return
        ref[...] = total.astype(bf16)
        if i in (0, 2):

            @pl.when(z_odd)
            def _():
                rs_push(w, ref, Z_A if i == 0 else Z_Y, YN)

        if i in (0, 1):

            @pl.when(z_even)
            def _():
                rs_push(w, ref, Z_A if i == 0 else Z_X, XN)

    def rs_first_turn(w):
        turn(w, Z_A, z_odd, r_block(w, Z_NEAR + cx), r_block(w, Z_NEAR + cy), Z_X, Z_Y)

    def rs_final(w):
        final = final_of(w)
        if w in Z_FIRST:
            rs_await(w, Z_X)
            rs_await(w, Z_Y)
            final[...] = sum3(final, r_block(w, Z_X), r_block(w, Z_Y))
        else:
            for i in (1, 2, 3):
                rs_await(w, SLOT_V + nearest[i])
            parts = [r_block(w, SLOT_V + nearest[i])[...].astype(f32) for i in (1, 2, 3)]
            final[...] = final[...] + (parts[0] + parts[1] + parts[2])
        if w not in (IN2, PACK):
            hand_out(w).start()

    def exchange(i):
        src, dst = {
            0: lambda: (PK.at[m], PK.at[m]),
            1: lambda: (R0.at[m], R0.at[m]),
            2: lambda: (S.at[0], X.at[0]),
            3: lambda: (SB, XB),
            4: lambda: (S.at[1], X.at[1]),
            5: lambda: (S.at[0], X.at[0]),
            6: lambda: (S.at[1], X.at[1]),
            7: lambda: (fin_in2.at[m], fin_in2.at[m]),
            8: lambda: (fin_pack.at[m], fin_pack.at[m]),
        }[i]()
        return remote(src, dst, ex_send.at[i], ex_recv.at[i], SIB)

    def swap_start(i):
        exchange(i).start()

    def swap_wait(i):
        exchange(i).wait()

    def by_rows(step, body, unroll=4):
        def one(i, carry):
            body(pl.ds(pl.multiple_of(i * step, step), step))
            return carry

        lax.fori_loop(0, rows // step, one, 0, unroll=unroll)

    halves = (slice(0, half), slice(half, width))

    def pad_of(slot):
        lens = [lengths[s] for s in range(series)]
        total = jnp.zeros(slot.shape, jnp.int32)
        for s in range(series):
            inside = jnp.logical_and(slot >= s * seq, slot < (s + 1) * seq)
            total = jnp.where(inside, (s + 1) * seq - lens[s], total)
        return total

    def series_of(slot):
        total = jnp.zeros(slot.shape, jnp.int32)
        for s in range(1, series):
            total = total + (slot >= s * seq).astype(jnp.int32)
        return total

    lane = lax.broadcasted_iota(jnp.int32, (1, half), 1).astype(f32)
    in_head = lane - HD * jnp.floor((lane + 0.5) / HD)
    first = in_head < HD // 2

    small_copies = [
        pltpu.make_async_copy(src, dst, small_sem.at[i]) for i, (src, dst) in enumerate(zip(small_hbm, small))
    ]

    def prepare():
        for c in small_copies[:2]:
            c.wait()
        slot_col = lax.broadcasted_iota(jnp.int32, (rows, 1), 0)
        keep = jnp.broadcast_to((slot_col >= pad_of(slot_col)).astype(f32), keep_col.shape)
        keep_col[...] = keep
        lane_i = lax.broadcasted_iota(jnp.int32, (rows, PL), 1)
        tall = jnp.concatenate([values_t[...].astype(f32), jnp.zeros((PL - patch, rows), f32)], 0)
        inx[...] = jnp.where(
            lane_i < patch,
            tall.T * keep,
            jnp.where(lane_i < 2 * patch, 1.0 - keep, (lane_i == 2 * patch).astype(f32)),
        ).astype(bf16)

        key_slot = lax.broadcasted_iota(jnp.int32, (1, rows), 1)
        key_ok = (key_slot >= pad_of(key_slot)).astype(jnp.int32)
        key_series = series_of(key_slot)

        def bias_rows(s):
            shape = (s.size, rows)
            a = lax.broadcasted_iota(jnp.int32, shape, 0) + s.start
            b = jnp.broadcast_to(key_slot, shape)
            same = series_of(a) == jnp.broadcast_to(key_series, shape)
            ok = jnp.logical_or(jnp.broadcast_to(key_ok, shape) == 1, a == b)
            allowed = jnp.logical_and(jnp.logical_and(same, b <= a), ok)
            bias[s, :] = jnp.where(allowed, 0.0, -1e30)

        by_rows(32, bias_rows, 1)
        turn_i = jnp.where(first, in_head, in_head - HD // 2)
        frequency = jnp.exp(turn_i * (-2.0 * math.log(10000.0) / HD))

        def rope_rows(s):
            slot = lax.broadcasted_iota(jnp.int32, (s.size, 1), 0) + s.start
            place = (slot - pad_of(slot)).astype(f32)
            angle = place * frequency
            rope_c[s, :] = jnp.cos(angle)
            sine = jnp.sin(angle)
            rope_s[s, :] = jnp.where(first, -sine, sine)

        by_rows(16, rope_rows, 1)

    def rope(t, s, inverse):
        other = jnp.where(first, pltpu.roll(t, half - HD // 2, 1), pltpu.roll(t, HD // 2, 1))
        turned = other * rope_s[s, :]
        return t * rope_c[s, :] - turned if inverse else t * rope_c[s, :] + turned

    gain_lane = lax.broadcasted_iota(jnp.int32, (16, PL), 1)

    def pre_act():
        for cols in halves:
            tmp[:, cols] = dot(inx[...], PK[0, cols, :], 1, 1)

    def token_hidden():
        for i in range(2):
            pick = (gain_lane == 2 * patch + 1 + i).astype(bf16)
            gains[i] = dot(pick, PK[1], 1, 1)[0:8]
        pre_act()

        def silu_rows(s):
            t = tmp[s, :]
            hid[s, :] = (t / (1.0 + jnp.exp(-t))).astype(bf16)

        by_rows(16, silu_rows)

    def token_out():
        R0[m] = dot(hid[...], W[IN2], 1, 0) + dot(inx[...], PK[1, mcols, :], 1, 1)

    def norm_rows(load, gain, out):
        def body(s):
            a, b = load(s)
            mean = (jnp.sum(a * a, -1, keepdims=True) + jnp.sum(b * b, -1, keepdims=True)) / width
            scale = lax.rsqrt(mean + 1e-06)
            out[s, halves[0]] = (a * scale * gain[0:1, halves[0]]).astype(bf16)
            out[s, halves[1]] = (b * scale * gain[0:1, halves[1]]).astype(bf16)

        by_rows(16, body)

    def norm_first():
        norm_rows(lambda s: (R0[0, s, :], R0[1, s, :]), gains.at[0], nrm)

    def project(w, out):
        tmp[:, halves[0]] = dot(nrm[...], W[w], 1, 0)

        def body(s):
            out[s, :] = rope(tmp[s, halves[0]], s, False).astype(bf16)

        by_rows(16, body)

    def project_v():
        v[...] = dot(nrm[...], W[WV], 1, 0).astype(bf16)

    win = 256
    scale = HD ** (-0.5)
    win_lane = lax.broadcasted_iota(jnp.int32, (1, win), 1)

    def head_window(h):
        low = jnp.minimum(lax.div(h * HD, 128) * 128, half - win)
        inside = jnp.logical_and(win_lane >= h * HD - low, win_lane < h * HD - low + HD)
        return pl.ds(pl.multiple_of(low, 128), win), inside

    def only(inside, t):
        return jnp.where(inside, t.astype(f32), 0.0).astype(bf16)

    def attend():
        att[...] = jnp.zeros_like(att)

        def one(h, carry):
            cols, inside = head_window(h)
            score = dot(only(inside, q[:, cols]), k[:, cols], 1, 1) * scale + bias[...]
            exponent = jnp.exp(score - jnp.max(score, -1, keepdims=True))
            p = exponent / jnp.sum(exponent, -1, keepdims=True)
            prob[h] = p
            mixed = dot(p.astype(bf16), v[:, cols], 1, 0)
            att[:, cols] = jnp.where(inside, mixed, att[:, cols].astype(f32)).astype(bf16)
            return carry

        lax.fori_loop(0, heads, one, 0, unroll=2)

    def widen(dst, terms):
        for cols in halves:
            total = None
            for left, w in terms:
                part = dot(left[...], W[w, cols, :], 1, 1)
                total = part if total is None else total + part
            dst[:, cols] = total.astype(dst.dtype)

    def attend_out():
        widen(S.at[0], [(att, WOUT)])

    def norm_second():
        def body(s):
            for i, cols in enumerate(halves):
                R1[s, cols] = R0[i, s, :] + (S[0, s, cols] + X[0, s, cols])

        by_rows(16, body)
        norm_rows(lambda s: (R1[s, halves[0]], R1[s, halves[1]]), gains.at[1], nrm2)

    def feed_up():
        tmp[:, halves[0]] = dot(nrm2[...], W[WUP], 1, 0)

        def gelu_rows(s):
            t = tmp[s, halves[0]]
            phi = 0.5 * (1.0 + lax.erf(t * (2.0**-0.5)))
            mlp[s, :] = (t * phi).astype(bf16)
            gprime[s, :] = phi + t * jnp.exp(-0.5 * t * t) * ((2.0 * math.pi) ** -0.5)

        by_rows(16, gelu_rows)

    def weight_grad(w, left, right):
        for r in halves:
            G[w, r, :] = dot(left[:, r], right, 0, 0).astype(bf16)

    def grad_down():
        cot_copy.wait()
        weight_grad(WDOWN, cot, mlp[...])

    def grad_hidden():
        tmp[:, halves[0]] = dot(cot[...], W[WDOWN], 1, 0)

        def dup_rows(s):
            dup[s, :] = (tmp[s, halves[0]] * gprime[s, :]).astype(bf16)

        by_rows(16, dup_rows)

    def grad_up():
        weight_grad(WUP, nrm2, dup[...])

    def feed_down():
        widen(SB, [(mlp, WDOWN)])

    def grad_norm2():
        widen(S.at[1], [(dup, WUP)])

    out_copy = pltpu.make_async_copy(out_rows, o_out, out_sem.at[PACK])
    in2_copy = pltpu.make_async_copy(in2_rows, o_in2, out_sem.at[IN2])

    def write_output():
        def body(s):
            out_rows[s, :] = (R1[s, :] + (SB[s, :].astype(f32) + XB[s, :].astype(f32))).astype(bf16)

        by_rows(16, body)
        out_copy.start()

    def norm_grad(load, i_part, gain, base, out, keep_sum):
        def body(i, carry):
            s = pl.ds(pl.multiple_of(i * 16, 16), 16)
            xs = load(s)
            mean = sum(jnp.sum(t * t, -1, keepdims=True) for t in xs) / width
            r = lax.rsqrt(mean + 1e-06)
            n1 = [t * r for t in xs]
            dn = [S[i_part, s, c] + X[i_part, s, c] for c in halves]
            gd = [gain[0:1, c] * t for c, t in zip(halves, dn)]
            along = sum(jnp.sum(a * b, -1, keepdims=True) for a, b in zip(gd, n1)) / width
            for c, a, b in zip(halves, gd, n1):
                out(s, c, base(s, c) + r * (a - b * along))
            for c, a, b in zip(halves, dn, n1):
                prod = a * b
                accg[:, c] += prod[0:8] + prod[8:16]
            return carry

        accg[...] = jnp.zeros_like(accg)
        lax.fori_loop(0, rows // 16, body, 0, unroll=4)
        total = accg[...]
        high = total.astype(bf16)
        keep_sum[...] = jnp.concatenate([high.astype(f32), total - high.astype(f32)], 0).astype(bf16)

    def norm_grad2():
        def out(s, c, t):
            R1[s, c] = t
            nrm2[s, c] = t.astype(bf16)

        norm_grad(
            lambda s: [R1[s, c] for c in halves],
            1,
            gains.at[1],
            lambda s, c: cot[s, c].astype(f32),
            out,
            dgs.at[1],
        )

    def norm_grad1():
        def out(s, c, t):
            dr0[s, c] = t.astype(bf16)

        norm_grad(
            lambda s: [R0[i, s, :] for i in range(2)],
            0,
            gains.at[0],
            lambda s, c: R1[s, c],
            out,
            dgs.at[0],
        )

    def grad_out():
        weight_grad(WOUT, nrm2, att[...])

    def grad_attended():
        att[...] = dot(nrm2[...], W[WOUT], 1, 0).astype(bf16)

    def attend_back():
        dv[...] = jnp.zeros_like(dv)
        tmp[...] = jnp.zeros_like(tmp)

        def one(h, carry):
            cols, inside = head_window(h)
            cols2 = pl.ds(pl.multiple_of(cols.start + half, 128), win)
            p = prob[h]
            da = only(inside, att[:, cols])
            dp = dot(da, v[:, cols], 1, 1)
            ds = (p * (dp - jnp.sum(dp * p, -1, keepdims=True))).astype(bf16)
            dv_h = dot(p.astype(bf16), da, 0, 0)
            dq_h = dot(ds, k[:, cols], 1, 0) * scale
            dk_h = dot(ds, q[:, cols], 0, 0) * scale
            dv[:, cols] = jnp.where(inside, dv_h, dv[:, cols].astype(f32)).astype(bf16)
            tmp[:, cols] = jnp.where(inside, dq_h, tmp[:, cols])
            tmp[:, cols2] = jnp.where(inside, dk_h, tmp[:, cols2])
            return carry

        lax.fori_loop(0, heads, one, 0, unroll=2)

    def unrotate():
        def body(s):
            dq[s, :] = rope(tmp[s, halves[0]], s, True).astype(bf16)
            dk[s, :] = rope(tmp[s, halves[1]], s, True).astype(bf16)

        by_rows(16, body)

    def grad_norm1():
        widen(S.at[0], [(dq, WQ), (dk, WK), (dv, WV)])

    def grad_in2():
        weight_grad(IN2, hid, dr0[:, mcols])

    def grad_token():
        for c in halves:
            S[1, :, c] = dot(dr0[:, mcols], W[IN2, c, :], 1, 1)

    def grad_pre():
        def body(s):
            t = tmp[s, :]
            sig = 1.0 / (1.0 + jnp.exp(-t))
            grad = (S[1, s, :] + X[1, s, :]) * (sig * (1.0 + t * (1.0 - sig)))
            nrm[s, :] = grad.astype(bf16)

        by_rows(16, body)

    def grad_values():
        total = dot(nrm[...], PK[0], 1, 0) + dot(dr0[...], PK[1], 1, 0)
        o_dval[...] = (total * keep_col[...]).T[0:patch, :]

    def grad_pack():
        @pl.when(m == 0)
        def _():
            for r in halves:
                GP[r, :] = dot(nrm[:, r], inx[...], 0, 0).astype(bf16)

        @pl.when(m == 1)
        def _():
            for r in halves:
                total = dot(dr0[:, r], inx[...], 0, 0)
                for i in range(2):
                    pick = (gain_lane == 2 * patch + 1 + i).astype(bf16)
                    total = total + dot(dgs[i, :, r], pick, 0, 0)
                GP[r, :] = total.astype(bf16)

    def write_in2():
        for i, c in enumerate(halves):
            in2_rows[:, c] = fin_in2[i]
        in2_copy.start()

    def write_small():
        tok_in = 2 * patch
        one, two = fin_pack[0].T, fin_pack[1].T
        o_in1[...] = one[0:tok_in]
        o_b1[...] = one[tok_in : tok_in + 1]
        o_res[...] = two[0:tok_in]
        o_b2[...] = two[tok_in : tok_in + 1]
        o_gattn[...] = two[tok_in + 1 : tok_in + 2]
        o_gmlp[...] = two[tok_in + 2 : tok_in + 3]

    barrier = pltpu.get_barrier_semaphore()
    for dev in (XN, YN, SIB):
        pl.semaphore_signal(barrier, inc=1, device_id=dev, device_id_type=MESH)
    each_other_plane(
        lambda zb: pl.semaphore_signal(barrier, inc=1, device_id=plane(zb), device_id_type=MESH)
    )
    for c in small_copies[2:] + small_copies[:2]:
        c.start()
    order = ITEMS[1:]
    for w in order:
        own_copy(w).start()
    cot_copy = pltpu.make_async_copy(cot_hbm, cot, lsem.at[PACK])
    cot_copy.start()

    for c in small_copies[2:]:
        c.wait()

    @pl.when(m == 0)
    def _():
        pack_block(PK.at[0, row_of(f)], w_in1, [b_in1])

    @pl.when(m == 1)
    def _():
        pack_block(PK.at[1, row_of(f)], w_res, [b_in2, g_attn, g_mlp])

    pl.semaphore_wait(barrier, 6)

    ag_ready(IN2)
    ag_own_xy(IN2)
    ag_ready(XTRA)
    ag_own_xy(XTRA)
    ag_ready(WOUT)
    ag_own_xy(WOUT)
    ag_own_z(IN2)
    ag_column(IN2, 1)
    ag_first_x(XTRA)
    ag_ready(WQ)
    ag_own_xy(WQ)
    ag_ready(WUP)
    ag_own_xy(WUP)
    ag_own_xy(PACK)
    prepare()
    ag_own_z(PACK)
    ag_column(IN2, 2)
    ag_column(IN2, 3)
    ag_ready(WK)
    ag_own_z(WK)
    ag_own_z(WQ)
    ag_column(PACK, 1)
    ag_own_xy(WK)
    ag_plane(PACK, 0)
    ag_plane(IN2, 1)
    ag_column(WK, 2)
    ag_first_y(XTRA)
    ag_ready(WV)
    ag_own_xy(WV)
    ag_own_z(WV)
    ag_column(PACK, 2)
    ag_own_z(XTRA)
    ag_plane(IN2, 0)
    ag_plane(IN2, 2)
    ag_first_d(XTRA)
    ag_column(PACK, 3)
    ag_plane(WK, 0)
    ag_own_z(WOUT)
    ag_column(WQ, 1)
    ag_column(WQ, 2)
    ag_plane(IN2, 3)
    ag_own_z(WUP)
    ag_column(WK, 1)
    ag_plane(WQ, 1)
    ag_plane(PACK, 3)
    ag_plane(PACK, 1)
    ag_plane(PACK, 2)
    ag_column(WV, 1)
    ag_plane(WK, 2)
    ag_last(PACK)
    ag_column(WV, 2)
    ag_column(WK, 3)
    ag_column(WQ, 3)
    ag_relay(XTRA, 1)
    ag_column(WV, 3)
    ag_last(IN2)
    ag_plane(WV, 1)
    ag_plane(WQ, 2)
    swap_start(0)
    ag_plane(WK, 1)
    ag_plane(WV, 0)
    ag_column(WOUT, 1)
    ag_relay(XTRA, 0)
    swap_wait(0)
    ag_plane(WV, 3)
    ag_plane(WK, 3)
    ag_plane(WQ, 0)
    ag_plane(WV, 2)
    ag_last(XTRA)
    token_hidden()
    ag_ready(WDOWN)
    ag_own_z(WDOWN)
    ag_first_x(WUP)
    ag_first_y(WUP)
    ag_plane(WQ, 3)
    token_out()
    ag_column(WOUT, 2)
    ag_column(WOUT, 3)
    swap_start(1)
    ag_last(WK)
    swap_wait(1)
    ag_last(WQ)
    ag_plane(WOUT, 1)
    norm_first()
    ag_first_d(WUP)
    ag_last(WV)
    ag_own_xy(WDOWN)
    ag_plane(WOUT, 0)
    project(WK, k)
    ag_column(WDOWN, 2)
    project_v()
    ag_plane(WOUT, 3)
    ag_plane(WOUT, 2)
    project(WQ, q)
    ag_relay(WUP, 0)
    ag_column(WDOWN, 1)
    ag_column(WDOWN, 3)
    attend()
    ag_last(WOUT)
    ag_plane(WDOWN, 0)
    attend_out()
    ag_plane(WDOWN, 2)
    swap_start(2)
    ag_plane(WDOWN, 1)
    ag_relay(WUP, 1)
    ag_plane(WDOWN, 3)
    swap_wait(2)
    norm_second()
    ag_last(WUP)
    feed_up()
    grad_down()
    rs_start(WDOWN, 0)
    ag_last(WDOWN)
    grad_hidden()
    rs_start(WDOWN, 1)
    grad_up()
    feed_down()
    swap_start(3)
    rs_start(WDOWN, 2)
    rs_first_far(WUP, 0)
    grad_norm2()
    rs_first_far(WUP, 1)
    rs_turn(WDOWN, 0)
    swap_start(4)
    swap_wait(3)
    rs_turn(WDOWN, 1)
    rs_first_near(WUP)
    write_output()
    rs_start(WDOWN, 3)
    swap_wait(4)
    norm_grad2()
    grad_out()
    grad_attended()
    rs_start(WOUT, 2)
    rs_turn(WDOWN, 2)
    rs_start(WOUT, 0)
    rs_out(WDOWN, 2)
    rs_start(WOUT, 1)
    attend_back()
    rs_relay(WUP, 0)
    unrotate()
    weight_grad(WQ, nrm, dq[...])
    weight_grad(WK, nrm, dk[...])
    rs_start(WK, 1)
    weight_grad(WV, nrm, dv[...])
    rs_out(WDOWN, 3)
    rs_start(WK, 0)
    grad_norm1()
    rs_turn(WOUT, 0)
    swap_start(5)
    rs_start(WQ, 1)
    rs_relay(WUP, 1)
    rs_start(WV, 0)
    rs_turn(WK, 0)
    rs_first_far(XTRA, 0)
    swap_wait(5)
    rs_start(WQ, 0)
    rs_turn(WK, 1)
    norm_grad1()
    grad_in2()
    rs_start(IN2, 1)
    rs_start(IN2, 0)
    grad_token()
    rs_first_far(XTRA, 1)
    rs_out(WOUT, 3)
    rs_start(IN2, 3)
    rs_start(IN2, 2)
    rs_start(WV, 3)
    pre_act()
    swap_start(6)
    rs_start(WQ, 2)
    rs_turn(WQ, 0)
    swap_wait(6)
    grad_pre()
    rs_first_near(XTRA)
    grad_pack()
    rs_out(WK, 3)
    rs_start(PACK, 0)
    rs_relay(XTRA, 0)
    rs_start(PACK, 3)
    grad_values()
    rs_turn(IN2, 0)
    rs_turn(IN2, 2)
    rs_relay(XTRA, 1)
    rs_start(WV, 2)
    rs_turn(IN2, 1)
    rs_out(IN2, 3)
    rs_turn(PACK, 3)
    rs_out(WK, 2)
    rs_turn(WQ, 2)
    rs_start(WK, 2)
    rs_turn(WQ, 1)
    rs_zsum(WUP, 3)
    rs_turn(WV, 2)
    rs_turn(WV, 0)
    rs_out(WQ, 1)
    rs_out(IN2, 2)
    rs_start(PACK, 1)
    rs_start(WQ, 3)
    rs_turn(PACK, 0)
    rs_zsum(XTRA, 0)
    rs_start(PACK, 2)
    rs_turn(WOUT, 2)
    rs_out(IN2, 1)
    rs_turn(IN2, 3)
    rs_zsum(XTRA, 3)
    rs_out(WQ, 3)
    rs_turn(PACK, 1)
    rs_zsum(XTRA, 2)
    rs_turn(PACK, 2)
    rs_zsum(WUP, 0)
    rs_turn(WDOWN, 3)
    rs_start(WV, 1)
    rs_out(WDOWN, 1)
    rs_out(PACK, 3)
    rs_out(WV, 3)
    rs_out(WQ, 2)
    rs_turn(WK, 2)
    rs_out(PACK, 1)
    rs_turn(WV, 3)
    rs_out(IN2, 0)
    rs_turn(WQ, 3)
    rs_start(WK, 3)
    rs_out(PACK, 2)
    rs_turn(WV, 1)
    rs_out(WK, 1)
    rs_zsum(XTRA, 1)
    rs_out(WV, 1)
    rs_zsum(WUP, 1)
    rs_zsum(WUP, 2)
    rs_turn(WOUT, 1)
    rs_out(WDOWN, 0)
    rs_start(WOUT, 3)
    rs_final(IN2)
    rs_first_turn(WUP)
    rs_out(WV, 2)
    rs_out(WQ, 0)
    rs_final(WDOWN)
    rs_out(WOUT, 1)
    rs_out(WV, 0)
    rs_turn(WK, 3)
    rs_turn(WOUT, 3)
    rs_out(WOUT, 2)
    swap_start(7)
    rs_final(WV)
    rs_out(PACK, 0)
    rs_final(PACK)
    rs_first_turn(XTRA)
    swap_start(8)
    rs_out(WK, 0)
    rs_final(WQ)
    rs_final(WUP)
    rs_final(WK)
    rs_final(XTRA)
    rs_out(WOUT, 0)
    rs_final(WOUT)
    swap_wait(7)
    write_in2()
    swap_wait(8)
    write_small()

    for w in ITEMS:
        if w not in (IN2, PACK):
            hand_out(w).wait()
    out_copy.wait()
    in2_copy.wait()

    def drain(ref, sem):
        remote(ref, ref, sem, sem, XN).wait_send()

    for w in ITEMS:
        drain(w_rows(w, pl.ds(0, (11 if w in PLANE_FIRST else 15) * blk)), ag_send.at[w])
        if w in PLANE_FIRST:

            @pl.when(inner)
            def _():
                drain(w_rows(w, pl.ds(0, 8 * blk)), ag_send.at[w])

        drain(recv[w].at[pl.ds(0, 15)], rs_send.at[w])


def pack_block(dst, matrix, vectors):
    tok_in, blk = matrix.shape
    parts = [matrix[...].astype(f32)] + [t[...].astype(f32) for t in vectors]
    parts.append(jnp.zeros((PL - tok_in - len(vectors), blk), f32))
    tall = jnp.concatenate(parts, 0)
    wide = jnp.concatenate([tall, jnp.zeros((PL, PL - blk), f32)], 1)
    dst[...] = wide.T[0:blk].astype(bf16)


def copy_kernel(count, *refs):
    sources, targets, held, sems = refs[:count], refs[count : 2 * count], refs[2 * count : -1], refs[-1]
    inward = [pltpu.make_async_copy(sources[i], held[i], sems.at[0, i]) for i in range(count)]
    outward = [pltpu.make_async_copy(held[i], targets[i], sems.at[1, i]) for i in range(count)]
    for c in inward:
        c.start()
    for a, b in zip(inward, outward):
        a.wait()
        b.start()
    for c in outward:
        c.wait()


def rotate(vectors, places):
    half_width = vectors.shape[-1] // 2
    frequency = 10000.0 ** (-2.0 * jnp.arange(half_width, dtype=jnp.float32) / vectors.shape[-1])
    angles = places[:, :, None, None] * frequency
    cosine = jnp.cos(angles)
    sine_val = jnp.sin(angles)
    first_half = vectors[..., :half_width]
    second_half = vectors[..., half_width:]
    return jnp.concatenate(
        [
            first_half * cosine - second_half * sine_val,
            second_half * cosine + first_half * sine_val,
        ],
        -1,
    )


def rms_norm(resid_rows, gain_vec):
    return (
        resid_rows
        * lax.rsqrt(jnp.mean(resid_rows * resid_rows, -1, keepdims=True) + 1e-06)
        * gain_vec
    )


def activate(up_rows):
    return jax.nn.gelu(up_rows, approximate=False)


def general_device(
    values,
    lengths,
    w_in1,
    b_in1,
    w_in2,
    b_in2,
    w_res,
    g_attn,
    w_qkv,
    w_out,
    g_mlp,
    w_up,
    w_down,
    cotangent,
):
    f32 = jnp.float32
    bf16 = jnp.bfloat16
    gathered = (
        lax.all_gather(w_in1, "fsdp", axis=1, tiled=True),
        lax.all_gather(b_in1, "fsdp", axis=0, tiled=True),
        lax.all_gather(w_in2, "fsdp", axis=0, tiled=True),
        lax.all_gather(b_in2, "fsdp", axis=0, tiled=True),
        lax.all_gather(w_res, "fsdp", axis=1, tiled=True),
        lax.all_gather(g_attn, "fsdp", axis=0, tiled=True),
        lax.all_gather(w_qkv, "fsdp", axis=0, tiled=True),
        lax.all_gather(w_out, "fsdp", axis=1, tiled=True),
        lax.all_gather(g_mlp, "fsdp", axis=0, tiled=True),
        lax.all_gather(w_up, "fsdp", axis=0, tiled=True),
        lax.all_gather(w_down, "fsdp", axis=1, tiled=True),
    )
    (
        full_in1,
        full_b1,
        full_in2,
        full_b2,
        full_res,
        full_gattn,
        full_qkv,
        full_out,
        full_gmlp,
        full_up,
        full_down,
    ) = gathered
    series = lengths.shape[0]
    seq_len = values.shape[0] // series
    patch_len = values.shape[1]
    slot_ids = jnp.arange(seq_len, dtype=jnp.int32)
    pad_count = seq_len - lengths
    padded = slot_ids[None, :] < pad_count[:, None]
    places = (slot_ids[None, :] - pad_count[:, None]).astype(f32)
    keep_mask = (1.0 - padded.astype(f32)).reshape(-1, 1)
    inputs = jnp.concatenate(
        [values.astype(f32) * keep_mask, jnp.broadcast_to(1.0 - keep_mask, values.shape)], 1
    ).astype(bf16)
    pre_act = jnp.dot(inputs, full_in1, preferred_element_type=f32) + full_b1.astype(f32)
    hidden = jax.nn.silu(pre_act).astype(bf16)
    resid0 = (
        jnp.dot(hidden, full_in2, preferred_element_type=f32)
        + full_b2.astype(f32)
        + jnp.dot(inputs, full_res, preferred_element_type=f32)
    )
    gain_attn = full_gattn.astype(f32)
    normed = rms_norm(resid0, gain_attn).astype(bf16)
    projected = jnp.einsum("td,dch->tch", normed, full_qkv, preferred_element_type=f32)
    local_heads = projected.shape[2] // HD
    head_shape = (series, seq_len, local_heads, HD)
    queries = rotate(projected[:, 0].reshape(head_shape), places).astype(bf16)
    key_rows = rotate(projected[:, 1].reshape(head_shape), places).astype(bf16)
    value_heads = projected[:, 2].reshape(head_shape).astype(bf16)
    causal = slot_ids[None, :] <= slot_ids[:, None]
    diagonal = slot_ids[None, :] == slot_ids[:, None]
    allowed = (causal[None] & (jnp.logical_not(padded)[:, None, :] | diagonal[None]))[:, None]
    scale = HD ** (-0.5)

    def score_block():
        raw = jnp.einsum("sqhe,skhe->shqk", queries, key_rows, preferred_element_type=f32) * scale
        return jnp.where(allowed, raw, -1e30)

    scores = score_block()
    row_max = jnp.max(scores, -1, keepdims=True)
    exponent = jnp.exp(scores - row_max)
    row_total = jnp.sum(exponent, -1, keepdims=True)
    log_total = row_max + jnp.log(row_total)
    attn_probs = (exponent / row_total).astype(bf16)
    attended = (
        jnp.einsum("shqk,skhe->sqhe", attn_probs, value_heads, preferred_element_type=f32)
        .reshape(-1, local_heads * HD)
        .astype(bf16)
    )
    branch_one = lax.psum(jnp.dot(attended, full_out, preferred_element_type=f32), "mp")
    resid1 = resid0 + branch_one
    gain_mlp = full_gmlp.astype(f32)
    normed2 = rms_norm(resid1, gain_mlp).astype(bf16)
    up_rows = jnp.dot(normed2, full_up, preferred_element_type=f32)
    mlp_hidden = activate(up_rows).astype(bf16)
    branch_two = lax.psum(
        jnp.dot(mlp_hidden, full_down, preferred_element_type=f32).astype(jnp.bfloat16), "mp"
    ).astype(jnp.float32)
    result = (resid1 + branch_two).astype(bf16)
    again = (
        lax.all_gather(w_in1, "fsdp", axis=1, tiled=True),
        lax.all_gather(b_in1, "fsdp", axis=0, tiled=True),
        lax.all_gather(w_in2, "fsdp", axis=0, tiled=True),
        lax.all_gather(b_in2, "fsdp", axis=0, tiled=True),
        lax.all_gather(w_res, "fsdp", axis=1, tiled=True),
        lax.all_gather(g_attn, "fsdp", axis=0, tiled=True),
        lax.all_gather(w_qkv, "fsdp", axis=0, tiled=True),
        lax.all_gather(w_out, "fsdp", axis=1, tiled=True),
        lax.all_gather(g_mlp, "fsdp", axis=0, tiled=True),
        lax.all_gather(w_up, "fsdp", axis=0, tiled=True),
        lax.all_gather(w_down, "fsdp", axis=1, tiled=True),
    )
    (
        back_in1,
        back_b1,
        back_in2,
        back_b2,
        back_res,
        back_gattn,
        back_qkv,
        back_out,
        back_gmlp,
        back_up,
        back_down,
    ) = again
    cot_rows = cotangent.astype(f32)
    grad_down = jnp.einsum("tf,td->fd", mlp_hidden, cotangent, preferred_element_type=f32)
    grad_hidden = jnp.einsum("td,fd->tf", cotangent, back_down, preferred_element_type=f32)
    unused_one, pull_mlp = jax.vjp(activate, up_rows)
    grad_up_rows = pull_mlp(grad_hidden)[0].astype(bf16)
    grad_up = jnp.einsum("td,tf->df", normed2, grad_up_rows, preferred_element_type=f32)
    norm_part2 = jnp.einsum("tf,df->td", grad_up_rows, back_up, preferred_element_type=f32)
    norm_grad2 = lax.psum(norm_part2, "mp")
    unused_two, pull_norm2 = jax.vjp(rms_norm, resid1, back_gmlp.astype(f32))
    resid_part1, grad_gmlp = pull_norm2(norm_grad2)
    resid1_grad = cot_rows + resid_part1
    out_grad = resid1_grad.astype(bf16)
    grad_out = jnp.einsum("th,td->hd", attended, out_grad, preferred_element_type=f32)
    attended_grad = (
        jnp.einsum("td,hd->th", out_grad, back_out, preferred_element_type=f32)
        .astype(bf16)
        .reshape(head_shape)
    )
    scores = score_block()
    probs_full = jnp.exp(scores - log_total)
    value_grad = jnp.einsum(
        "shqk,sqhe->skhe", probs_full.astype(bf16), attended_grad, preferred_element_type=f32
    )
    prob_grad = jnp.einsum(
        "sqhe,skhe->shqk", attended_grad, value_heads, preferred_element_type=f32
    )
    score_grad = (
        probs_full * (prob_grad - jnp.sum(prob_grad * probs_full, -1, keepdims=True))
    ).astype(bf16)
    query_grad = (
        jnp.einsum("shqk,skhe->sqhe", score_grad, key_rows, preferred_element_type=f32) * scale
    )
    key_grad = (
        jnp.einsum("shqk,sqhe->skhe", score_grad, queries, preferred_element_type=f32) * scale
    )
    width_local = local_heads * HD
    qkv_rows = jnp.stack(
        [
            rotate(query_grad, -places).reshape(-1, width_local),
            rotate(key_grad, -places).reshape(-1, width_local),
            value_grad.reshape(-1, width_local),
        ],
        1,
    ).astype(bf16)
    grad_qkv = jnp.einsum("td,tch->dch", normed, qkv_rows, preferred_element_type=f32)
    norm_part1 = jnp.einsum("tch,dch->td", qkv_rows, back_qkv, preferred_element_type=f32)
    norm_grad1 = lax.psum(norm_part1, "mp")
    unused_three, pull_norm1 = jax.vjp(rms_norm, resid0, back_gattn.astype(f32))
    resid_part0, grad_gattn = pull_norm1(norm_grad1)
    resid0_grad = (resid1_grad + resid_part0).astype(bf16)
    grad_in2 = jnp.einsum("th,td->hd", hidden, resid0_grad, preferred_element_type=f32)
    grad_b2 = jnp.sum(resid0_grad.astype(f32), 0)
    grad_res = jnp.einsum("tp,td->pd", inputs, resid0_grad, preferred_element_type=f32)
    hidden_grad = jnp.einsum("td,hd->th", resid0_grad, back_in2, preferred_element_type=f32)
    unused_four, pull_silu = jax.vjp(jax.nn.silu, pre_act)
    pre_grad = pull_silu(hidden_grad)[0].astype(bf16)
    grad_in1 = jnp.einsum("tp,th->ph", inputs, pre_grad, preferred_element_type=f32)
    grad_b1 = jnp.sum(pre_grad.astype(f32), 0)
    input_grad = jnp.einsum(
        "th,ph->tp", pre_grad, back_in1, preferred_element_type=f32
    ) + jnp.einsum("td,pd->tp", resid0_grad, back_res, preferred_element_type=f32)
    values_grad = input_grad[:, :patch_len] * keep_mask
    shares = tuple(
        (
            lax.psum_scatter(grad_in1, "fsdp", scatter_dimension=1, tiled=True),
            lax.psum_scatter(grad_b1, "fsdp", scatter_dimension=0, tiled=True),
            lax.psum_scatter(grad_in2, "fsdp", scatter_dimension=0, tiled=True),
            lax.psum_scatter(grad_b2, "fsdp", scatter_dimension=0, tiled=True),
            lax.psum_scatter(grad_res, "fsdp", scatter_dimension=1, tiled=True),
            lax.psum_scatter(grad_gattn, "fsdp", scatter_dimension=0, tiled=True),
            lax.psum_scatter(grad_qkv, "fsdp", scatter_dimension=0, tiled=True),
            lax.psum_scatter(grad_out, "fsdp", scatter_dimension=1, tiled=True),
            lax.psum_scatter(grad_gmlp, "fsdp", scatter_dimension=0, tiled=True),
            lax.psum_scatter(grad_up, "fsdp", scatter_dimension=0, tiled=True),
            lax.psum_scatter(grad_down, "fsdp", scatter_dimension=1, tiled=True),
        )
    )
    return (result, values_grad) + shares


def fused_device(
    values,
    lengths,
    w_in1,
    b_in1,
    w_in2,
    b_in2,
    w_res,
    g_attn,
    w_qkv,
    w_out,
    g_mlp,
    w_up,
    w_down,
    cotangent,
):
    rows, width = cotangent.shape
    half = w_out.shape[0]
    blk = w_in2.shape[0]
    patch = values.shape[1]
    tok_in = w_in1.shape[0]
    heads = half // HD
    vmem = pl.BlockSpec(memory_space=pltpu.VMEM)
    hbm = pl.BlockSpec(memory_space=pl.ANY)

    def shape(*dims, dtype=f32):
        return jax.ShapeDtypeStruct(dims, dtype)

    out_shape = (
        shape(rows, width, dtype=bf16),
        shape(patch, rows),
        shape(tok_in, blk),
        shape(1, blk),
        shape(blk, width),
        shape(1, blk),
        shape(tok_in, blk),
        shape(1, blk),
        shape(3, blk, half),
        shape(blk, half),
        shape(1, blk),
        shape(blk, half),
        shape(blk, half),
    )
    V = pltpu.VMEM
    small = [
        lengths,
        values.T,
        w_in1,
        w_res,
        b_in1[None],
        b_in2[None],
        g_attn[None],
        g_mlp[None],
    ]
    scratch = [
        [pltpu.SMEM(lengths.shape, lengths.dtype)] + [V(a.shape, a.dtype) for a in small[1:]],
        V((NW, width, half), bf16),
        V((2, width, PL), bf16),
        V((NW, width, half), bf16),
        V((width, PL), bf16),
        {
            w: V((Z_SLOTS if w in Z_FIRST else SLOTS, blk, cols_of(w, half)[1] - cols_of(w, half)[0]), bf16)
            for w in ITEMS
        },
        V((2, rows, half), f32),
        V((rows, width), f32),
        V((2, rows, width), f32),
        V((2, rows, width), f32),
        V((rows, width), bf16),
        V((rows, width), bf16),
        V((rows, width), bf16),
        V((rows, width), bf16),
        V((rows, width), bf16),
        V((rows, half), bf16),
        V((rows, half), bf16),
        V((rows, half), bf16),
        V((heads, rows, rows), f32),
        V((rows, half), bf16),
        V((rows, half), f32),
        V((rows, half), bf16),
        V((rows, width), bf16),
        V((rows, half), bf16),
        V((rows, half), bf16),
        V((rows, half), bf16),
        V((rows, half), bf16),
        V((rows, width), f32),
        V((rows, width), bf16),
        V((rows, half), f32),
        V((rows, half), f32),
        V((rows, rows), f32),
        V((rows, PL), bf16),
        V((2, 8, width), f32),
        V((2, 16, width), bf16),
        V((8, width), f32),
        V((rows, PL), f32),
        V((NW - 1, blk, half), f32),
        V((2, blk, half), f32),
        V((2, blk, PL), f32),
        V((rows, width), bf16),
        V((blk, width), f32),
        pltpu.SemaphoreType.DMA((9,)),
        pltpu.SemaphoreType.DMA((9, 16)),
        pltpu.SemaphoreType.DMA((9,)),
        pltpu.SemaphoreType.DMA((9, Z_SLOTS)),
        pltpu.SemaphoreType.DMA((9,)),
        pltpu.SemaphoreType.DMA((9,)),
        pltpu.SemaphoreType.DMA((9,)),
        pltpu.SemaphoreType.DMA((9,)),
        pltpu.SemaphoreType.DMA((len(small),)),
    ]
    results = pl.pallas_call(
        layer_kernel,
        name="layer",
        out_shape=out_shape,
        in_specs=[[hbm] * len(small)] + [hbm] * 6,
        out_specs=(hbm,) + (vmem,) * 3 + (hbm,) + (vmem,) * 3 + (hbm,) * 2 + (vmem,) + (hbm,) * 2,
        scratch_shapes=scratch,
        compiler_params=pltpu.CompilerParams(
            collective_id=0, has_side_effects=True, vmem_limit_bytes=VMEM_BYTES
        ),
    )(
        small,
        w_in2,
        jnp.transpose(w_qkv, (1, 0, 2)),
        w_out.T,
        w_up,
        w_down.T,
        cotangent,
    )
    (
        out,
        d_values,
        d_in1,
        d_b1,
        d_in2,
        d_b2,
        d_res,
        d_gattn,
        d_qkv,
        d_out,
        d_gmlp,
        d_up,
        d_down,
    ) = pl.pallas_call(
        functools.partial(copy_kernel, len(out_shape)),
        name="hand_over",
        out_shape=out_shape,
        in_specs=[hbm] * len(out_shape),
        out_specs=(hbm,) * len(out_shape),
        scratch_shapes=[V(s.shape, s.dtype) for s in out_shape]
        + [pltpu.SemaphoreType.DMA((2, len(out_shape)))],
    )(*results)
    return (
        out,
        d_values.T,
        d_in1,
        d_b1[0],
        d_in2,
        d_b2[0],
        d_res,
        d_gattn[0],
        jnp.transpose(d_qkv, (1, 0, 2)),
        d_out.T,
        d_gmlp[0],
        d_up,
        d_down.T,
    )


def on_device(*args):
    blk, width = args[4].shape
    half = args[9].shape[0]
    shards = width // blk
    series = args[1].shape[0]
    fits = (
        shards == 16
        and 2 * half == width
        and blk % 16 == 0
        and half % 128 == 0
        and args[0].shape[0] % 64 == 0
        and series <= 8
    )
    return (fused_device if fits else general_device)(*args)


def solution(mesh):
    in_specs = (
        P("fsdp", None),
        P("fsdp"),
        P(None, "fsdp"),
        P("fsdp"),
        P("fsdp", None),
        P("fsdp"),
        P(None, "fsdp"),
        P("fsdp"),
        P("fsdp", None, "mp"),
        P("mp", "fsdp"),
        P("fsdp"),
        P("fsdp", "mp"),
        P("mp", "fsdp"),
        P("fsdp", None),
    )
    out_specs = (
        P("fsdp", None),
        P("fsdp", None),
        P(None, "fsdp"),
        P("fsdp"),
        P("fsdp", None),
        P("fsdp"),
        P(None, "fsdp"),
        P("fsdp"),
        P("fsdp", None, "mp"),
        P("mp", "fsdp"),
        P("fsdp"),
        P("fsdp", "mp"),
        P("mp", "fsdp"),
    )
    return jax.shard_map(
        on_device, mesh=mesh, in_specs=in_specs, out_specs=out_specs, check_vma=False
    )
```

```python
import functools
import math

import jax
import jax.numpy as jnp
from jax import lax
from jax.experimental import pallas as pl
from jax.experimental.pallas import tpu as pltpu
from jax.sharding import PartitionSpec as P

HD = 80
MESH = pl.DeviceIdType.MESH
VMEM_BYTES = 63 * 2**20
f32 = jnp.float32
bf16 = jnp.bfloat16

IN2, WQ, WK, WV, WOUT, WUP, WDOWN, PACK, XTRA = range(9)
NW = 7
PL = 128
SPLIT, CUT = WQ, 384
ITEMS = (PACK, IN2, WQ, WK, WV, WOUT, WUP, WDOWN) + (() if SPLIT is None else (XTRA,))
PLANE_FIRST = (WUP, XTRA)
Z_FIRST = (WUP, XTRA)


def cols_of(w, half):
    if SPLIT is None or w not in (SPLIT, XTRA):
        return 0, PL if w == PACK else half
    return (0, CUT) if w == SPLIT else (CUT, half)


SLOT_A, SLOT_X, SLOT_Y, SLOT_V, SLOTS = 0, 4, 8, 12, 16
Z_RELAY, Z_NEAR, Z_FAR, Z_A, Z_X, Z_Y, Z_SLOTS = 0, 8, 12, 16, 17, 18, 19


def dot(left, right, left_dim, right_dim):
    return lax.dot_general(
        left, right, (((left_dim,), (right_dim,)), ((), ())), preferred_element_type=f32
    )


def layer_kernel(
    small_hbm,
    in2,
    qkv,
    out_t,
    up,
    down_t,
    cot_hbm,
    o_out,
    o_dval,
    o_in1,
    o_b1,
    o_in2,
    o_b2,
    o_res,
    o_gattn,
    o_qkv,
    o_wout,
    o_gmlp,
    o_up,
    o_down,
    small,
    W,
    PK,
    G,
    GP,
    recv,
    R0,
    R1,
    S,
    X,
    SB,
    XB,
    hid,
    nrm,
    nrm2,
    q,
    k,
    v,
    prob,
    att,
    gprime,
    mlp,
    cot,
    dup,
    dq,
    dk,
    dv,
    tmp,
    dr0,
    rope_c,
    rope_s,
    bias,
    inx,
    gains,
    dgs,
    accg,
    keep_col,
    fin,
    fin_in2,
    fin_pack,
    out_rows,
    in2_rows,
    ag_send,
    ag_recv,
    rs_send,
    rs_recv,
    ex_send,
    ex_recv,
    lsem,
    out_sem,
    small_sem,
):
    lengths, values_t, w_in1, w_res, b_in1, b_in2, g_attn, g_mlp = small
    rows, width = cot.shape
    half = W.shape[2]
    blk = in2.shape[0]
    series = lengths.shape[0]
    seq = rows // series
    heads = half // HD
    patch = values_t.shape[0]

    f = lax.axis_index("fsdp")
    m = lax.axis_index("mp")
    x = lax.rem(f, 2)
    y = lax.rem(lax.div(f, 2), 2)
    z = lax.div(f, 4)
    c0 = f - 4 * z
    cx = c0 + 1 - 2 * x
    cy = c0 + 2 - 4 * y
    cd = 3 - c0
    XN, YN, SIB = (4 * z + cx, m), (4 * z + cy, m), (f, 1 - m)
    z_high = (z >= 2).astype(jnp.int32)
    inner = jnp.logical_and(z > 0, z < 3)
    z_inner = inner.astype(jnp.int32)
    z_near = z + 1 - 2 * lax.rem(z, 2)
    z_far = 2 - z_high
    z_even = lax.rem(z, 2) == 0
    z_odd = jnp.logical_not(z_even)

    def plane(zb):
        return (4 * zb + c0, m)

    def near(i):
        swap = (i == 0).astype(jnp.int32) - (i == 1).astype(jnp.int32)
        low = i + z_inner * swap
        return low + z_high * (3 - 2 * low)

    def each_plane(order, body, start=0):
        def step(i, carry):
            body(order(i))
            return carry

        lax.fori_loop(start, 4, step, 0)

    def each_other_plane(body):
        each_plane(near, body, 1)

    nearest = [near(jnp.int32(i)) for i in range(4)]

    def row_of(b):
        return pl.ds(pl.multiple_of(b * blk, 16), blk)

    def whole(w):
        return SPLIT if w == XTRA else w

    def part(ref, w, *index):
        low, high = cols_of(w, half)
        return ref.at[(*index, slice(low, high))]

    def w_rows(w, r):
        return PK.at[m, r] if w == PACK else part(W, w, whole(w), r)

    def w_block(w, b):
        return w_rows(w, row_of(b))

    def g_block(w, b):
        return GP.at[row_of(b)] if w == PACK else part(G, w, whole(w), row_of(b))

    def r_block(w, s):
        return recv[w].at[s]

    def remote(src, dst, send, recv, dev):
        return pltpu.make_async_remote_copy(
            src_ref=src, dst_ref=dst, send_sem=send, recv_sem=recv, device_id=dev, device_id_type=MESH
        )

    def ag_push(w, b, *devs):
        ref = w_block(w, b)
        for dev in devs:
            remote(ref, ref, ag_send.at[w], ag_recv.at[w, b], dev).start()

    def ag_await(w, b):
        ref = w_block(w, b)
        remote(ref, ref, ag_send.at[w], ag_recv.at[w, b], XN).wait_recv()

    mcols = pl.ds(pl.multiple_of(m * half, 128), half)

    def own_copy(w):
        if w == IN2:
            src = in2.at[:, mcols]
        elif whole(w) in (WQ, WK, WV):
            src = part(qkv, w, whole(w) - WQ, slice(None))
        else:
            src = part({WOUT: out_t, WUP: up, WDOWN: down_t}[whole(w)], w, slice(None))
        return pltpu.make_async_copy(src, w_block(w, f), lsem.at[w])

    def ag_ready(w):
        own_copy(w).wait()

    def ag_own_xy(w):
        ag_push(w, f, XN, YN)

    def ag_own_z(w):
        if w in PLANE_FIRST:
            ag_push(w, f, plane(z_near), plane(z_far))
        else:
            each_other_plane(lambda zb: ag_push(w, f, plane(zb)))

    def ag_column(w, i):
        b = 4 * nearest[i] + c0
        ag_await(w, b)
        ag_push(w, b, XN, YN)

    def ag_from_x(w, zb, even):
        ag_await(w, 4 * zb + cx)

        @pl.when(even)
        def _():
            ag_push(w, 4 * zb + cx, YN)

    def ag_from_y(w, zb, even):
        ag_await(w, 4 * zb + cy)

        @pl.when(jnp.logical_not(even))
        def _():
            ag_push(w, 4 * zb + cy, XN)

    def ag_plane(w, i):
        even = lax.rem(nearest[i], 2) == 0
        ag_from_x(w, nearest[i], even)
        ag_from_y(w, nearest[i], even)

    def turns_y(w):
        return z_odd if w in (XTRA, PACK) else z_even

    def ag_first_x(w):
        ag_from_x(w, z, turns_y(w))
        ag_push(w, 4 * z + cx, plane(z_near), plane(z_far))

    def ag_first_y(w):
        ag_from_y(w, z, turns_y(w))
        ag_push(w, 4 * z + cy, plane(z_near), plane(z_far))

    def ag_first_d(w):
        ag_await(w, 4 * z + cd)
        ag_push(w, 4 * z + cd, plane(z_near), plane(z_far))

    def ag_relay(w, i):
        @pl.when(inner)
        def _():
            zb = (3 - z, 3 * (1 - z_high))[i]
            for c in (c0, cx, cy, cd):
                ag_await(w, 4 * zb + c)
                ag_push(w, 4 * zb + c, plane(3 * z_high))

    def ag_last(w):
        if w in PLANE_FIRST:
            for c in (c0, cx, cy, cd):
                ag_await(w, 4 * z_near + c)

            @pl.when(jnp.logical_not(inner))
            def _():
                for zb in (z_far, 3 - z):
                    for c in (c0, cx, cy, cd):
                        ag_await(w, 4 * zb + c)
        else:
            each_plane(near, lambda zb: ag_await(w, 4 * zb + cd))

    def final_of(w):
        if w == PACK:
            return fin_pack.at[m]
        if w == IN2:
            return fin_in2.at[m]
        return part(fin, w, whole(w) - WQ, slice(None))

    targets = [o_qkv.at[0], o_qkv.at[1], o_qkv.at[2], o_wout, o_up, o_down]

    def hand_out(w):
        target = part(targets[whole(w) - WQ], w, slice(None))
        return pltpu.make_async_copy(final_of(w), target, out_sem.at[w])

    def rs_push(w, src, slot, dev):
        remote(src, r_block(w, slot), rs_send.at[w], rs_recv.at[w, slot], dev).start()

    def rs_await(w, slot):
        ref = r_block(w, slot)
        remote(ref, ref, rs_send.at[w], rs_recv.at[w, slot], XN).wait_recv()

    def add_to(ref, other):
        ref[...] = (ref[...].astype(f32) + other[...].astype(f32)).astype(bf16)

    def sum3(a, b, c):
        return a[...].astype(f32) + b[...].astype(f32) + c[...].astype(f32)

    def rs_start(w, i):
        zb = nearest[3 - i]
        even = lax.rem(zb, 2) == 0

        @pl.when(even)
        def _():
            rs_push(w, g_block(w, 4 * zb + cd), SLOT_A + zb, YN)
            rs_push(w, g_block(w, 4 * zb + cy), SLOT_Y + zb, YN)

        @pl.when(jnp.logical_not(even))
        def _():
            rs_push(w, g_block(w, 4 * zb + cd), SLOT_A + zb, XN)
            rs_push(w, g_block(w, 4 * zb + cx), SLOT_X + zb, XN)

    def turn(w, slot_a, even, own_x, own_y, slot_x, slot_y):
        rs_await(w, slot_a)
        ref = r_block(w, slot_a)

        @pl.when(even)
        def _():
            add_to(ref, own_x)
            rs_push(w, ref, slot_x, XN)

        @pl.when(jnp.logical_not(even))
        def _():
            add_to(ref, own_y)
            rs_push(w, ref, slot_y, YN)

    def rs_turn(w, i):
        zb = nearest[3 - i]
        own_x, own_y = g_block(w, 4 * zb + cx), g_block(w, 4 * zb + cy)
        turn(w, SLOT_A + zb, lax.rem(zb, 2) == 0, own_x, own_y, SLOT_X + zb, SLOT_Y + zb)

    def rs_out(w, i):
        zb = nearest[i]
        rs_await(w, SLOT_X + zb)
        rs_await(w, SLOT_Y + zb)
        ref = r_block(w, SLOT_X + zb)
        total = sum3(g_block(w, 4 * zb + c0), ref, r_block(w, SLOT_Y + zb))
        if i == 0:
            final_of(w)[...] = total
        else:
            ref[...] = total.astype(bf16)
            rs_push(w, ref, SLOT_V + z, plane(zb))

    def rs_first_far(w, i):
        @pl.when(jnp.logical_not(inner))
        def _():
            zb = (3 - z, z_far)[i]
            for c in (cd, cx, cy, c0):
                slot = Z_RELAY + 4 * lax.rem(zb, 2) + c
                rs_push(w, g_block(w, 4 * zb + c), slot, plane(1 + z_high))

    def rs_first_near(w):
        for c in (cd, cx, cy, c0):
            rs_push(w, g_block(w, 4 * z_near + c), Z_NEAR + c, plane(z_near))

    def rs_relay(w, i):
        @pl.when(inner)
        def _():
            zb = (3 * (1 - z_high), z_far)[i]
            for c in (cd, cx, cy, c0):
                slot = Z_RELAY + 4 * lax.rem(zb, 2) + c
                rs_await(w, slot)
                ref = r_block(w, slot)
                add_to(ref, g_block(w, 4 * zb + c))
                rs_push(w, ref, Z_FAR + c, plane(zb))

    def rs_zsum(w, i):
        c = (cd, cx, cy, c0)[i]
        rs_await(w, Z_NEAR + c)
        rs_await(w, Z_FAR + c)
        ref = r_block(w, Z_NEAR + c)
        total = sum3(ref, r_block(w, Z_FAR + c), g_block(w, 4 * z + c))
        if i == 3:
            final_of(w)[...] = total
            return
        ref[...] = total.astype(bf16)
        if i in (0, 2):

            @pl.when(z_odd)
            def _():
                rs_push(w, ref, Z_A if i == 0 else Z_Y, YN)

        if i in (0, 1):

            @pl.when(z_even)
            def _():
                rs_push(w, ref, Z_A if i == 0 else Z_X, XN)

    def rs_first_turn(w):
        turn(w, Z_A, z_odd, r_block(w, Z_NEAR + cx), r_block(w, Z_NEAR + cy), Z_X, Z_Y)

    def rs_final(w):
        final = final_of(w)
        if w in Z_FIRST:
            rs_await(w, Z_X)
            rs_await(w, Z_Y)
            final[...] = sum3(final, r_block(w, Z_X), r_block(w, Z_Y))
        else:
            for i in (1, 2, 3):
                rs_await(w, SLOT_V + nearest[i])
            parts = [r_block(w, SLOT_V + nearest[i])[...].astype(f32) for i in (1, 2, 3)]
            final[...] = final[...] + (parts[0] + parts[1] + parts[2])
        if w not in (IN2, PACK):
            hand_out(w).start()

    def exchange(i):
        src, dst = {
            0: lambda: (PK.at[m], PK.at[m]),
            1: lambda: (R0.at[m], R0.at[m]),
            2: lambda: (S.at[0], X.at[0]),
            3: lambda: (SB, XB),
            4: lambda: (S.at[1], X.at[1]),
            5: lambda: (S.at[0], X.at[0]),
            6: lambda: (S.at[1], X.at[1]),
            7: lambda: (fin_in2.at[m], fin_in2.at[m]),
            8: lambda: (fin_pack.at[m], fin_pack.at[m]),
        }[i]()
        return remote(src, dst, ex_send.at[i], ex_recv.at[i], SIB)

    def swap_start(i):
        exchange(i).start()

    def swap_wait(i):
        exchange(i).wait()

    def by_rows(step, body, unroll=4):
        def one(i, carry):
            body(pl.ds(pl.multiple_of(i * step, step), step))
            return carry

        lax.fori_loop(0, rows // step, one, 0, unroll=unroll)

    halves = (slice(0, half), slice(half, width))

    def pad_of(slot):
        lens = [lengths[s] for s in range(series)]
        total = jnp.zeros(slot.shape, jnp.int32)
        for s in range(series):
            inside = jnp.logical_and(slot >= s * seq, slot < (s + 1) * seq)
            total = jnp.where(inside, (s + 1) * seq - lens[s], total)
        return total

    def series_of(slot):
        total = jnp.zeros(slot.shape, jnp.int32)
        for s in range(1, series):
            total = total + (slot >= s * seq).astype(jnp.int32)
        return total

    lane = lax.broadcasted_iota(jnp.int32, (1, half), 1).astype(f32)
    in_head = lane - HD * jnp.floor((lane + 0.5) / HD)
    first = in_head < HD // 2

    small_copies = [
        pltpu.make_async_copy(src, dst, small_sem.at[i]) for i, (src, dst) in enumerate(zip(small_hbm, small))
    ]

    def prepare():
        for c in small_copies[:2]:
            c.wait()
        slot_col = lax.broadcasted_iota(jnp.int32, (rows, 1), 0)
        keep = jnp.broadcast_to((slot_col >= pad_of(slot_col)).astype(f32), keep_col.shape)
        keep_col[...] = keep
        lane_i = lax.broadcasted_iota(jnp.int32, (rows, PL), 1)
        tall = jnp.concatenate([values_t[...].astype(f32), jnp.zeros((PL - patch, rows), f32)], 0)
        inx[...] = jnp.where(
            lane_i < patch,
            tall.T * keep,
            jnp.where(lane_i < 2 * patch, 1.0 - keep, (lane_i == 2 * patch).astype(f32)),
        ).astype(bf16)

        key_slot = lax.broadcasted_iota(jnp.int32, (1, rows), 1)
        key_ok = (key_slot >= pad_of(key_slot)).astype(jnp.int32)
        key_series = series_of(key_slot)

        def bias_rows(s):
            shape = (s.size, rows)
            a = lax.broadcasted_iota(jnp.int32, shape, 0) + s.start
            b = jnp.broadcast_to(key_slot, shape)
            same = series_of(a) == jnp.broadcast_to(key_series, shape)
            ok = jnp.logical_or(jnp.broadcast_to(key_ok, shape) == 1, a == b)
            allowed = jnp.logical_and(jnp.logical_and(same, b <= a), ok)
            bias[s, :] = jnp.where(allowed, 0.0, -1e30)

        by_rows(32, bias_rows, 1)
        turn_i = jnp.where(first, in_head, in_head - HD // 2)
        frequency = jnp.exp(turn_i * (-2.0 * math.log(10000.0) / HD))

        def rope_rows(s):
            slot = lax.broadcasted_iota(jnp.int32, (s.size, 1), 0) + s.start
            place = (slot - pad_of(slot)).astype(f32)
            angle = place * frequency
            rope_c[s, :] = jnp.cos(angle)
            sine = jnp.sin(angle)
            rope_s[s, :] = jnp.where(first, -sine, sine)

        by_rows(16, rope_rows, 1)

    def rope(t, s, inverse):
        other = jnp.where(first, pltpu.roll(t, half - HD // 2, 1), pltpu.roll(t, HD // 2, 1))
        turned = other * rope_s[s, :]
        return t * rope_c[s, :] - turned if inverse else t * rope_c[s, :] + turned

    gain_lane = lax.broadcasted_iota(jnp.int32, (16, PL), 1)

    def pre_act():
        for cols in halves:
            tmp[:, cols] = dot(inx[...], PK[0, cols, :], 1, 1)

    def token_hidden():
        for i in range(2):
            pick = (gain_lane == 2 * patch + 1 + i).astype(bf16)
            gains[i] = dot(pick, PK[1], 1, 1)[0:8]
        pre_act()

        def silu_rows(s):
            t = tmp[s, :]
            hid[s, :] = (t / (1.0 + jnp.exp(-t))).astype(bf16)

        by_rows(16, silu_rows)

    def token_out():
        R0[m] = dot(hid[...], W[IN2], 1, 0) + dot(inx[...], PK[1, mcols, :], 1, 1)

    def norm_rows(load, gain, out):
        def body(s):
            a, b = load(s)
            mean = (jnp.sum(a * a, -1, keepdims=True) + jnp.sum(b * b, -1, keepdims=True)) / width
            scale = lax.rsqrt(mean + 1e-06)
            out[s, halves[0]] = (a * scale * gain[0:1, halves[0]]).astype(bf16)
            out[s, halves[1]] = (b * scale * gain[0:1, halves[1]]).astype(bf16)

        by_rows(16, body)

    def norm_first():
        norm_rows(lambda s: (R0[0, s, :], R0[1, s, :]), gains.at[0], nrm)

    def project(w, out):
        tmp[:, halves[0]] = dot(nrm[...], W[w], 1, 0)

        def body(s):
            out[s, :] = rope(tmp[s, halves[0]], s, False).astype(bf16)

        by_rows(16, body)

    def project_v():
        v[...] = dot(nrm[...], W[WV], 1, 0).astype(bf16)

    win = 256
    scale = HD ** (-0.5)
    win_lane = lax.broadcasted_iota(jnp.int32, (1, win), 1)

    def head_window(h):
        low = jnp.minimum(lax.div(h * HD, 128) * 128, half - win)
        inside = jnp.logical_and(win_lane >= h * HD - low, win_lane < h * HD - low + HD)
        return pl.ds(pl.multiple_of(low, 128), win), inside

    def only(inside, t):
        return jnp.where(inside, t.astype(f32), 0.0).astype(bf16)

    def attend():
        att[...] = jnp.zeros_like(att)

        def one(h, carry):
            cols, inside = head_window(h)
            score = dot(only(inside, q[:, cols]), k[:, cols], 1, 1) * scale + bias[...]
            exponent = jnp.exp(score - jnp.max(score, -1, keepdims=True))
            p = exponent / jnp.sum(exponent, -1, keepdims=True)
            prob[h] = p
            mixed = dot(p.astype(bf16), v[:, cols], 1, 0)
            att[:, cols] = jnp.where(inside, mixed, att[:, cols].astype(f32)).astype(bf16)
            return carry

        lax.fori_loop(0, heads, one, 0, unroll=2)

    def widen(dst, terms):
        for cols in halves:
            total = None
            for left, w in terms:
                part = dot(left[...], W[w, cols, :], 1, 1)
                total = part if total is None else total + part
            dst[:, cols] = total.astype(dst.dtype)

    def attend_out():
        widen(S.at[0], [(att, WOUT)])

    def norm_second():
        def body(s):
            for i, cols in enumerate(halves):
                R1[s, cols] = R0[i, s, :] + (S[0, s, cols] + X[0, s, cols])

        by_rows(16, body)
        norm_rows(lambda s: (R1[s, halves[0]], R1[s, halves[1]]), gains.at[1], nrm2)

    def feed_up():
        tmp[:, halves[0]] = dot(nrm2[...], W[WUP], 1, 0)

        def gelu_rows(s):
            t = tmp[s, halves[0]]
            phi = 0.5 * (1.0 + lax.erf(t * (2.0**-0.5)))
            mlp[s, :] = (t * phi).astype(bf16)
            gprime[s, :] = phi + t * jnp.exp(-0.5 * t * t) * ((2.0 * math.pi) ** -0.5)

        by_rows(16, gelu_rows)

    def weight_grad(w, left, right):
        for r in halves:
            G[w, r, :] = dot(left[:, r], right, 0, 0).astype(bf16)

    def grad_down():
        cot_copy.wait()
        weight_grad(WDOWN, cot, mlp[...])

    def grad_hidden():
        tmp[:, halves[0]] = dot(cot[...], W[WDOWN], 1, 0)

        def dup_rows(s):
            dup[s, :] = (tmp[s, halves[0]] * gprime[s, :]).astype(bf16)

        by_rows(16, dup_rows)

    def grad_up():
        weight_grad(WUP, nrm2, dup[...])

    def feed_down():
        widen(SB, [(mlp, WDOWN)])

    def grad_norm2():
        widen(S.at[1], [(dup, WUP)])

    out_copy = pltpu.make_async_copy(out_rows, o_out, out_sem.at[PACK])
    in2_copy = pltpu.make_async_copy(in2_rows, o_in2, out_sem.at[IN2])

    def write_output():
        def body(s):
            out_rows[s, :] = (R1[s, :] + (SB[s, :].astype(f32) + XB[s, :].astype(f32))).astype(bf16)

        by_rows(16, body)
        out_copy.start()

    def norm_grad(load, i_part, gain, base, out, keep_sum):
        def body(i, carry):
            s = pl.ds(pl.multiple_of(i * 16, 16), 16)
            xs = load(s)
            mean = sum(jnp.sum(t * t, -1, keepdims=True) for t in xs) / width
            r = lax.rsqrt(mean + 1e-06)
            n1 = [t * r for t in xs]
            dn = [S[i_part, s, c] + X[i_part, s, c] for c in halves]
            gd = [gain[0:1, c] * t for c, t in zip(halves, dn)]
            along = sum(jnp.sum(a * b, -1, keepdims=True) for a, b in zip(gd, n1)) / width
            for c, a, b in zip(halves, gd, n1):
                out(s, c, base(s, c) + r * (a - b * along))
            for c, a, b in zip(halves, dn, n1):
                prod = a * b
                accg[:, c] += prod[0:8] + prod[8:16]
            return carry

        accg[...] = jnp.zeros_like(accg)
        lax.fori_loop(0, rows // 16, body, 0, unroll=4)
        total = accg[...]
        high = total.astype(bf16)
        keep_sum[...] = jnp.concatenate([high.astype(f32), total - high.astype(f32)], 0).astype(bf16)

    def norm_grad2():
        def out(s, c, t):
            R1[s, c] = t
            nrm2[s, c] = t.astype(bf16)

        norm_grad(
            lambda s: [R1[s, c] for c in halves],
            1,
            gains.at[1],
            lambda s, c: cot[s, c].astype(f32),
            out,
            dgs.at[1],
        )

    def norm_grad1():
        def out(s, c, t):
            dr0[s, c] = t.astype(bf16)

        norm_grad(
            lambda s: [R0[i, s, :] for i in range(2)],
            0,
            gains.at[0],
            lambda s, c: R1[s, c],
            out,
            dgs.at[0],
        )

    def grad_out():
        weight_grad(WOUT, nrm2, att[...])

    def grad_attended():
        att[...] = dot(nrm2[...], W[WOUT], 1, 0).astype(bf16)

    def attend_back():
        dv[...] = jnp.zeros_like(dv)
        tmp[...] = jnp.zeros_like(tmp)

        def one(h, carry):
            cols, inside = head_window(h)
            cols2 = pl.ds(pl.multiple_of(cols.start + half, 128), win)
            p = prob[h]
            da = only(inside, att[:, cols])
            dp = dot(da, v[:, cols], 1, 1)
            ds = (p * (dp - jnp.sum(dp * p, -1, keepdims=True))).astype(bf16)
            dv_h = dot(p.astype(bf16), da, 0, 0)
            dq_h = dot(ds, k[:, cols], 1, 0) * scale
            dk_h = dot(ds, q[:, cols], 0, 0) * scale
            dv[:, cols] = jnp.where(inside, dv_h, dv[:, cols].astype(f32)).astype(bf16)
            tmp[:, cols] = jnp.where(inside, dq_h, tmp[:, cols])
            tmp[:, cols2] = jnp.where(inside, dk_h, tmp[:, cols2])
            return carry

        lax.fori_loop(0, heads, one, 0, unroll=2)

    def unrotate():
        def body(s):
            dq[s, :] = rope(tmp[s, halves[0]], s, True).astype(bf16)
            dk[s, :] = rope(tmp[s, halves[1]], s, True).astype(bf16)

        by_rows(16, body)

    def grad_norm1():
        widen(S.at[0], [(dq, WQ), (dk, WK), (dv, WV)])

    def grad_in2():
        weight_grad(IN2, hid, dr0[:, mcols])

    def grad_token():
        for c in halves:
            S[1, :, c] = dot(dr0[:, mcols], W[IN2, c, :], 1, 1)

    def grad_pre():
        def body(s):
            t = tmp[s, :]
            sig = 1.0 / (1.0 + jnp.exp(-t))
            grad = (S[1, s, :] + X[1, s, :]) * (sig * (1.0 + t * (1.0 - sig)))
            nrm[s, :] = grad.astype(bf16)

        by_rows(16, body)

    def grad_values():
        total = dot(nrm[...], PK[0], 1, 0) + dot(dr0[...], PK[1], 1, 0)
        o_dval[...] = (total * keep_col[...]).T[0:patch, :]

    def grad_pack():
        @pl.when(m == 0)
        def _():
            for r in halves:
                GP[r, :] = dot(nrm[:, r], inx[...], 0, 0).astype(bf16)

        @pl.when(m == 1)
        def _():
            for r in halves:
                total = dot(dr0[:, r], inx[...], 0, 0)
                for i in range(2):
                    pick = (gain_lane == 2 * patch + 1 + i).astype(bf16)
                    total = total + dot(dgs[i, :, r], pick, 0, 0)
                GP[r, :] = total.astype(bf16)

    def write_in2():
        for i, c in enumerate(halves):
            in2_rows[:, c] = fin_in2[i]
        in2_copy.start()

    def write_small():
        tok_in = 2 * patch
        one, two = fin_pack[0].T, fin_pack[1].T
        o_in1[...] = one[0:tok_in]
        o_b1[...] = one[tok_in : tok_in + 1]
        o_res[...] = two[0:tok_in]
        o_b2[...] = two[tok_in : tok_in + 1]
        o_gattn[...] = two[tok_in + 1 : tok_in + 2]
        o_gmlp[...] = two[tok_in + 2 : tok_in + 3]

    barrier = pltpu.get_barrier_semaphore()
    for dev in (XN, YN, SIB):
        pl.semaphore_signal(barrier, inc=1, device_id=dev, device_id_type=MESH)
    each_other_plane(
        lambda zb: pl.semaphore_signal(barrier, inc=1, device_id=plane(zb), device_id_type=MESH)
    )
    for c in small_copies[2:] + small_copies[:2]:
        c.start()
    order = ITEMS[1:]
    for w in order:
        own_copy(w).start()
    cot_copy = pltpu.make_async_copy(cot_hbm, cot, lsem.at[PACK])
    cot_copy.start()

    for c in small_copies[2:]:
        c.wait()

    @pl.when(m == 0)
    def _():
        pack_block(PK.at[0, row_of(f)], w_in1, [b_in1])

    @pl.when(m == 1)
    def _():
        pack_block(PK.at[1, row_of(f)], w_res, [b_in2, g_attn, g_mlp])

    pl.semaphore_wait(barrier, 6)

    ag_own_z(PACK)
    ag_ready(WQ)
    ag_own_z(WQ)
    ag_ready(IN2)
    ag_own_xy(IN2)
    ag_own_z(IN2)
    ag_ready(XTRA)
    ag_own_xy(XTRA)
    ag_ready(WV)
    ag_own_xy(WV)
    ag_own_xy(PACK)
    ag_ready(WK)
    ag_own_xy(WK)
    ag_column(PACK, 3)
    ag_column(WQ, 1)
    ag_ready(WOUT)
    ag_own_xy(WOUT)
    ag_own_z(WK)
    ag_own_z(WV)
    ag_column(WQ, 2)
    ag_ready(WUP)
    ag_own_xy(WUP)
    ag_column(PACK, 2)
    ag_column(PACK, 1)
    ag_plane(IN2, 0)
    ag_plane(PACK, 0)
    prepare()
    ag_first_y(XTRA)
    ag_plane(PACK, 3)
    ag_plane(PACK, 2)
    ag_first_x(XTRA)
    ag_own_z(XTRA)
    ag_plane(PACK, 1)
    ag_column(IN2, 3)
    ag_first_d(XTRA)
    ag_column(WK, 1)
    ag_plane(WK, 0)
    ag_own_xy(WQ)
    ag_own_z(WOUT)
    ag_last(PACK)
    ag_column(IN2, 1)
    ag_column(IN2, 2)
    ag_plane(IN2, 3)
    ag_plane(WK, 1)
    ag_plane(WV, 0)
    ag_column(WV, 1)
    ag_column(WQ, 3)
    ag_own_z(WUP)
    ag_plane(IN2, 1)
    ag_plane(IN2, 2)
    swap_start(0)
    ag_column(WK, 2)
    ag_plane(WV, 1)
    ag_ready(WDOWN)
    ag_own_z(WDOWN)
    ag_plane(WQ, 2)
    ag_plane(WQ, 0)
    ag_last(IN2)
    ag_plane(WQ, 3)
    ag_relay(XTRA, 1)
    ag_first_x(WUP)
    ag_column(WV, 2)
    ag_column(WOUT, 1)
    ag_first_y(WUP)
    swap_wait(0)
    token_hidden()
    token_out()
    ag_column(WV, 3)
    ag_column(WK, 3)
    swap_start(1)
    ag_plane(WQ, 1)
    ag_plane(WV, 2)
    swap_wait(1)
    ag_relay(XTRA, 0)
    ag_plane(WV, 3)
    ag_column(WOUT, 3)
    norm_first()
    ag_plane(WK, 3)
    ag_last(WQ)
    ag_plane(WK, 2)
    ag_plane(WOUT, 1)
    ag_first_d(WUP)
    ag_last(WV)
    ag_column(WDOWN, 1)
    ag_own_xy(WDOWN)
    ag_last(XTRA)
    project_v()
    ag_column(WOUT, 2)
    ag_column(WDOWN, 3)
    ag_relay(WUP, 1)
    ag_plane(WOUT, 3)
    ag_last(WK)
    ag_plane(WOUT, 0)
    project(WK, k)
    project(WQ, q)
    attend()
    ag_plane(WOUT, 2)
    ag_column(WDOWN, 2)
    ag_relay(WUP, 0)
    ag_last(WOUT)
    attend_out()
    swap_start(2)
    ag_plane(WDOWN, 1)
    ag_plane(WDOWN, 0)
    ag_plane(WDOWN, 2)
    ag_plane(WDOWN, 3)
    swap_wait(2)
    norm_second()
    ag_last(WUP)
    feed_up()
    grad_down()
    rs_start(WDOWN, 1)
    rs_start(WDOWN, 0)
    ag_last(WDOWN)
    grad_hidden()
    feed_down()
    grad_up()
    rs_first_far(WUP, 1)
    swap_start(3)
    grad_norm2()
    rs_turn(WDOWN, 1)
    rs_turn(WDOWN, 0)
    rs_start(WDOWN, 3)
    swap_start(4)
    swap_wait(3)
    write_output()
    rs_start(WDOWN, 2)
    swap_wait(4)
    rs_out(WDOWN, 3)
    rs_out(WDOWN, 2)
    norm_grad2()
    grad_out()
    rs_start(WOUT, 1)
    rs_start(WOUT, 0)
    rs_first_far(WUP, 0)
    grad_attended()
    rs_first_near(WUP)
    rs_start(WOUT, 2)
    rs_relay(WUP, 1)
    rs_turn(WDOWN, 2)
    attend_back()
    unrotate()
    rs_turn(WOUT, 1)
    weight_grad(WV, nrm, dv[...])
    rs_start(WOUT, 3)
    weight_grad(WQ, nrm, dq[...])
    rs_start(WQ, 2)
    grad_norm1()
    rs_first_far(XTRA, 1)
    rs_turn(WOUT, 0)
    rs_start(WQ, 1)
    weight_grad(WK, nrm, dk[...])
    pre_act()
    rs_start(WK, 0)
    swap_start(5)
    rs_first_far(XTRA, 0)
    rs_start(WK, 1)
    rs_relay(WUP, 0)
    rs_start(WQ, 0)
    rs_out(WOUT, 3)
    rs_out(WOUT, 2)
    swap_wait(5)
    norm_grad1()
    grad_in2()
    grad_token()
    rs_start(IN2, 1)
    rs_start(WV, 0)
    swap_start(6)
    rs_start(IN2, 2)
    rs_turn(IN2, 1)
    rs_start(WK, 2)
    rs_turn(WK, 1)
    rs_turn(WV, 0)
    rs_turn(WOUT, 2)
    swap_wait(6)
    grad_pre()
    rs_start(IN2, 0)
    rs_first_near(XTRA)
    grad_pack()
    rs_start(IN2, 3)
    rs_turn(WK, 0)
    rs_relay(XTRA, 1)
    rs_relay(XTRA, 0)
    rs_turn(IN2, 2)
    rs_start(PACK, 2)
    rs_out(WDOWN, 1)
    rs_turn(WK, 2)
    rs_start(PACK, 3)
    rs_turn(WQ, 1)
    rs_start(PACK, 0)
    rs_out(IN2, 2)
    rs_start(PACK, 1)
    rs_out(WV, 3)
    rs_start(WV, 3)
    grad_values()
    rs_out(WK, 2)
    rs_start(WV, 1)
    rs_turn(IN2, 3)
    rs_turn(PACK, 2)
    rs_turn(PACK, 1)
    rs_out(WK, 3)
    rs_out(IN2, 1)
    rs_start(WV, 2)
    rs_out(IN2, 0)
    rs_out(WOUT, 1)
    rs_turn(WOUT, 3)
    rs_turn(WV, 1)
    rs_turn(IN2, 0)
    rs_turn(PACK, 3)
    rs_out(PACK, 1)
    rs_turn(PACK, 0)
    rs_out(PACK, 2)
    rs_turn(WQ, 0)
    rs_zsum(XTRA, 0)
    rs_start(WK, 3)
    rs_turn(WQ, 2)
    rs_out(PACK, 3)
    rs_zsum(XTRA, 3)
    rs_zsum(XTRA, 2)
    rs_start(WQ, 3)
    rs_turn(WV, 2)
    rs_turn(WDOWN, 3)
    rs_out(IN2, 3)
    rs_out(WV, 2)
    rs_turn(WK, 3)
    rs_zsum(WUP, 0)
    rs_zsum(XTRA, 1)
    rs_turn(WV, 3)
    rs_out(WK, 1)
    rs_out(WOUT, 0)
    rs_out(WDOWN, 0)
    rs_out(WQ, 3)
    rs_turn(WQ, 3)
    rs_final(WOUT)
    rs_out(PACK, 0)
    rs_zsum(WUP, 3)
    rs_first_turn(XTRA)
    rs_out(WQ, 1)
    rs_zsum(WUP, 1)
    rs_zsum(WUP, 2)
    rs_final(IN2)
    rs_out(WK, 0)
    swap_start(7)
    rs_final(PACK)
    rs_out(WV, 1)
    rs_first_turn(WUP)
    rs_out(WQ, 2)
    rs_final(XTRA)
    rs_final(WDOWN)
    swap_start(8)
    rs_out(WV, 0)
    rs_out(WQ, 0)
    rs_final(WV)
    rs_final(WK)
    rs_final(WUP)
    swap_wait(7)
    write_in2()
    swap_wait(8)
    rs_final(WQ)
    write_small()

    for w in ITEMS:
        if w not in (IN2, PACK):
            hand_out(w).wait()
    out_copy.wait()
    in2_copy.wait()

    def drain(ref, sem):
        remote(ref, ref, sem, sem, XN).wait_send()

    for w in ITEMS:
        drain(w_rows(w, pl.ds(0, (11 if w in PLANE_FIRST else 15) * blk)), ag_send.at[w])
        if w in PLANE_FIRST:

            @pl.when(inner)
            def _():
                drain(w_rows(w, pl.ds(0, 8 * blk)), ag_send.at[w])

        drain(recv[w].at[pl.ds(0, 15)], rs_send.at[w])


def pack_block(dst, matrix, vectors):
    tok_in, blk = matrix.shape
    parts = [matrix[...].astype(f32)] + [t[...].astype(f32) for t in vectors]
    parts.append(jnp.zeros((PL - tok_in - len(vectors), blk), f32))
    tall = jnp.concatenate(parts, 0)
    wide = jnp.concatenate([tall, jnp.zeros((PL, PL - blk), f32)], 1)
    dst[...] = wide.T[0:blk].astype(bf16)


def copy_kernel(count, *refs):
    sources, targets, held, sems = refs[:count], refs[count : 2 * count], refs[2 * count : -1], refs[-1]
    inward = [pltpu.make_async_copy(sources[i], held[i], sems.at[0, i]) for i in range(count)]
    outward = [pltpu.make_async_copy(held[i], targets[i], sems.at[1, i]) for i in range(count)]
    for c in inward:
        c.start()
    for a, b in zip(inward, outward):
        a.wait()
        b.start()
    for c in outward:
        c.wait()


def rotate(vectors, places):
    half_width = vectors.shape[-1] // 2
    frequency = 10000.0 ** (-2.0 * jnp.arange(half_width, dtype=jnp.float32) / vectors.shape[-1])
    angles = places[:, :, None, None] * frequency
    cosine = jnp.cos(angles)
    sine_val = jnp.sin(angles)
    first_half = vectors[..., :half_width]
    second_half = vectors[..., half_width:]
    return jnp.concatenate(
        [
            first_half * cosine - second_half * sine_val,
            second_half * cosine + first_half * sine_val,
        ],
        -1,
    )


def rms_norm(resid_rows, gain_vec):
    return (
        resid_rows
        * lax.rsqrt(jnp.mean(resid_rows * resid_rows, -1, keepdims=True) + 1e-06)
        * gain_vec
    )


def activate(up_rows):
    return jax.nn.gelu(up_rows, approximate=False)


def general_device(
    values,
    lengths,
    w_in1,
    b_in1,
    w_in2,
    b_in2,
    w_res,
    g_attn,
    w_qkv,
    w_out,
    g_mlp,
    w_up,
    w_down,
    cotangent,
):
    f32 = jnp.float32
    bf16 = jnp.bfloat16
    gathered = (
        lax.all_gather(w_in1, "fsdp", axis=1, tiled=True),
        lax.all_gather(b_in1, "fsdp", axis=0, tiled=True),
        lax.all_gather(w_in2, "fsdp", axis=0, tiled=True),
        lax.all_gather(b_in2, "fsdp", axis=0, tiled=True),
        lax.all_gather(w_res, "fsdp", axis=1, tiled=True),
        lax.all_gather(g_attn, "fsdp", axis=0, tiled=True),
        lax.all_gather(w_qkv, "fsdp", axis=0, tiled=True),
        lax.all_gather(w_out, "fsdp", axis=1, tiled=True),
        lax.all_gather(g_mlp, "fsdp", axis=0, tiled=True),
        lax.all_gather(w_up, "fsdp", axis=0, tiled=True),
        lax.all_gather(w_down, "fsdp", axis=1, tiled=True),
    )
    (
        full_in1,
        full_b1,
        full_in2,
        full_b2,
        full_res,
        full_gattn,
        full_qkv,
        full_out,
        full_gmlp,
        full_up,
        full_down,
    ) = gathered
    series = lengths.shape[0]
    seq_len = values.shape[0] // series
    patch_len = values.shape[1]
    slot_ids = jnp.arange(seq_len, dtype=jnp.int32)
    pad_count = seq_len - lengths
    padded = slot_ids[None, :] < pad_count[:, None]
    places = (slot_ids[None, :] - pad_count[:, None]).astype(f32)
    keep_mask = (1.0 - padded.astype(f32)).reshape(-1, 1)
    inputs = jnp.concatenate(
        [values.astype(f32) * keep_mask, jnp.broadcast_to(1.0 - keep_mask, values.shape)], 1
    ).astype(bf16)
    pre_act = jnp.dot(inputs, full_in1, preferred_element_type=f32) + full_b1.astype(f32)
    hidden = jax.nn.silu(pre_act).astype(bf16)
    resid0 = (
        jnp.dot(hidden, full_in2, preferred_element_type=f32)
        + full_b2.astype(f32)
        + jnp.dot(inputs, full_res, preferred_element_type=f32)
    )
    gain_attn = full_gattn.astype(f32)
    normed = rms_norm(resid0, gain_attn).astype(bf16)
    projected = jnp.einsum("td,dch->tch", normed, full_qkv, preferred_element_type=f32)
    local_heads = projected.shape[2] // HD
    head_shape = (series, seq_len, local_heads, HD)
    queries = rotate(projected[:, 0].reshape(head_shape), places).astype(bf16)
    key_rows = rotate(projected[:, 1].reshape(head_shape), places).astype(bf16)
    value_heads = projected[:, 2].reshape(head_shape).astype(bf16)
    causal = slot_ids[None, :] <= slot_ids[:, None]
    diagonal = slot_ids[None, :] == slot_ids[:, None]
    allowed = (causal[None] & (jnp.logical_not(padded)[:, None, :] | diagonal[None]))[:, None]
    scale = HD ** (-0.5)

    def score_block():
        raw = jnp.einsum("sqhe,skhe->shqk", queries, key_rows, preferred_element_type=f32) * scale
        return jnp.where(allowed, raw, -1e30)

    scores = score_block()
    row_max = jnp.max(scores, -1, keepdims=True)
    exponent = jnp.exp(scores - row_max)
    row_total = jnp.sum(exponent, -1, keepdims=True)
    log_total = row_max + jnp.log(row_total)
    attn_probs = (exponent / row_total).astype(bf16)
    attended = (
        jnp.einsum("shqk,skhe->sqhe", attn_probs, value_heads, preferred_element_type=f32)
        .reshape(-1, local_heads * HD)
        .astype(bf16)
    )
    branch_one = lax.psum(jnp.dot(attended, full_out, preferred_element_type=f32), "mp")
    resid1 = resid0 + branch_one
    gain_mlp = full_gmlp.astype(f32)
    normed2 = rms_norm(resid1, gain_mlp).astype(bf16)
    up_rows = jnp.dot(normed2, full_up, preferred_element_type=f32)
    mlp_hidden = activate(up_rows).astype(bf16)
    branch_two = lax.psum(
        jnp.dot(mlp_hidden, full_down, preferred_element_type=f32).astype(jnp.bfloat16), "mp"
    ).astype(jnp.float32)
    result = (resid1 + branch_two).astype(bf16)
    again = (
        lax.all_gather(w_in1, "fsdp", axis=1, tiled=True),
        lax.all_gather(b_in1, "fsdp", axis=0, tiled=True),
        lax.all_gather(w_in2, "fsdp", axis=0, tiled=True),
        lax.all_gather(b_in2, "fsdp", axis=0, tiled=True),
        lax.all_gather(w_res, "fsdp", axis=1, tiled=True),
        lax.all_gather(g_attn, "fsdp", axis=0, tiled=True),
        lax.all_gather(w_qkv, "fsdp", axis=0, tiled=True),
        lax.all_gather(w_out, "fsdp", axis=1, tiled=True),
        lax.all_gather(g_mlp, "fsdp", axis=0, tiled=True),
        lax.all_gather(w_up, "fsdp", axis=0, tiled=True),
        lax.all_gather(w_down, "fsdp", axis=1, tiled=True),
    )
    (
        back_in1,
        back_b1,
        back_in2,
        back_b2,
        back_res,
        back_gattn,
        back_qkv,
        back_out,
        back_gmlp,
        back_up,
        back_down,
    ) = again
    cot_rows = cotangent.astype(f32)
    grad_down = jnp.einsum("tf,td->fd", mlp_hidden, cotangent, preferred_element_type=f32)
    grad_hidden = jnp.einsum("td,fd->tf", cotangent, back_down, preferred_element_type=f32)
    unused_one, pull_mlp = jax.vjp(activate, up_rows)
    grad_up_rows = pull_mlp(grad_hidden)[0].astype(bf16)
    grad_up = jnp.einsum("td,tf->df", normed2, grad_up_rows, preferred_element_type=f32)
    norm_part2 = jnp.einsum("tf,df->td", grad_up_rows, back_up, preferred_element_type=f32)
    norm_grad2 = lax.psum(norm_part2, "mp")
    unused_two, pull_norm2 = jax.vjp(rms_norm, resid1, back_gmlp.astype(f32))
    resid_part1, grad_gmlp = pull_norm2(norm_grad2)
    resid1_grad = cot_rows + resid_part1
    out_grad = resid1_grad.astype(bf16)
    grad_out = jnp.einsum("th,td->hd", attended, out_grad, preferred_element_type=f32)
    attended_grad = (
        jnp.einsum("td,hd->th", out_grad, back_out, preferred_element_type=f32)
        .astype(bf16)
        .reshape(head_shape)
    )
    scores = score_block()
    probs_full = jnp.exp(scores - log_total)
    value_grad = jnp.einsum(
        "shqk,sqhe->skhe", probs_full.astype(bf16), attended_grad, preferred_element_type=f32
    )
    prob_grad = jnp.einsum(
        "sqhe,skhe->shqk", attended_grad, value_heads, preferred_element_type=f32
    )
    score_grad = (
        probs_full * (prob_grad - jnp.sum(prob_grad * probs_full, -1, keepdims=True))
    ).astype(bf16)
    query_grad = (
        jnp.einsum("shqk,skhe->sqhe", score_grad, key_rows, preferred_element_type=f32) * scale
    )
    key_grad = (
        jnp.einsum("shqk,sqhe->skhe", score_grad, queries, preferred_element_type=f32) * scale
    )
    width_local = local_heads * HD
    qkv_rows = jnp.stack(
        [
            rotate(query_grad, -places).reshape(-1, width_local),
            rotate(key_grad, -places).reshape(-1, width_local),
            value_grad.reshape(-1, width_local),
        ],
        1,
    ).astype(bf16)
    grad_qkv = jnp.einsum("td,tch->dch", normed, qkv_rows, preferred_element_type=f32)
    norm_part1 = jnp.einsum("tch,dch->td", qkv_rows, back_qkv, preferred_element_type=f32)
    norm_grad1 = lax.psum(norm_part1, "mp")
    unused_three, pull_norm1 = jax.vjp(rms_norm, resid0, back_gattn.astype(f32))
    resid_part0, grad_gattn = pull_norm1(norm_grad1)
    resid0_grad = (resid1_grad + resid_part0).astype(bf16)
    grad_in2 = jnp.einsum("th,td->hd", hidden, resid0_grad, preferred_element_type=f32)
    grad_b2 = jnp.sum(resid0_grad.astype(f32), 0)
    grad_res = jnp.einsum("tp,td->pd", inputs, resid0_grad, preferred_element_type=f32)
    hidden_grad = jnp.einsum("td,hd->th", resid0_grad, back_in2, preferred_element_type=f32)
    unused_four, pull_silu = jax.vjp(jax.nn.silu, pre_act)
    pre_grad = pull_silu(hidden_grad)[0].astype(bf16)
    grad_in1 = jnp.einsum("tp,th->ph", inputs, pre_grad, preferred_element_type=f32)
    grad_b1 = jnp.sum(pre_grad.astype(f32), 0)
    input_grad = jnp.einsum(
        "th,ph->tp", pre_grad, back_in1, preferred_element_type=f32
    ) + jnp.einsum("td,pd->tp", resid0_grad, back_res, preferred_element_type=f32)
    values_grad = input_grad[:, :patch_len] * keep_mask
    shares = tuple(
        (
            lax.psum_scatter(grad_in1, "fsdp", scatter_dimension=1, tiled=True),
            lax.psum_scatter(grad_b1, "fsdp", scatter_dimension=0, tiled=True),
            lax.psum_scatter(grad_in2, "fsdp", scatter_dimension=0, tiled=True),
            lax.psum_scatter(grad_b2, "fsdp", scatter_dimension=0, tiled=True),
            lax.psum_scatter(grad_res, "fsdp", scatter_dimension=1, tiled=True),
            lax.psum_scatter(grad_gattn, "fsdp", scatter_dimension=0, tiled=True),
            lax.psum_scatter(grad_qkv, "fsdp", scatter_dimension=0, tiled=True),
            lax.psum_scatter(grad_out, "fsdp", scatter_dimension=1, tiled=True),
            lax.psum_scatter(grad_gmlp, "fsdp", scatter_dimension=0, tiled=True),
            lax.psum_scatter(grad_up, "fsdp", scatter_dimension=0, tiled=True),
            lax.psum_scatter(grad_down, "fsdp", scatter_dimension=1, tiled=True),
        )
    )
    return (result, values_grad) + shares


def fused_device(
    values,
    lengths,
    w_in1,
    b_in1,
    w_in2,
    b_in2,
    w_res,
    g_attn,
    w_qkv,
    w_out,
    g_mlp,
    w_up,
    w_down,
    cotangent,
):
    rows, width = cotangent.shape
    half = w_out.shape[0]
    blk = w_in2.shape[0]
    patch = values.shape[1]
    tok_in = w_in1.shape[0]
    heads = half // HD
    vmem = pl.BlockSpec(memory_space=pltpu.VMEM)
    hbm = pl.BlockSpec(memory_space=pl.ANY)

    def shape(*dims, dtype=f32):
        return jax.ShapeDtypeStruct(dims, dtype)

    out_shape = (
        shape(rows, width, dtype=bf16),
        shape(patch, rows),
        shape(tok_in, blk),
        shape(1, blk),
        shape(blk, width),
        shape(1, blk),
        shape(tok_in, blk),
        shape(1, blk),
        shape(3, blk, half),
        shape(blk, half),
        shape(1, blk),
        shape(blk, half),
        shape(blk, half),
    )
    V = pltpu.VMEM
    small = [
        lengths,
        values.T,
        w_in1,
        w_res,
        b_in1[None],
        b_in2[None],
        g_attn[None],
        g_mlp[None],
    ]
    scratch = [
        [pltpu.SMEM(lengths.shape, lengths.dtype)] + [V(a.shape, a.dtype) for a in small[1:]],
        V((NW, width, half), bf16),
        V((2, width, PL), bf16),
        V((NW, width, half), bf16),
        V((width, PL), bf16),
        {
            w: V((Z_SLOTS if w in Z_FIRST else SLOTS, blk, cols_of(w, half)[1] - cols_of(w, half)[0]), bf16)
            for w in ITEMS
        },
        V((2, rows, half), f32),
        V((rows, width), f32),
        V((2, rows, width), f32),
        V((2, rows, width), f32),
        V((rows, width), bf16),
        V((rows, width), bf16),
        V((rows, width), bf16),
        V((rows, width), bf16),
        V((rows, width), bf16),
        V((rows, half), bf16),
        V((rows, half), bf16),
        V((rows, half), bf16),
        V((heads, rows, rows), f32),
        V((rows, half), bf16),
        V((rows, half), f32),
        V((rows, half), bf16),
        V((rows, width), bf16),
        V((rows, half), bf16),
        V((rows, half), bf16),
        V((rows, half), bf16),
        V((rows, half), bf16),
        V((rows, width), f32),
        V((rows, width), bf16),
        V((rows, half), f32),
        V((rows, half), f32),
        V((rows, rows), f32),
        V((rows, PL), bf16),
        V((2, 8, width), f32),
        V((2, 16, width), bf16),
        V((8, width), f32),
        V((rows, PL), f32),
        V((NW - 1, blk, half), f32),
        V((2, blk, half), f32),
        V((2, blk, PL), f32),
        V((rows, width), bf16),
        V((blk, width), f32),
        pltpu.SemaphoreType.DMA((9,)),
        pltpu.SemaphoreType.DMA((9, 16)),
        pltpu.SemaphoreType.DMA((9,)),
        pltpu.SemaphoreType.DMA((9, Z_SLOTS)),
        pltpu.SemaphoreType.DMA((9,)),
        pltpu.SemaphoreType.DMA((9,)),
        pltpu.SemaphoreType.DMA((9,)),
        pltpu.SemaphoreType.DMA((9,)),
        pltpu.SemaphoreType.DMA((len(small),)),
    ]
    results = pl.pallas_call(
        layer_kernel,
        name="layer",
        out_shape=out_shape,
        in_specs=[[hbm] * len(small)] + [hbm] * 6,
        out_specs=(hbm,) + (vmem,) * 3 + (hbm,) + (vmem,) * 3 + (hbm,) * 2 + (vmem,) + (hbm,) * 2,
        scratch_shapes=scratch,
        compiler_params=pltpu.CompilerParams(
            collective_id=0, has_side_effects=True, vmem_limit_bytes=VMEM_BYTES
        ),
    )(
        small,
        w_in2,
        jnp.transpose(w_qkv, (1, 0, 2)),
        w_out.T,
        w_up,
        w_down.T,
        cotangent,
    )
    (
        out,
        d_values,
        d_in1,
        d_b1,
        d_in2,
        d_b2,
        d_res,
        d_gattn,
        d_qkv,
        d_out,
        d_gmlp,
        d_up,
        d_down,
    ) = pl.pallas_call(
        functools.partial(copy_kernel, len(out_shape)),
        name="hand_over",
        out_shape=out_shape,
        in_specs=[hbm] * len(out_shape),
        out_specs=(hbm,) * len(out_shape),
        scratch_shapes=[V(s.shape, s.dtype) for s in out_shape]
        + [pltpu.SemaphoreType.DMA((2, len(out_shape)))],
    )(*results)
    return (
        out,
        d_values.T,
        d_in1,
        d_b1[0],
        d_in2,
        d_b2[0],
        d_res,
        d_gattn[0],
        jnp.transpose(d_qkv, (1, 0, 2)),
        d_out.T,
        d_gmlp[0],
        d_up,
        d_down.T,
    )


def on_device(*args):
    blk, width = args[4].shape
    half = args[9].shape[0]
    shards = width // blk
    series = args[1].shape[0]
    fits = (
        shards == 16
        and 2 * half == width
        and blk % 16 == 0
        and half % 128 == 0
        and args[0].shape[0] % 64 == 0
        and series <= 8
    )
    return (fused_device if fits else general_device)(*args)


def solution(mesh):
    in_specs = (
        P("fsdp", None),
        P("fsdp"),
        P(None, "fsdp"),
        P("fsdp"),
        P("fsdp", None),
        P("fsdp"),
        P(None, "fsdp"),
        P("fsdp"),
        P("fsdp", None, "mp"),
        P("mp", "fsdp"),
        P("fsdp"),
        P("fsdp", "mp"),
        P("mp", "fsdp"),
        P("fsdp", None),
    )
    out_specs = (
        P("fsdp", None),
        P("fsdp", None),
        P(None, "fsdp"),
        P("fsdp"),
        P("fsdp", None),
        P("fsdp"),
        P(None, "fsdp"),
        P("fsdp"),
        P("fsdp", None, "mp"),
        P("mp", "fsdp"),
        P("fsdp"),
        P("fsdp", "mp"),
        P("mp", "fsdp"),
    )
    return jax.shard_map(
        on_device, mesh=mesh, in_specs=in_specs, out_specs=out_specs, check_vma=False
    )
```

```python
import functools
import math

import jax
import jax.numpy as jnp
from jax import lax
from jax.experimental import pallas as pl
from jax.experimental.pallas import tpu as pltpu
from jax.sharding import PartitionSpec as P

HD = 80
MESH = pl.DeviceIdType.MESH
VMEM_BYTES = 63 * 2**20
f32 = jnp.float32
bf16 = jnp.bfloat16

IN2, WQ, WK, WV, WOUT, WUP, WDOWN, PACK, XTRA = range(9)
NW = 7
PL = 128
SPLIT, CUT = WQ, 384
ITEMS = (PACK, IN2, WQ, WK, WV, WOUT, WUP, WDOWN) + (() if SPLIT is None else (XTRA,))
PLANE_FIRST = (WUP, XTRA)
Z_FIRST = (WUP, XTRA)


def cols_of(w, half):
    if SPLIT is None or w not in (SPLIT, XTRA):
        return 0, PL if w == PACK else half
    return (0, CUT) if w == SPLIT else (CUT, half)


SLOT_A, SLOT_X, SLOT_Y, SLOT_V, SLOTS = 0, 4, 8, 12, 16
Z_RELAY, Z_NEAR, Z_FAR, Z_A, Z_X, Z_Y, Z_SLOTS = 0, 8, 12, 16, 17, 18, 19


def dot(left, right, left_dim, right_dim):
    return lax.dot_general(
        left, right, (((left_dim,), (right_dim,)), ((), ())), preferred_element_type=f32
    )


def layer_kernel(
    small_hbm,
    in2,
    qkv,
    out_t,
    up,
    down_t,
    cot_hbm,
    o_out,
    o_dval,
    o_in1,
    o_b1,
    o_in2,
    o_b2,
    o_res,
    o_gattn,
    o_qkv,
    o_wout,
    o_gmlp,
    o_up,
    o_down,
    small,
    W,
    PK,
    G,
    GP,
    recv,
    R0,
    R1,
    S,
    X,
    SB,
    XB,
    hid,
    nrm,
    nrm2,
    q,
    k,
    v,
    prob,
    att,
    gprime,
    mlp,
    cot,
    dup,
    dq,
    dk,
    dv,
    tmp,
    dr0,
    rope_c,
    rope_s,
    bias,
    inx,
    gains,
    dgs,
    accg,
    keep_col,
    fin,
    fin_in2,
    fin_pack,
    out_rows,
    in2_rows,
    ag_send,
    ag_recv,
    rs_send,
    rs_recv,
    ex_send,
    ex_recv,
    lsem,
    out_sem,
    small_sem,
):
    lengths, values_t, w_in1, w_res, b_in1, b_in2, g_attn, g_mlp = small
    rows, width = cot.shape
    half = W.shape[2]
    blk = in2.shape[0]
    series = lengths.shape[0]
    seq = rows // series
    heads = half // HD
    patch = values_t.shape[0]

    f = lax.axis_index("fsdp")
    m = lax.axis_index("mp")
    x = lax.rem(f, 2)
    y = lax.rem(lax.div(f, 2), 2)
    z = lax.div(f, 4)
    c0 = f - 4 * z
    cx = c0 + 1 - 2 * x
    cy = c0 + 2 - 4 * y
    cd = 3 - c0
    XN, YN, SIB = (4 * z + cx, m), (4 * z + cy, m), (f, 1 - m)
    z_high = (z >= 2).astype(jnp.int32)
    inner = jnp.logical_and(z > 0, z < 3)
    z_inner = inner.astype(jnp.int32)
    z_near = z + 1 - 2 * lax.rem(z, 2)
    z_far = 2 - z_high
    z_even = lax.rem(z + m, 2) == 0
    z_odd = jnp.logical_not(z_even)

    def plane(zb):
        return (4 * zb + c0, m)

    def near(i):
        swap = (i == 0).astype(jnp.int32) - (i == 1).astype(jnp.int32)
        low = i + z_inner * swap
        return low + z_high * (3 - 2 * low)

    def each_plane(order, body, start=0):
        def step(i, carry):
            body(order(i))
            return carry

        lax.fori_loop(start, 4, step, 0)

    def each_other_plane(body):
        each_plane(near, body, 1)

    nearest = [near(jnp.int32(i)) for i in range(4)]

    def row_of(b):
        return pl.ds(pl.multiple_of(b * blk, 16), blk)

    def whole(w):
        return SPLIT if w == XTRA else w

    def part(ref, w, *index):
        low, high = cols_of(w, half)
        return ref.at[(*index, slice(low, high))]

    def w_rows(w, r):
        return PK.at[m, r] if w == PACK else part(W, w, whole(w), r)

    def w_block(w, b):
        return w_rows(w, row_of(b))

    def g_block(w, b):
        return GP.at[row_of(b)] if w == PACK else part(G, w, whole(w), row_of(b))

    def r_block(w, s):
        return recv[w].at[s]

    def remote(src, dst, send, recv, dev):
        return pltpu.make_async_remote_copy(
            src_ref=src, dst_ref=dst, send_sem=send, recv_sem=recv, device_id=dev, device_id_type=MESH
        )

    def ag_push(w, b, *devs):
        ref = w_block(w, b)
        for dev in devs:
            remote(ref, ref, ag_send.at[w], ag_recv.at[w, b], dev).start()

    def ag_await(w, b):
        ref = w_block(w, b)
        remote(ref, ref, ag_send.at[w], ag_recv.at[w, b], XN).wait_recv()

    mcols = pl.ds(pl.multiple_of(m * half, 128), half)

    def own_copy(w):
        if w == IN2:
            src = in2.at[:, mcols]
        elif whole(w) in (WQ, WK, WV):
            src = part(qkv, w, whole(w) - WQ, slice(None))
        else:
            src = part({WOUT: out_t, WUP: up, WDOWN: down_t}[whole(w)], w, slice(None))
        return pltpu.make_async_copy(src, w_block(w, f), lsem.at[w])

    def ag_ready(w):
        own_copy(w).wait()

    def ag_own_xy(w):
        ag_push(w, f, XN, YN)

    def ag_own_z(w):
        if w in PLANE_FIRST:
            ag_push(w, f, plane(z_near), plane(z_far))
        else:
            each_other_plane(lambda zb: ag_push(w, f, plane(zb)))

    def ag_column(w, i):
        b = 4 * nearest[i] + c0
        ag_await(w, b)
        ag_push(w, b, XN, YN)

    def ag_from_x(w, zb, even):
        ag_await(w, 4 * zb + cx)

        @pl.when(even)
        def _():
            ag_push(w, 4 * zb + cx, YN)

    def ag_from_y(w, zb, even):
        ag_await(w, 4 * zb + cy)

        @pl.when(jnp.logical_not(even))
        def _():
            ag_push(w, 4 * zb + cy, XN)

    def ag_plane(w, i):
        even = lax.rem(nearest[i] + m, 2) == 0
        ag_from_x(w, nearest[i], even)
        ag_from_y(w, nearest[i], even)

    def turns_y(w):
        return z_odd if w in (XTRA, PACK) else z_even

    def ag_first_x(w):
        ag_from_x(w, z, turns_y(w))
        ag_push(w, 4 * z + cx, plane(z_near), plane(z_far))

    def ag_first_y(w):
        ag_from_y(w, z, turns_y(w))
        ag_push(w, 4 * z + cy, plane(z_near), plane(z_far))

    def ag_first_d(w):
        ag_await(w, 4 * z + cd)
        ag_push(w, 4 * z + cd, plane(z_near), plane(z_far))

    def ag_relay(w, i):
        @pl.when(inner)
        def _():
            zb = (3 - z, 3 * (1 - z_high))[i]
            for c in (c0, cx, cy, cd):
                ag_await(w, 4 * zb + c)
                ag_push(w, 4 * zb + c, plane(3 * z_high))

    def ag_last(w):
        if w in PLANE_FIRST:
            for c in (c0, cx, cy, cd):
                ag_await(w, 4 * z_near + c)

            @pl.when(jnp.logical_not(inner))
            def _():
                for zb in (z_far, 3 - z):
                    for c in (c0, cx, cy, cd):
                        ag_await(w, 4 * zb + c)
        else:
            each_plane(near, lambda zb: ag_await(w, 4 * zb + cd))

    def final_of(w):
        if w == PACK:
            return fin_pack.at[m]
        if w == IN2:
            return fin_in2.at[m]
        return part(fin, w, whole(w) - WQ, slice(None))

    targets = [o_qkv.at[0], o_qkv.at[1], o_qkv.at[2], o_wout, o_up, o_down]

    def hand_out(w):
        target = part(targets[whole(w) - WQ], w, slice(None))
        return pltpu.make_async_copy(final_of(w), target, out_sem.at[w])

    def rs_push(w, src, slot, dev):
        remote(src, r_block(w, slot), rs_send.at[w], rs_recv.at[w, slot], dev).start()

    def rs_await(w, slot):
        ref = r_block(w, slot)
        remote(ref, ref, rs_send.at[w], rs_recv.at[w, slot], XN).wait_recv()

    def add_to(ref, other):
        ref[...] = (ref[...].astype(f32) + other[...].astype(f32)).astype(bf16)

    def sum3(a, b, c):
        return a[...].astype(f32) + b[...].astype(f32) + c[...].astype(f32)

    def rs_start(w, i):
        zb = nearest[3 - i]
        even = lax.rem(zb + m, 2) == 0

        @pl.when(even)
        def _():
            rs_push(w, g_block(w, 4 * zb + cd), SLOT_A + zb, YN)
            rs_push(w, g_block(w, 4 * zb + cy), SLOT_Y + zb, YN)

        @pl.when(jnp.logical_not(even))
        def _():
            rs_push(w, g_block(w, 4 * zb + cd), SLOT_A + zb, XN)
            rs_push(w, g_block(w, 4 * zb + cx), SLOT_X + zb, XN)

    def turn(w, slot_a, even, own_x, own_y, slot_x, slot_y):
        rs_await(w, slot_a)
        ref = r_block(w, slot_a)

        @pl.when(even)
        def _():
            add_to(ref, own_x)
            rs_push(w, ref, slot_x, XN)

        @pl.when(jnp.logical_not(even))
        def _():
            add_to(ref, own_y)
            rs_push(w, ref, slot_y, YN)

    def rs_turn(w, i):
        zb = nearest[3 - i]
        own_x, own_y = g_block(w, 4 * zb + cx), g_block(w, 4 * zb + cy)
        turn(w, SLOT_A + zb, lax.rem(zb + m, 2) == 0, own_x, own_y, SLOT_X + zb, SLOT_Y + zb)

    def rs_out(w, i):
        zb = nearest[i]
        rs_await(w, SLOT_X + zb)
        rs_await(w, SLOT_Y + zb)
        ref = r_block(w, SLOT_X + zb)
        total = sum3(g_block(w, 4 * zb + c0), ref, r_block(w, SLOT_Y + zb))
        if i == 0:
            final_of(w)[...] = total
        else:
            ref[...] = total.astype(bf16)
            rs_push(w, ref, SLOT_V + z, plane(zb))

    def rs_first_far(w, i):
        @pl.when(jnp.logical_not(inner))
        def _():
            zb = (3 - z, z_far)[i]
            for c in (cd, cx, cy, c0):
                slot = Z_RELAY + 4 * lax.rem(zb, 2) + c
                rs_push(w, g_block(w, 4 * zb + c), slot, plane(1 + z_high))

    def rs_first_near(w):
        for c in (cd, cx, cy, c0):
            rs_push(w, g_block(w, 4 * z_near + c), Z_NEAR + c, plane(z_near))

    def rs_relay(w, i):
        @pl.when(inner)
        def _():
            zb = (3 * (1 - z_high), z_far)[i]
            for c in (cd, cx, cy, c0):
                slot = Z_RELAY + 4 * lax.rem(zb, 2) + c
                rs_await(w, slot)
                ref = r_block(w, slot)
                add_to(ref, g_block(w, 4 * zb + c))
                rs_push(w, ref, Z_FAR + c, plane(zb))

    def rs_zsum(w, i):
        c = (cd, cx, cy, c0)[i]
        rs_await(w, Z_NEAR + c)
        rs_await(w, Z_FAR + c)
        ref = r_block(w, Z_NEAR + c)
        total = sum3(ref, r_block(w, Z_FAR + c), g_block(w, 4 * z + c))
        if i == 3:
            final_of(w)[...] = total
            return
        ref[...] = total.astype(bf16)
        if i in (0, 2):

            @pl.when(z_odd)
            def _():
                rs_push(w, ref, Z_A if i == 0 else Z_Y, YN)

        if i in (0, 1):

            @pl.when(z_even)
            def _():
                rs_push(w, ref, Z_A if i == 0 else Z_X, XN)

    def rs_first_turn(w):
        turn(w, Z_A, z_odd, r_block(w, Z_NEAR + cx), r_block(w, Z_NEAR + cy), Z_X, Z_Y)

    def rs_final(w):
        final = final_of(w)
        if w in Z_FIRST:
            rs_await(w, Z_X)
            rs_await(w, Z_Y)
            final[...] = sum3(final, r_block(w, Z_X), r_block(w, Z_Y))
        else:
            for i in (1, 2, 3):
                rs_await(w, SLOT_V + nearest[i])
            parts = [r_block(w, SLOT_V + nearest[i])[...].astype(f32) for i in (1, 2, 3)]
            final[...] = final[...] + (parts[0] + parts[1] + parts[2])
        if w not in (IN2, PACK):
            hand_out(w).start()

    def exchange(i):
        src, dst = {
            0: lambda: (PK.at[m], PK.at[m]),
            1: lambda: (R0.at[m], R0.at[m]),
            2: lambda: (S.at[0], X.at[0]),
            3: lambda: (SB, XB),
            4: lambda: (S.at[1], X.at[1]),
            5: lambda: (S.at[0], X.at[0]),
            6: lambda: (S.at[1], X.at[1]),
            7: lambda: (fin_in2.at[m], fin_in2.at[m]),
            8: lambda: (fin_pack.at[m], fin_pack.at[m]),
        }[i]()
        return remote(src, dst, ex_send.at[i], ex_recv.at[i], SIB)

    def swap_start(i):
        exchange(i).start()

    def swap_wait(i):
        exchange(i).wait()

    def by_rows(step, body, unroll=4):
        def one(i, carry):
            body(pl.ds(pl.multiple_of(i * step, step), step))
            return carry

        lax.fori_loop(0, rows // step, one, 0, unroll=unroll)

    halves = (slice(0, half), slice(half, width))

    def pad_of(slot):
        lens = [lengths[s] for s in range(series)]
        total = jnp.zeros(slot.shape, jnp.int32)
        for s in range(series):
            inside = jnp.logical_and(slot >= s * seq, slot < (s + 1) * seq)
            total = jnp.where(inside, (s + 1) * seq - lens[s], total)
        return total

    def series_of(slot):
        total = jnp.zeros(slot.shape, jnp.int32)
        for s in range(1, series):
            total = total + (slot >= s * seq).astype(jnp.int32)
        return total

    lane = lax.broadcasted_iota(jnp.int32, (1, half), 1).astype(f32)
    in_head = lane - HD * jnp.floor((lane + 0.5) / HD)
    first = in_head < HD // 2

    small_copies = [
        pltpu.make_async_copy(src, dst, small_sem.at[i]) for i, (src, dst) in enumerate(zip(small_hbm, small))
    ]

    def prepare():
        for c in small_copies[:2]:
            c.wait()
        slot_col = lax.broadcasted_iota(jnp.int32, (rows, 1), 0)
        keep = jnp.broadcast_to((slot_col >= pad_of(slot_col)).astype(f32), keep_col.shape)
        keep_col[...] = keep
        lane_i = lax.broadcasted_iota(jnp.int32, (rows, PL), 1)
        tall = jnp.concatenate([values_t[...].astype(f32), jnp.zeros((PL - patch, rows), f32)], 0)
        inx[...] = jnp.where(
            lane_i < patch,
            tall.T * keep,
            jnp.where(lane_i < 2 * patch, 1.0 - keep, (lane_i == 2 * patch).astype(f32)),
        ).astype(bf16)

        key_slot = lax.broadcasted_iota(jnp.int32, (1, rows), 1)
        key_ok = (key_slot >= pad_of(key_slot)).astype(jnp.int32)
        key_series = series_of(key_slot)

        def bias_rows(s):
            shape = (s.size, rows)
            a = lax.broadcasted_iota(jnp.int32, shape, 0) + s.start
            b = jnp.broadcast_to(key_slot, shape)
            same = series_of(a) == jnp.broadcast_to(key_series, shape)
            ok = jnp.logical_or(jnp.broadcast_to(key_ok, shape) == 1, a == b)
            allowed = jnp.logical_and(jnp.logical_and(same, b <= a), ok)
            bias[s, :] = jnp.where(allowed, 0.0, -1e30)

        by_rows(32, bias_rows, 1)
        turn_i = jnp.where(first, in_head, in_head - HD // 2)
        frequency = jnp.exp(turn_i * (-2.0 * math.log(10000.0) / HD))

        def rope_rows(s):
            slot = lax.broadcasted_iota(jnp.int32, (s.size, 1), 0) + s.start
            place = (slot - pad_of(slot)).astype(f32)
            angle = place * frequency
            rope_c[s, :] = jnp.cos(angle)
            sine = jnp.sin(angle)
            rope_s[s, :] = jnp.where(first, -sine, sine)

        by_rows(16, rope_rows, 1)

    def rope(t, s, inverse):
        other = jnp.where(first, pltpu.roll(t, half - HD // 2, 1), pltpu.roll(t, HD // 2, 1))
        turned = other * rope_s[s, :]
        return t * rope_c[s, :] - turned if inverse else t * rope_c[s, :] + turned

    gain_lane = lax.broadcasted_iota(jnp.int32, (16, PL), 1)

    def pre_act():
        for cols in halves:
            tmp[:, cols] = dot(inx[...], PK[0, cols, :], 1, 1)

    def token_hidden():
        for i in range(2):
            pick = (gain_lane == 2 * patch + 1 + i).astype(bf16)
            gains[i] = dot(pick, PK[1], 1, 1)[0:8]
        pre_act()

        def silu_rows(s):
            t = tmp[s, :]
            hid[s, :] = (t / (1.0 + jnp.exp(-t))).astype(bf16)

        by_rows(16, silu_rows)

    def token_out():
        R0[m] = dot(hid[...], W[IN2], 1, 0) + dot(inx[...], PK[1, mcols, :], 1, 1)

    def norm_rows(load, gain, out):
        def body(s):
            a, b = load(s)
            mean = (jnp.sum(a * a, -1, keepdims=True) + jnp.sum(b * b, -1, keepdims=True)) / width
            scale = lax.rsqrt(mean + 1e-06)
            out[s, halves[0]] = (a * scale * gain[0:1, halves[0]]).astype(bf16)
            out[s, halves[1]] = (b * scale * gain[0:1, halves[1]]).astype(bf16)

        by_rows(16, body)

    def norm_first():
        norm_rows(lambda s: (R0[0, s, :], R0[1, s, :]), gains.at[0], nrm)

    def project(w, out):
        tmp[:, halves[0]] = dot(nrm[...], W[w], 1, 0)

        def body(s):
            out[s, :] = rope(tmp[s, halves[0]], s, False).astype(bf16)

        by_rows(16, body)

    def project_v():
        v[...] = dot(nrm[...], W[WV], 1, 0).astype(bf16)

    win = 256
    scale = HD ** (-0.5)
    win_lane = lax.broadcasted_iota(jnp.int32, (1, win), 1)

    def head_window(h):
        low = jnp.minimum(lax.div(h * HD, 128) * 128, half - win)
        inside = jnp.logical_and(win_lane >= h * HD - low, win_lane < h * HD - low + HD)
        return pl.ds(pl.multiple_of(low, 128), win), inside

    def only(inside, t):
        return jnp.where(inside, t.astype(f32), 0.0).astype(bf16)

    def attend():
        att[...] = jnp.zeros_like(att)

        def one(h, carry):
            cols, inside = head_window(h)
            score = dot(only(inside, q[:, cols]), k[:, cols], 1, 1) * scale + bias[...]
            exponent = jnp.exp(score - jnp.max(score, -1, keepdims=True))
            p = exponent / jnp.sum(exponent, -1, keepdims=True)
            prob[h] = p
            mixed = dot(p.astype(bf16), v[:, cols], 1, 0)
            att[:, cols] = jnp.where(inside, mixed, att[:, cols].astype(f32)).astype(bf16)
            return carry

        lax.fori_loop(0, heads, one, 0, unroll=2)

    def widen(dst, terms):
        for cols in halves:
            total = None
            for left, w in terms:
                part = dot(left[...], W[w, cols, :], 1, 1)
                total = part if total is None else total + part
            dst[:, cols] = total.astype(dst.dtype)

    def attend_out():
        widen(S.at[0], [(att, WOUT)])

    def norm_second():
        def body(s):
            for i, cols in enumerate(halves):
                R1[s, cols] = R0[i, s, :] + (S[0, s, cols] + X[0, s, cols])

        by_rows(16, body)
        norm_rows(lambda s: (R1[s, halves[0]], R1[s, halves[1]]), gains.at[1], nrm2)

    def feed_up():
        tmp[:, halves[0]] = dot(nrm2[...], W[WUP], 1, 0)

        def gelu_rows(s):
            t = tmp[s, halves[0]]
            phi = 0.5 * (1.0 + lax.erf(t * (2.0**-0.5)))
            mlp[s, :] = (t * phi).astype(bf16)
            gprime[s, :] = phi + t * jnp.exp(-0.5 * t * t) * ((2.0 * math.pi) ** -0.5)

        by_rows(16, gelu_rows)

    def weight_grad(w, left, right):
        for r in halves:
            G[w, r, :] = dot(left[:, r], right, 0, 0).astype(bf16)

    def grad_down():
        cot_copy.wait()
        weight_grad(WDOWN, cot, mlp[...])

    def grad_hidden():
        tmp[:, halves[0]] = dot(cot[...], W[WDOWN], 1, 0)

        def dup_rows(s):
            dup[s, :] = (tmp[s, halves[0]] * gprime[s, :]).astype(bf16)

        by_rows(16, dup_rows)

    def grad_up():
        weight_grad(WUP, nrm2, dup[...])

    def feed_down():
        widen(SB, [(mlp, WDOWN)])

    def grad_norm2():
        widen(S.at[1], [(dup, WUP)])

    out_copy = pltpu.make_async_copy(out_rows, o_out, out_sem.at[PACK])
    in2_copy = pltpu.make_async_copy(in2_rows, o_in2, out_sem.at[IN2])

    def write_output():
        def body(s):
            out_rows[s, :] = (R1[s, :] + (SB[s, :].astype(f32) + XB[s, :].astype(f32))).astype(bf16)

        by_rows(16, body)
        out_copy.start()

    def norm_grad(load, i_part, gain, base, out, keep_sum):
        def body(i, carry):
            s = pl.ds(pl.multiple_of(i * 16, 16), 16)
            xs = load(s)
            mean = sum(jnp.sum(t * t, -1, keepdims=True) for t in xs) / width
            r = lax.rsqrt(mean + 1e-06)
            n1 = [t * r for t in xs]
            dn = [S[i_part, s, c] + X[i_part, s, c] for c in halves]
            gd = [gain[0:1, c] * t for c, t in zip(halves, dn)]
            along = sum(jnp.sum(a * b, -1, keepdims=True) for a, b in zip(gd, n1)) / width
            for c, a, b in zip(halves, gd, n1):
                out(s, c, base(s, c) + r * (a - b * along))
            for c, a, b in zip(halves, dn, n1):
                prod = a * b
                accg[:, c] += prod[0:8] + prod[8:16]
            return carry

        accg[...] = jnp.zeros_like(accg)
        lax.fori_loop(0, rows // 16, body, 0, unroll=4)
        total = accg[...]
        high = total.astype(bf16)
        keep_sum[...] = jnp.concatenate([high.astype(f32), total - high.astype(f32)], 0).astype(bf16)

    def norm_grad2():
        def out(s, c, t):
            R1[s, c] = t
            nrm2[s, c] = t.astype(bf16)

        norm_grad(
            lambda s: [R1[s, c] for c in halves],
            1,
            gains.at[1],
            lambda s, c: cot[s, c].astype(f32),
            out,
            dgs.at[1],
        )

    def norm_grad1():
        def out(s, c, t):
            dr0[s, c] = t.astype(bf16)

        norm_grad(
            lambda s: [R0[i, s, :] for i in range(2)],
            0,
            gains.at[0],
            lambda s, c: R1[s, c],
            out,
            dgs.at[0],
        )

    def grad_out():
        weight_grad(WOUT, nrm2, att[...])

    def grad_attended():
        att[...] = dot(nrm2[...], W[WOUT], 1, 0).astype(bf16)

    def attend_back():
        dv[...] = jnp.zeros_like(dv)
        tmp[...] = jnp.zeros_like(tmp)

        def one(h, carry):
            cols, inside = head_window(h)
            cols2 = pl.ds(pl.multiple_of(cols.start + half, 128), win)
            p = prob[h]
            da = only(inside, att[:, cols])
            dp = dot(da, v[:, cols], 1, 1)
            ds = (p * (dp - jnp.sum(dp * p, -1, keepdims=True))).astype(bf16)
            dv_h = dot(p.astype(bf16), da, 0, 0)
            dq_h = dot(ds, k[:, cols], 1, 0) * scale
            dk_h = dot(ds, q[:, cols], 0, 0) * scale
            dv[:, cols] = jnp.where(inside, dv_h, dv[:, cols].astype(f32)).astype(bf16)
            tmp[:, cols] = jnp.where(inside, dq_h, tmp[:, cols])
            tmp[:, cols2] = jnp.where(inside, dk_h, tmp[:, cols2])
            return carry

        lax.fori_loop(0, heads, one, 0, unroll=2)

    def unrotate():
        def body(s):
            dq[s, :] = rope(tmp[s, halves[0]], s, True).astype(bf16)
            dk[s, :] = rope(tmp[s, halves[1]], s, True).astype(bf16)

        by_rows(16, body)

    def grad_norm1():
        widen(S.at[0], [(dq, WQ), (dk, WK), (dv, WV)])

    def grad_in2():
        weight_grad(IN2, hid, dr0[:, mcols])

    def grad_token():
        for c in halves:
            S[1, :, c] = dot(dr0[:, mcols], W[IN2, c, :], 1, 1)

    def grad_pre():
        def body(s):
            t = tmp[s, :]
            sig = 1.0 / (1.0 + jnp.exp(-t))
            grad = (S[1, s, :] + X[1, s, :]) * (sig * (1.0 + t * (1.0 - sig)))
            nrm[s, :] = grad.astype(bf16)

        by_rows(16, body)

    def grad_values():
        total = dot(nrm[...], PK[0], 1, 0) + dot(dr0[...], PK[1], 1, 0)
        o_dval[...] = (total * keep_col[...]).T[0:patch, :]

    def grad_pack():
        @pl.when(m == 0)
        def _():
            for r in halves:
                GP[r, :] = dot(nrm[:, r], inx[...], 0, 0).astype(bf16)

        @pl.when(m == 1)
        def _():
            for r in halves:
                total = dot(dr0[:, r], inx[...], 0, 0)
                for i in range(2):
                    pick = (gain_lane == 2 * patch + 1 + i).astype(bf16)
                    total = total + dot(dgs[i, :, r], pick, 0, 0)
                GP[r, :] = total.astype(bf16)

    def write_in2():
        for i, c in enumerate(halves):
            in2_rows[:, c] = fin_in2[i]
        in2_copy.start()

    def write_small():
        tok_in = 2 * patch
        one, two = fin_pack[0].T, fin_pack[1].T
        o_in1[...] = one[0:tok_in]
        o_b1[...] = one[tok_in : tok_in + 1]
        o_res[...] = two[0:tok_in]
        o_b2[...] = two[tok_in : tok_in + 1]
        o_gattn[...] = two[tok_in + 1 : tok_in + 2]
        o_gmlp[...] = two[tok_in + 2 : tok_in + 3]

    barrier = pltpu.get_barrier_semaphore()
    for dev in (XN, YN, SIB):
        pl.semaphore_signal(barrier, inc=1, device_id=dev, device_id_type=MESH)
    each_other_plane(
        lambda zb: pl.semaphore_signal(barrier, inc=1, device_id=plane(zb), device_id_type=MESH)
    )
    for c in small_copies[2:] + small_copies[:2]:
        c.start()
    order = ITEMS[1:]
    for w in order:
        own_copy(w).start()
    cot_copy = pltpu.make_async_copy(cot_hbm, cot, lsem.at[PACK])
    cot_copy.start()

    for c in small_copies[2:]:
        c.wait()

    @pl.when(m == 0)
    def _():
        pack_block(PK.at[0, row_of(f)], w_in1, [b_in1])

    @pl.when(m == 1)
    def _():
        pack_block(PK.at[1, row_of(f)], w_res, [b_in2, g_attn, g_mlp])

    pl.semaphore_wait(barrier, 6)

    ag_own_z(PACK)
    ag_ready(WUP)
    ag_own_xy(WUP)
    ag_ready(WQ)
    ag_own_z(WQ)
    ag_ready(WK)
    ag_own_xy(WK)
    ag_column(PACK, 3)
    ag_ready(WOUT)
    ag_own_xy(WOUT)
    ag_ready(IN2)
    ag_own_z(IN2)
    ag_ready(WV)
    ag_own_xy(WV)
    ag_own_xy(PACK)
    ag_column(PACK, 1)
    ag_column(IN2, 1)
    ag_plane(WK, 0)
    prepare()
    ag_column(WQ, 3)
    ag_column(WQ, 2)
    ag_own_z(WV)
    ag_ready(XTRA)
    ag_own_xy(XTRA)
    ag_plane(PACK, 0)
    ag_column(PACK, 2)
    ag_plane(PACK, 3)
    ag_plane(IN2, 1)
    ag_column(IN2, 3)
    ag_plane(PACK, 1)
    ag_own_z(WK)
    ag_first_x(XTRA)
    ag_plane(PACK, 2)
    ag_column(IN2, 2)
    ag_own_z(XTRA)
    ag_first_y(XTRA)
    ag_own_xy(WQ)
    ag_column(WK, 1)
    ag_last(PACK)
    ag_own_xy(IN2)
    ag_column(WV, 1)
    ag_column(WQ, 1)
    ag_column(WV, 2)
    ag_plane(IN2, 2)
    ag_plane(WK, 1)
    ag_column(WV, 3)
    ag_first_d(XTRA)
    ag_own_z(WOUT)
    ag_plane(IN2, 0)
    ag_column(WK, 3)
    ag_ready(WDOWN)
    ag_own_z(WDOWN)
    ag_plane(IN2, 3)
    ag_relay(XTRA, 1)
    ag_plane(WV, 0)
    ag_first_y(WUP)
    ag_plane(WV, 2)
    swap_start(0)
    swap_wait(0)
    ag_own_z(WUP)
    ag_first_x(WUP)
    ag_column(WK, 2)
    token_hidden()
    ag_last(IN2)
    ag_plane(WQ, 0)
    token_out()
    swap_start(1)
    ag_plane(WQ, 1)
    ag_plane(WV, 1)
    ag_plane(WV, 3)
    ag_first_d(WUP)
    ag_plane(WK, 3)
    ag_column(WOUT, 1)
    ag_plane(WK, 2)
    ag_plane(WQ, 2)
    swap_wait(1)
    ag_plane(WQ, 3)
    norm_first()
    ag_last(WV)
    ag_column(WOUT, 2)
    ag_column(WDOWN, 1)
    ag_column(WOUT, 3)
    ag_plane(WOUT, 0)
    ag_own_xy(WDOWN)
    ag_relay(XTRA, 0)
    project_v()
    ag_last(WK)
    ag_last(XTRA)
    ag_plane(WOUT, 1)
    project(WK, k)
    ag_last(WQ)
    ag_column(WDOWN, 2)
    project(WQ, q)
    ag_plane(WOUT, 2)
    ag_relay(WUP, 1)
    ag_plane(WOUT, 3)
    attend()
    ag_column(WDOWN, 3)
    ag_relay(WUP, 0)
    ag_last(WOUT)
    attend_out()
    swap_start(2)
    ag_plane(WDOWN, 1)
    ag_plane(WDOWN, 2)
    ag_plane(WDOWN, 3)
    ag_plane(WDOWN, 0)
    swap_wait(2)
    norm_second()
    ag_last(WUP)
    feed_up()
    grad_down()
    rs_start(WDOWN, 0)
    rs_start(WDOWN, 1)
    ag_last(WDOWN)
    grad_hidden()
    grad_up()
    rs_first_far(WUP, 1)
    feed_down()
    swap_start(3)
    grad_norm2()
    swap_start(4)
    rs_turn(WDOWN, 1)
    rs_turn(WDOWN, 0)
    rs_start(WDOWN, 3)
    rs_start(WDOWN, 2)
    swap_wait(3)
    write_output()
    swap_wait(4)
    norm_grad2()
    rs_out(WDOWN, 2)
    grad_out()
    rs_start(WOUT, 1)
    rs_first_far(WUP, 0)
    rs_start(WOUT, 0)
    rs_out(WDOWN, 3)
    rs_start(WOUT, 3)
    grad_attended()
    attend_back()
    rs_first_near(WUP)
    rs_start(WOUT, 2)
    rs_relay(WUP, 1)
    unrotate()
    weight_grad(WK, nrm, dk[...])
    rs_start(WK, 1)
    grad_norm1()
    rs_turn(WOUT, 1)
    swap_start(5)
    weight_grad(WQ, nrm, dq[...])
    pre_act()
    rs_first_far(XTRA, 1)
    rs_turn(WOUT, 0)
    weight_grad(WV, nrm, dv[...])
    rs_start(WQ, 2)
    rs_first_near(XTRA)
    swap_wait(5)
    norm_grad1()
    rs_start(WV, 0)
    rs_start(WQ, 1)
    rs_relay(WUP, 0)
    grad_token()
    swap_start(6)
    grad_in2()
    rs_start(IN2, 1)
    rs_first_far(XTRA, 0)
    rs_turn(WK, 1)
    rs_start(IN2, 2)
    rs_turn(WOUT, 2)
    rs_turn(WV, 0)
    swap_wait(6)
    rs_start(WV, 1)
    rs_start(WQ, 0)
    grad_pre()
    rs_out(WOUT, 3)
    rs_turn(WQ, 2)
    rs_out(WOUT, 2)
    grad_pack()
    rs_turn(IN2, 1)
    rs_start(WK, 2)
    rs_turn(WDOWN, 3)
    rs_turn(WDOWN, 2)
    rs_start(PACK, 1)
    rs_relay(XTRA, 1)
    rs_start(WK, 0)
    rs_out(IN2, 2)
    rs_turn(IN2, 2)
    rs_start(PACK, 3)
    rs_start(PACK, 0)
    rs_start(IN2, 0)
    rs_start(PACK, 2)
    rs_out(WV, 3)
    rs_turn(WOUT, 3)
    rs_out(WDOWN, 1)
    rs_out(WK, 2)
    rs_turn(WK, 2)
    rs_turn(WK, 0)
    rs_out(WOUT, 1)
    rs_start(IN2, 3)
    rs_turn(IN2, 0)
    rs_turn(WV, 1)
    rs_relay(XTRA, 0)
    rs_zsum(WUP, 0)
    rs_turn(PACK, 1)
    rs_start(WV, 3)
    rs_out(IN2, 1)
    rs_turn(PACK, 0)
    rs_out(WOUT, 0)
    grad_values()
    rs_start(WV, 2)
    rs_turn(PACK, 2)
    rs_turn(PACK, 3)
    rs_final(WOUT)
    rs_out(IN2, 3)
    rs_out(WK, 1)
    rs_start(WK, 3)
    rs_out(WK, 3)
    rs_turn(WQ, 0)
    rs_turn(WV, 3)
    rs_out(PACK, 3)
    rs_zsum(XTRA, 0)
    rs_turn(IN2, 3)
    rs_out(PACK, 2)
    rs_turn(WV, 2)
    rs_turn(WQ, 1)
    rs_out(PACK, 1)
    rs_turn(WK, 3)
    rs_zsum(XTRA, 1)
    rs_zsum(WUP, 3)
    rs_zsum(XTRA, 3)
    rs_out(PACK, 0)
    rs_out(WV, 2)
    rs_start(WQ, 3)
    rs_zsum(WUP, 1)
    rs_out(WDOWN, 0)
    rs_final(WDOWN)
    rs_out(WQ, 1)
    rs_out(WV, 0)
    rs_out(IN2, 0)
    rs_out(WQ, 3)
    rs_final(IN2)
    swap_start(7)
    rs_zsum(XTRA, 2)
    rs_out(WV, 1)
    rs_zsum(WUP, 2)
    rs_first_turn(WUP)
    rs_final(PACK)
    rs_first_turn(XTRA)
    swap_start(8)
    rs_out(WQ, 2)
    rs_turn(WQ, 3)
    rs_out(WK, 0)
    rs_final(WV)
    rs_final(WK)
    swap_wait(7)
    write_in2()
    swap_wait(8)
    rs_final(WUP)
    rs_final(XTRA)
    rs_out(WQ, 0)
    rs_final(WQ)
    write_small()

    for w in ITEMS:
        if w not in (IN2, PACK):
            hand_out(w).wait()
    out_copy.wait()
    in2_copy.wait()

    def drain(ref, sem):
        remote(ref, ref, sem, sem, XN).wait_send()

    for w in ITEMS:
        drain(w_rows(w, pl.ds(0, (11 if w in PLANE_FIRST else 15) * blk)), ag_send.at[w])
        if w in PLANE_FIRST:

            @pl.when(inner)
            def _():
                drain(w_rows(w, pl.ds(0, 8 * blk)), ag_send.at[w])

        drain(recv[w].at[pl.ds(0, 15)], rs_send.at[w])


def pack_block(dst, matrix, vectors):
    tok_in, blk = matrix.shape
    parts = [matrix[...].astype(f32)] + [t[...].astype(f32) for t in vectors]
    parts.append(jnp.zeros((PL - tok_in - len(vectors), blk), f32))
    tall = jnp.concatenate(parts, 0)
    wide = jnp.concatenate([tall, jnp.zeros((PL, PL - blk), f32)], 1)
    dst[...] = wide.T[0:blk].astype(bf16)


def copy_kernel(count, *refs):
    sources, targets, held, sems = refs[:count], refs[count : 2 * count], refs[2 * count : -1], refs[-1]
    inward = [pltpu.make_async_copy(sources[i], held[i], sems.at[0, i]) for i in range(count)]
    outward = [pltpu.make_async_copy(held[i], targets[i], sems.at[1, i]) for i in range(count)]
    for c in inward:
        c.start()
    for a, b in zip(inward, outward):
        a.wait()
        b.start()
    for c in outward:
        c.wait()


def rotate(vectors, places):
    half_width = vectors.shape[-1] // 2
    frequency = 10000.0 ** (-2.0 * jnp.arange(half_width, dtype=jnp.float32) / vectors.shape[-1])
    angles = places[:, :, None, None] * frequency
    cosine = jnp.cos(angles)
    sine_val = jnp.sin(angles)
    first_half = vectors[..., :half_width]
    second_half = vectors[..., half_width:]
    return jnp.concatenate(
        [
            first_half * cosine - second_half * sine_val,
            second_half * cosine + first_half * sine_val,
        ],
        -1,
    )


def rms_norm(resid_rows, gain_vec):
    return (
        resid_rows
        * lax.rsqrt(jnp.mean(resid_rows * resid_rows, -1, keepdims=True) + 1e-06)
        * gain_vec
    )


def activate(up_rows):
    return jax.nn.gelu(up_rows, approximate=False)


def general_device(
    values,
    lengths,
    w_in1,
    b_in1,
    w_in2,
    b_in2,
    w_res,
    g_attn,
    w_qkv,
    w_out,
    g_mlp,
    w_up,
    w_down,
    cotangent,
):
    f32 = jnp.float32
    bf16 = jnp.bfloat16
    gathered = (
        lax.all_gather(w_in1, "fsdp", axis=1, tiled=True),
        lax.all_gather(b_in1, "fsdp", axis=0, tiled=True),
        lax.all_gather(w_in2, "fsdp", axis=0, tiled=True),
        lax.all_gather(b_in2, "fsdp", axis=0, tiled=True),
        lax.all_gather(w_res, "fsdp", axis=1, tiled=True),
        lax.all_gather(g_attn, "fsdp", axis=0, tiled=True),
        lax.all_gather(w_qkv, "fsdp", axis=0, tiled=True),
        lax.all_gather(w_out, "fsdp", axis=1, tiled=True),
        lax.all_gather(g_mlp, "fsdp", axis=0, tiled=True),
        lax.all_gather(w_up, "fsdp", axis=0, tiled=True),
        lax.all_gather(w_down, "fsdp", axis=1, tiled=True),
    )
    (
        full_in1,
        full_b1,
        full_in2,
        full_b2,
        full_res,
        full_gattn,
        full_qkv,
        full_out,
        full_gmlp,
        full_up,
        full_down,
    ) = gathered
    series = lengths.shape[0]
    seq_len = values.shape[0] // series
    patch_len = values.shape[1]
    slot_ids = jnp.arange(seq_len, dtype=jnp.int32)
    pad_count = seq_len - lengths
    padded = slot_ids[None, :] < pad_count[:, None]
    places = (slot_ids[None, :] - pad_count[:, None]).astype(f32)
    keep_mask = (1.0 - padded.astype(f32)).reshape(-1, 1)
    inputs = jnp.concatenate(
        [values.astype(f32) * keep_mask, jnp.broadcast_to(1.0 - keep_mask, values.shape)], 1
    ).astype(bf16)
    pre_act = jnp.dot(inputs, full_in1, preferred_element_type=f32) + full_b1.astype(f32)
    hidden = jax.nn.silu(pre_act).astype(bf16)
    resid0 = (
        jnp.dot(hidden, full_in2, preferred_element_type=f32)
        + full_b2.astype(f32)
        + jnp.dot(inputs, full_res, preferred_element_type=f32)
    )
    gain_attn = full_gattn.astype(f32)
    normed = rms_norm(resid0, gain_attn).astype(bf16)
    projected = jnp.einsum("td,dch->tch", normed, full_qkv, preferred_element_type=f32)
    local_heads = projected.shape[2] // HD
    head_shape = (series, seq_len, local_heads, HD)
    queries = rotate(projected[:, 0].reshape(head_shape), places).astype(bf16)
    key_rows = rotate(projected[:, 1].reshape(head_shape), places).astype(bf16)
    value_heads = projected[:, 2].reshape(head_shape).astype(bf16)
    causal = slot_ids[None, :] <= slot_ids[:, None]
    diagonal = slot_ids[None, :] == slot_ids[:, None]
    allowed = (causal[None] & (jnp.logical_not(padded)[:, None, :] | diagonal[None]))[:, None]
    scale = HD ** (-0.5)

    def score_block():
        raw = jnp.einsum("sqhe,skhe->shqk", queries, key_rows, preferred_element_type=f32) * scale
        return jnp.where(allowed, raw, -1e30)

    scores = score_block()
    row_max = jnp.max(scores, -1, keepdims=True)
    exponent = jnp.exp(scores - row_max)
    row_total = jnp.sum(exponent, -1, keepdims=True)
    log_total = row_max + jnp.log(row_total)
    attn_probs = (exponent / row_total).astype(bf16)
    attended = (
        jnp.einsum("shqk,skhe->sqhe", attn_probs, value_heads, preferred_element_type=f32)
        .reshape(-1, local_heads * HD)
        .astype(bf16)
    )
    branch_one = lax.psum(jnp.dot(attended, full_out, preferred_element_type=f32), "mp")
    resid1 = resid0 + branch_one
    gain_mlp = full_gmlp.astype(f32)
    normed2 = rms_norm(resid1, gain_mlp).astype(bf16)
    up_rows = jnp.dot(normed2, full_up, preferred_element_type=f32)
    mlp_hidden = activate(up_rows).astype(bf16)
    branch_two = lax.psum(
        jnp.dot(mlp_hidden, full_down, preferred_element_type=f32).astype(jnp.bfloat16), "mp"
    ).astype(jnp.float32)
    result = (resid1 + branch_two).astype(bf16)
    again = (
        lax.all_gather(w_in1, "fsdp", axis=1, tiled=True),
        lax.all_gather(b_in1, "fsdp", axis=0, tiled=True),
        lax.all_gather(w_in2, "fsdp", axis=0, tiled=True),
        lax.all_gather(b_in2, "fsdp", axis=0, tiled=True),
        lax.all_gather(w_res, "fsdp", axis=1, tiled=True),
        lax.all_gather(g_attn, "fsdp", axis=0, tiled=True),
        lax.all_gather(w_qkv, "fsdp", axis=0, tiled=True),
        lax.all_gather(w_out, "fsdp", axis=1, tiled=True),
        lax.all_gather(g_mlp, "fsdp", axis=0, tiled=True),
        lax.all_gather(w_up, "fsdp", axis=0, tiled=True),
        lax.all_gather(w_down, "fsdp", axis=1, tiled=True),
    )
    (
        back_in1,
        back_b1,
        back_in2,
        back_b2,
        back_res,
        back_gattn,
        back_qkv,
        back_out,
        back_gmlp,
        back_up,
        back_down,
    ) = again
    cot_rows = cotangent.astype(f32)
    grad_down = jnp.einsum("tf,td->fd", mlp_hidden, cotangent, preferred_element_type=f32)
    grad_hidden = jnp.einsum("td,fd->tf", cotangent, back_down, preferred_element_type=f32)
    unused_one, pull_mlp = jax.vjp(activate, up_rows)
    grad_up_rows = pull_mlp(grad_hidden)[0].astype(bf16)
    grad_up = jnp.einsum("td,tf->df", normed2, grad_up_rows, preferred_element_type=f32)
    norm_part2 = jnp.einsum("tf,df->td", grad_up_rows, back_up, preferred_element_type=f32)
    norm_grad2 = lax.psum(norm_part2, "mp")
    unused_two, pull_norm2 = jax.vjp(rms_norm, resid1, back_gmlp.astype(f32))
    resid_part1, grad_gmlp = pull_norm2(norm_grad2)
    resid1_grad = cot_rows + resid_part1
    out_grad = resid1_grad.astype(bf16)
    grad_out = jnp.einsum("th,td->hd", attended, out_grad, preferred_element_type=f32)
    attended_grad = (
        jnp.einsum("td,hd->th", out_grad, back_out, preferred_element_type=f32)
        .astype(bf16)
        .reshape(head_shape)
    )
    scores = score_block()
    probs_full = jnp.exp(scores - log_total)
    value_grad = jnp.einsum(
        "shqk,sqhe->skhe", probs_full.astype(bf16), attended_grad, preferred_element_type=f32
    )
    prob_grad = jnp.einsum(
        "sqhe,skhe->shqk", attended_grad, value_heads, preferred_element_type=f32
    )
    score_grad = (
        probs_full * (prob_grad - jnp.sum(prob_grad * probs_full, -1, keepdims=True))
    ).astype(bf16)
    query_grad = (
        jnp.einsum("shqk,skhe->sqhe", score_grad, key_rows, preferred_element_type=f32) * scale
    )
    key_grad = (
        jnp.einsum("shqk,sqhe->skhe", score_grad, queries, preferred_element_type=f32) * scale
    )
    width_local = local_heads * HD
    qkv_rows = jnp.stack(
        [
            rotate(query_grad, -places).reshape(-1, width_local),
            rotate(key_grad, -places).reshape(-1, width_local),
            value_grad.reshape(-1, width_local),
        ],
        1,
    ).astype(bf16)
    grad_qkv = jnp.einsum("td,tch->dch", normed, qkv_rows, preferred_element_type=f32)
    norm_part1 = jnp.einsum("tch,dch->td", qkv_rows, back_qkv, preferred_element_type=f32)
    norm_grad1 = lax.psum(norm_part1, "mp")
    unused_three, pull_norm1 = jax.vjp(rms_norm, resid0, back_gattn.astype(f32))
    resid_part0, grad_gattn = pull_norm1(norm_grad1)
    resid0_grad = (resid1_grad + resid_part0).astype(bf16)
    grad_in2 = jnp.einsum("th,td->hd", hidden, resid0_grad, preferred_element_type=f32)
    grad_b2 = jnp.sum(resid0_grad.astype(f32), 0)
    grad_res = jnp.einsum("tp,td->pd", inputs, resid0_grad, preferred_element_type=f32)
    hidden_grad = jnp.einsum("td,hd->th", resid0_grad, back_in2, preferred_element_type=f32)
    unused_four, pull_silu = jax.vjp(jax.nn.silu, pre_act)
    pre_grad = pull_silu(hidden_grad)[0].astype(bf16)
    grad_in1 = jnp.einsum("tp,th->ph", inputs, pre_grad, preferred_element_type=f32)
    grad_b1 = jnp.sum(pre_grad.astype(f32), 0)
    input_grad = jnp.einsum(
        "th,ph->tp", pre_grad, back_in1, preferred_element_type=f32
    ) + jnp.einsum("td,pd->tp", resid0_grad, back_res, preferred_element_type=f32)
    values_grad = input_grad[:, :patch_len] * keep_mask
    shares = tuple(
        (
            lax.psum_scatter(grad_in1, "fsdp", scatter_dimension=1, tiled=True),
            lax.psum_scatter(grad_b1, "fsdp", scatter_dimension=0, tiled=True),
            lax.psum_scatter(grad_in2, "fsdp", scatter_dimension=0, tiled=True),
            lax.psum_scatter(grad_b2, "fsdp", scatter_dimension=0, tiled=True),
            lax.psum_scatter(grad_res, "fsdp", scatter_dimension=1, tiled=True),
            lax.psum_scatter(grad_gattn, "fsdp", scatter_dimension=0, tiled=True),
            lax.psum_scatter(grad_qkv, "fsdp", scatter_dimension=0, tiled=True),
            lax.psum_scatter(grad_out, "fsdp", scatter_dimension=1, tiled=True),
            lax.psum_scatter(grad_gmlp, "fsdp", scatter_dimension=0, tiled=True),
            lax.psum_scatter(grad_up, "fsdp", scatter_dimension=0, tiled=True),
            lax.psum_scatter(grad_down, "fsdp", scatter_dimension=1, tiled=True),
        )
    )
    return (result, values_grad) + shares


def fused_device(
    values,
    lengths,
    w_in1,
    b_in1,
    w_in2,
    b_in2,
    w_res,
    g_attn,
    w_qkv,
    w_out,
    g_mlp,
    w_up,
    w_down,
    cotangent,
):
    rows, width = cotangent.shape
    half = w_out.shape[0]
    blk = w_in2.shape[0]
    patch = values.shape[1]
    tok_in = w_in1.shape[0]
    heads = half // HD
    vmem = pl.BlockSpec(memory_space=pltpu.VMEM)
    hbm = pl.BlockSpec(memory_space=pl.ANY)

    def shape(*dims, dtype=f32):
        return jax.ShapeDtypeStruct(dims, dtype)

    out_shape = (
        shape(rows, width, dtype=bf16),
        shape(patch, rows),
        shape(tok_in, blk),
        shape(1, blk),
        shape(blk, width),
        shape(1, blk),
        shape(tok_in, blk),
        shape(1, blk),
        shape(3, blk, half),
        shape(blk, half),
        shape(1, blk),
        shape(blk, half),
        shape(blk, half),
    )
    V = pltpu.VMEM
    small = [
        lengths,
        values.T,
        w_in1,
        w_res,
        b_in1[None],
        b_in2[None],
        g_attn[None],
        g_mlp[None],
    ]
    scratch = [
        [pltpu.SMEM(lengths.shape, lengths.dtype)] + [V(a.shape, a.dtype) for a in small[1:]],
        V((NW, width, half), bf16),
        V((2, width, PL), bf16),
        V((NW, width, half), bf16),
        V((width, PL), bf16),
        {
            w: V((Z_SLOTS if w in Z_FIRST else SLOTS, blk, cols_of(w, half)[1] - cols_of(w, half)[0]), bf16)
            for w in ITEMS
        },
        V((2, rows, half), f32),
        V((rows, width), f32),
        V((2, rows, width), f32),
        V((2, rows, width), f32),
        V((rows, width), bf16),
        V((rows, width), bf16),
        V((rows, width), bf16),
        V((rows, width), bf16),
        V((rows, width), bf16),
        V((rows, half), bf16),
        V((rows, half), bf16),
        V((rows, half), bf16),
        V((heads, rows, rows), f32),
        V((rows, half), bf16),
        V((rows, half), f32),
        V((rows, half), bf16),
        V((rows, width), bf16),
        V((rows, half), bf16),
        V((rows, half), bf16),
        V((rows, half), bf16),
        V((rows, half), bf16),
        V((rows, width), f32),
        V((rows, width), bf16),
        V((rows, half), f32),
        V((rows, half), f32),
        V((rows, rows), f32),
        V((rows, PL), bf16),
        V((2, 8, width), f32),
        V((2, 16, width), bf16),
        V((8, width), f32),
        V((rows, PL), f32),
        V((NW - 1, blk, half), f32),
        V((2, blk, half), f32),
        V((2, blk, PL), f32),
        V((rows, width), bf16),
        V((blk, width), f32),
        pltpu.SemaphoreType.DMA((9,)),
        pltpu.SemaphoreType.DMA((9, 16)),
        pltpu.SemaphoreType.DMA((9,)),
        pltpu.SemaphoreType.DMA((9, Z_SLOTS)),
        pltpu.SemaphoreType.DMA((9,)),
        pltpu.SemaphoreType.DMA((9,)),
        pltpu.SemaphoreType.DMA((9,)),
        pltpu.SemaphoreType.DMA((9,)),
        pltpu.SemaphoreType.DMA((len(small),)),
    ]
    results = pl.pallas_call(
        layer_kernel,
        name="layer",
        out_shape=out_shape,
        in_specs=[[hbm] * len(small)] + [hbm] * 6,
        out_specs=(hbm,) + (vmem,) * 3 + (hbm,) + (vmem,) * 3 + (hbm,) * 2 + (vmem,) + (hbm,) * 2,
        scratch_shapes=scratch,
        compiler_params=pltpu.CompilerParams(
            collective_id=0, has_side_effects=True, vmem_limit_bytes=VMEM_BYTES
        ),
    )(
        small,
        w_in2,
        jnp.transpose(w_qkv, (1, 0, 2)),
        w_out.T,
        w_up,
        w_down.T,
        cotangent,
    )
    (
        out,
        d_values,
        d_in1,
        d_b1,
        d_in2,
        d_b2,
        d_res,
        d_gattn,
        d_qkv,
        d_out,
        d_gmlp,
        d_up,
        d_down,
    ) = pl.pallas_call(
        functools.partial(copy_kernel, len(out_shape)),
        name="hand_over",
        out_shape=out_shape,
        in_specs=[hbm] * len(out_shape),
        out_specs=(hbm,) * len(out_shape),
        scratch_shapes=[V(s.shape, s.dtype) for s in out_shape]
        + [pltpu.SemaphoreType.DMA((2, len(out_shape)))],
    )(*results)
    return (
        out,
        d_values.T,
        d_in1,
        d_b1[0],
        d_in2,
        d_b2[0],
        d_res,
        d_gattn[0],
        jnp.transpose(d_qkv, (1, 0, 2)),
        d_out.T,
        d_gmlp[0],
        d_up,
        d_down.T,
    )


def on_device(*args):
    blk, width = args[4].shape
    half = args[9].shape[0]
    shards = width // blk
    series = args[1].shape[0]
    fits = (
        shards == 16
        and 2 * half == width
        and blk % 16 == 0
        and half % 128 == 0
        and args[0].shape[0] % 64 == 0
        and series <= 8
    )
    return (fused_device if fits else general_device)(*args)


def solution(mesh):
    in_specs = (
        P("fsdp", None),
        P("fsdp"),
        P(None, "fsdp"),
        P("fsdp"),
        P("fsdp", None),
        P("fsdp"),
        P(None, "fsdp"),
        P("fsdp"),
        P("fsdp", None, "mp"),
        P("mp", "fsdp"),
        P("fsdp"),
        P("fsdp", "mp"),
        P("mp", "fsdp"),
        P("fsdp", None),
    )
    out_specs = (
        P("fsdp", None),
        P("fsdp", None),
        P(None, "fsdp"),
        P("fsdp"),
        P("fsdp", None),
        P("fsdp"),
        P(None, "fsdp"),
        P("fsdp"),
        P("fsdp", None, "mp"),
        P("mp", "fsdp"),
        P("fsdp"),
        P("fsdp", "mp"),
        P("mp", "fsdp"),
    )
    return jax.shard_map(
        on_device, mesh=mesh, in_specs=in_specs, out_specs=out_specs, check_vma=False
    )
```
